256 devices in a mesh: fluid: 32 (over y, x, core), wall: 8 (over z).
Axes of the slice: x: 4, y: 4, z: 8, core: 2. Of those that a mesh axis runs over, the one named last changes fastest.
Arguments:
- flow_state: float32 [4, 512, 32, 1024], P(None, 'fluid', None, 'wall'), may hold values from -6 to 6
- regions: int32 [512, 32, 1024], P('fluid', None, 'wall'), may hold values from 0 to 127
- obs_tiles: bfloat16 [32, 8, 32, 128, 128], P('fluid', 'wall'), may hold values from -0.5 to 0.5
- measured: bfloat16 [32, 8, 32, 3, 128], P('fluid', 'wall'), may hold values from -6 to 6
- tile_dest: int32 [32, 8, 32], P('fluid', 'wall'), may hold values from 0 to 31, as said below
- cell_list: int32 [32, 8, 32, 4], P('fluid', 'wall'), may hold values from 0 to 511
Outputs:
- velocity_next: float32 [3, 512, 32, 1024], P(None, 'fluid', None, 'wall')
- adjoint: float32 [3, 512, 32, 1024], P(None, 'fluid', None, 'wall')
- sensitivity: float32 [4096], P(('fluid', 'wall'))
The draws below stay inside these ranges and needn't reach their ends.
Inputs may be any that keep to these rules, and one draw needn't show every extreme that they name: `tile_dest`: each device's list names every fluid block at most 4 times. In each wall column one fluid block is named exactly 4 times by the list of every device of that column.
All inputs are finite; a program needn't handle non-finite values.
Results may differ from the reference program's by a relative error of at most 0.0032.
Values may be sent and summed in bfloat16 or wider, within the bound.
A program may use at most 128 MiB of HBM per device.

```python
import jax
import jax.numpy as jnp
from jax import lax

CX = 16
CY = 32
TW = 128
CAP = 4
TILE_DEV = 32
REG_DEV = 16
NX = 512
NZ = 1024
N_FLUID = 32
N_WALL = 8


def draw_tile_dest(key, part):
    key_hot, key_rows = jax.random.split(jax.random.fold_in(key, 11), 2)
    hot_block = jax.random.randint(key_hot, (N_WALL,), 0, N_FLUID)
    slot_pool = jnp.arange((N_FLUID - 1) * CAP, dtype=jnp.int32) // CAP
    device_keys = jax.random.split(key_rows, N_FLUID * N_WALL)

    def draw_device(device_key, hot_here):
        key_pick, key_order = jax.random.split(device_key)
        others_rows = jax.random.permutation(key_pick, slot_pool)[:TILE_DEV - CAP]
        others_rows = others_rows + (others_rows >= hot_here).astype(jnp.int32)
        all_rows = jnp.concatenate([jnp.full((CAP,), hot_here, jnp.int32), others_rows])
        return jax.random.permutation(key_order, all_rows)
    hot_each = jnp.tile(hot_block, N_FLUID)
    drawn = jax.vmap(draw_device)(device_keys, hot_each)
    return drawn.reshape(N_FLUID, N_WALL, TILE_DEV).astype(jnp.int32)


def touch_ends(array, rng, smallest, largest):
    longest = array.shape.index(max(array.shape))
    spots = []
    for shift in (0, 1):
        where = [jax.random.randint(jax.random.fold_in(rng, axis), (), 0, length) for axis, length in enumerate(array.shape)]
        where[longest] = (where[longest] + shift) % array.shape[longest]
        spots.append(tuple(where))
    return array.at[spots[0]].set(smallest).at[spots[1]].set(largest)


def block_levels(rng, shape, shards, least, largest):
    factor_of, own = 1.0, jax.random.fold_in(rng, 6)
    for axis_at, parts in shards:
        draws = jnp.exp(jax.random.uniform(jax.random.fold_in(own, axis_at), (parts,), jnp.float32, least / len(shards), largest / len(shards)))
        factor_of = factor_of * jnp.repeat(draws, shape[axis_at] // parts).reshape([-1 if axis == axis_at else 1 for axis in range(len(shape))])
    return factor_of


def gaussian(key, shape, width, most, pieces=(), kind=jnp.bfloat16):
    result = width * jax.random.normal(key, shape, jnp.float32)
    if pieces:
        result = result * block_levels(key, shape, pieces, -0.22, 0.18)
    return jnp.clip(result, -most, most).astype(kind)


def setup_inputs(seed: int = 0) -> dict:
    splits = jax.random.split(jax.random.key(seed), 7)
    flow_state = gaussian(splits[0], (4, NX, CY, NZ), 1.0, 6.0, ((1, 32), (3, 8)), jnp.float32)
    regions = touch_ends(jax.random.randint(splits[1], (NX, CY, NZ), 0, REG_DEV * N_WALL), jax.random.fold_in(splits[1], 1), 0, (REG_DEV * N_WALL) - 1).astype(jnp.int32)
    obs_tiles = gaussian(splits[2], (N_FLUID, N_WALL, TILE_DEV, TW, TW), TW ** -0.5, 0.5, ((0, 32), (1, 8)))
    measured = gaussian(splits[3], (N_FLUID, N_WALL, TILE_DEV, 3, TW), 1.0, 6.0, ((0, 32), (1, 8)))
    tile_dest = draw_tile_dest(jax.random.fold_in(splits[6], 71), 0)
    cell_list = touch_ends(jax.random.randint(splits[5], (N_FLUID, N_WALL, N_FLUID, CAP), 0, CX * CY), jax.random.fold_in(splits[5], 1), 0, (CX * CY) - 1).astype(jnp.int32)
    return {"flow_state": flow_state, "regions": regions, "obs_tiles": obs_tiles, "measured": measured, "tile_dest": tile_dest, "cell_list": cell_list}


time_step = 0.12
nu_floor = 0.1
nu_spread = 0.9
relax_sq = 4.0
sens_scale = 0.03


def face_differences(padded, spatial):
    extent = padded.shape[spatial]
    upper_cells = lax.slice_in_dim(padded, 1, extent, axis=spatial)
    lower_cells = lax.slice_in_dim(padded, 0, extent - 1, axis=spatial)
    face_jump = upper_cells - lower_cells
    for across in (1, 2, 3):
        if across != spatial:
            face_jump = lax.slice_in_dim(face_jump, 1, face_jump.shape[across] - 1, axis=across)
    return face_jump


def viscosity(face_jump):
    shear_sq = jnp.sum(face_jump * face_jump, axis=0)
    return nu_floor + nu_spread * jnp.power(1.0 + relax_sq * shear_sq, -0.25)


def divergence(face_nus, face_jumps):
    summed = 0.0
    for spatial, nu_face, face_jump in zip((1, 2, 3), face_nus, face_jumps):
        face_flux = nu_face[None] * face_jump
        extent = face_flux.shape[spatial]
        summed = summed + lax.slice_in_dim(face_flux, 1, extent, axis=spatial) - lax.slice_in_dim(face_flux, 0, extent - 1, axis=spatial)
    return summed


def forward(padded):
    velocity = padded[:3]
    pressure = padded[3:4]
    face_jumps = [face_differences(velocity, spatial) for spatial in (1, 2, 3)]
    face_nus = [viscosity(face_jump) for face_jump in face_jumps]
    halves = []
    for spatial in (1, 2, 3):
        pressure_jump = face_differences(pressure, spatial)
        extent = pressure_jump.shape[spatial]
        halves.append(0.5 * (lax.slice_in_dim(pressure_jump, 1, extent, axis=spatial) + lax.slice_in_dim(pressure_jump, 0, extent - 1, axis=spatial)))
    gradient = jnp.concatenate(halves, axis=0)
    interior = padded[:3, 1:-1, 1:-1, 1:-1]
    velocity_next = interior + time_step * (divergence(face_nus, face_jumps) - gradient)
    return velocity_next, face_nus


def adjoint_step(padded_forcing, face_nus):
    face_jumps = [face_differences(padded_forcing, spatial) for spatial in (1, 2, 3)]
    return padded_forcing[:, 1:-1, 1:-1, 1:-1] + time_step * divergence(face_nus, face_jumps)


def reference(flow_state, regions, obs_tiles, measured, tile_dest, cell_list):
    padded = jnp.pad(flow_state, ((0, 0), (1, 1), (1, 1), (1, 1)))
    velocity_next, face_nus = forward(padded)
    obs_velocity = velocity_next.astype(jnp.bfloat16)
    block_groups = N_FLUID
    walls = N_WALL
    fluid_idx = jnp.arange(block_groups, dtype=jnp.int32)[:, None, None]
    wall_idx = jnp.arange(walls, dtype=jnp.int32)[None, :, None]
    same_target = tile_dest[..., :, None] == tile_dest[..., None, :]
    before = jnp.arange(TILE_DEV)[None, :] < jnp.arange(TILE_DEV)[:, None]
    slot_rank = jnp.sum((same_target & before).astype(jnp.int32), axis=-1)
    cell_tile = cell_list[tile_dest, wall_idx, fluid_idx, slot_rank]
    cell_x = tile_dest * CX + cell_tile // CY
    cell_y = cell_tile % CY
    wall_full = jnp.broadcast_to(wall_idx, tile_dest.shape)
    obs_grid = obs_velocity.reshape(3, block_groups * CX, CY, walls, TW)
    cell_values = obs_grid[:, cell_x, cell_y, wall_full].astype(jnp.float32)
    weights = obs_tiles.astype(jnp.float32)
    model_velocity = jnp.einsum("fwtij,cfwtj->fwtci", weights, cell_values)
    data_residual = (model_velocity - measured.astype(jnp.float32)).astype(jnp.bfloat16)
    contrib = jnp.einsum("fwtij,fwtci->cfwtj", weights, data_residual.astype(jnp.float32))
    forcing = jnp.zeros((3, block_groups * CX, CY, walls, TW), jnp.float32).at[:, cell_x, cell_y, wall_full].add(contrib)
    forcing = forcing.reshape(3, block_groups * CX, CY, walls * TW)
    padded_forcing = jnp.pad(forcing, ((0, 0), (1, 1), (1, 1), (1, 1)))
    adjoint = adjoint_step(padded_forcing, face_nus)
    product = jnp.sum(adjoint * velocity_next, axis=0)
    reg_count = REG_DEV * walls
    owner_block = (jnp.arange(block_groups * CX, dtype=jnp.int32) // CX)[:, None, None]
    segment = owner_block * reg_count + regions
    region_totals = jax.ops.segment_sum(product.reshape(-1), segment.reshape(-1), num_segments=reg_count * block_groups)
    return velocity_next, adjoint, sens_scale * region_totals
```

```python
import functools

import jax
import jax.numpy as jnp
from jax import lax
from jax.experimental import pallas as pl
from jax.experimental.pallas import tpu as pltpu
from jax.sharding import PartitionSpec as P

CX, CY, TW = 16, 32, 128
CAP = 4
REG_DEV = 16
CELLS = CX * CY
TOP = 8
END = TOP + CY
ROWS = END + 8
MSG = 16

time_step = 0.12
nu_floor = 0.1
nu_spread = 0.9
relax_sq = 4.0
sens_scale = 0.03

MESH = pl.DeviceIdType.MESH
F32 = jnp.float32
BF16 = jnp.bfloat16


def iota(shape, dim):
    return lax.broadcasted_iota(jnp.int32, shape, dim)


def viscosity(jumps):
    base = 1.0 + relax_sq * (jumps[0] * jumps[0] + jumps[1] * jumps[1] + jumps[2] * jumps[2])
    root = lax.rsqrt(base)
    return nu_floor + nu_spread * (root * lax.rsqrt(root))


def pack_edges(planes, count, out_ref):
    half = ((iota((8, TW), 1) + 1) % TW) // 2

    def step(x, packed):
        packed = list(packed)
        for k in range(4):
            slot = 4 * x + k
            mine = half == slot
            for c in range(count):
                rows = planes[c, x + 1, TOP + 8 * k : TOP + 8 * k + 8, :]
                packed[c] = jnp.where(mine, pltpu.roll(rows, 2 * slot, 1), packed[c])
        return tuple(packed)

    packed = lax.fori_loop(0, CX, step, tuple(jnp.zeros((8, TW), F32) for _ in range(count)))
    for c in range(count):
        out_ref[c] = packed[c]


def packed_halo(low, high):
    even = iota((8, TW), 1) % 2 == 0
    return jnp.where(even, pltpu.roll(low, 1, 1), pltpu.roll(high, TW - 1, 1))


def unpack_edges(packed, x):
    rolled = [pltpu.roll(packed, (TW - 2 * (4 * x + k)) % TW, 1) for k in range(4)]
    lane = iota((CY, TW), 1)
    return jnp.where((lane == 0) | (lane == TW - 1), jnp.concatenate(rolled, axis=0), 0.0)


def kernel(
    nf, nw, tiles,
    flow, regions, obs, meas, dest, cells,
    vn_out, adj_out, sens_out,
    vp, fp, vn, adj, nux, nuy, nuz, nup, zo, zl, zh, fo, fl, fh,
    wts, reg, meas16, mask16, gat, gatt, route, obsv, sb, rb, mis, contrib, sb2, rb2, rhs,
    onelo, maskhi, prod, lhs, ps, pr,
    load_sem, store_sem, hs, hr, hs2, hr2, as1, ar1, as2, ar2, ws, wr,
):
    f = lax.axis_index("fluid")
    w = lax.axis_index("wall")
    barrier = pltpu.get_barrier_semaphore()
    for d in range(1, nf):
        pl.semaphore_signal(barrier, inc=1, device_id={"fluid": lax.rem(f + d, nf), "wall": w}, device_id_type=MESH)
    for d in range(1, nw):
        pl.semaphore_signal(barrier, inc=1, device_id={"fluid": f, "wall": lax.rem(w + d, nw)}, device_id_type=MESH)

    flow_loads = [
        pltpu.make_async_copy(flow.at[c], vp.at[c, 1 : CX + 1, TOP:END, :], load_sem.at[c]) for c in range(4)
    ]
    for load in flow_loads:
        load.start()
    reg_load = pltpu.make_async_copy(regions, reg, load_sem.at[4])
    reg_load.start()
    obs_load = pltpu.make_async_copy(obs, wts, load_sem.at[5])
    obs_load.start()

    def zero_pads(x, _):
        for c in range(4):
            vp[c, x + 1, 0:TOP, :] = jnp.zeros((TOP, TW), F32)
            vp[c, x + 1, END:ROWS, :] = jnp.zeros((ROWS - END, TW), F32)
        for c in range(3):
            fp[c, x + 1, 0:TOP, :] = jnp.zeros((TOP, TW), F32)
            fp[c, x + 1, END:ROWS, :] = jnp.zeros((ROWS - END, TW), F32)
        return 0

    lax.fori_loop(0, CX, zero_pads, 0)

    @pl.when(f == 0)
    def _():
        vp[:, 0, TOP:END, :] = jnp.zeros((4, CY, TW), F32)
        fp[:, 0, TOP:END, :] = jnp.zeros((3, CY, TW), F32)

    @pl.when(f == nf - 1)
    def _():
        vp[:, CX + 1, TOP:END, :] = jnp.zeros((4, CY, TW), F32)
        fp[:, CX + 1, TOP:END, :] = jnp.zeros((3, CY, TW), F32)

    @pl.when(w == 0)
    def _():
        zl[...] = jnp.zeros((4, 8, TW), F32)
        fl[...] = jnp.zeros((3, 8, TW), F32)

    @pl.when(w == nw - 1)
    def _():
        zh[...] = jnp.zeros((4, 8, TW), F32)
        fh[...] = jnp.zeros((3, 8, TW), F32)

    row16 = iota((MSG, TW), 0)
    lane16 = iota((MSG, TW), 1)
    slot16 = row16 // CAP
    comp16 = row16 % CAP

    def build_gather(p, _):
        ids = jnp.where(
            slot16 == 0, cells[p, 0], jnp.where(slot16 == 1, cells[p, 1], jnp.where(slot16 == 2, cells[p, 2], cells[p, 3]))
        )
        at = pl.ds(pl.multiple_of(p * MSG, MSG), MSG)
        for q in range(CELLS // TW):
            gat[at, q * TW : (q + 1) * TW] = jnp.where(ids == lane16 + q * TW, 1.0, 0.0).astype(BF16)
        return 0

    lax.fori_loop(0, nf, build_gather, 0)

    for load in flow_loads:
        load.wait()
    pack_edges(vp, 4, zo)

    pl.semaphore_wait(barrier, nf - 1 + nw - 1)

    def halo_copies(low_src, low_dst, high_src, high_dst, packed, from_low, from_high, ss, rr):
        up = pltpu.make_async_remote_copy(
            src_ref=high_src, dst_ref=low_dst, send_sem=ss.at[0], recv_sem=rr.at[0],
            device_id={"fluid": lax.rem(f + 1, nf), "wall": w}, device_id_type=MESH)
        down = pltpu.make_async_remote_copy(
            src_ref=low_src, dst_ref=high_dst, send_sem=ss.at[1], recv_sem=rr.at[1],
            device_id={"fluid": lax.rem(f + nf - 1, nf), "wall": w}, device_id_type=MESH)
        right = pltpu.make_async_remote_copy(
            src_ref=packed, dst_ref=from_low, send_sem=ss.at[2], recv_sem=rr.at[2],
            device_id={"fluid": f, "wall": lax.rem(w + 1, nw)}, device_id_type=MESH)
        left = pltpu.make_async_remote_copy(
            src_ref=packed, dst_ref=from_high, send_sem=ss.at[3], recv_sem=rr.at[3],
            device_id={"fluid": f, "wall": lax.rem(w + nw - 1, nw)}, device_id_type=MESH)
        return up, down, right, left

    def start_x(copies):
        pl.when(f < nf - 1)(copies[0].start)
        pl.when(f > 0)(copies[1].start)

    def start_z(copies):
        pl.when(w < nw - 1)(copies[2].start)
        pl.when(w > 0)(copies[3].start)

    def wait_halo(copies):
        pl.when(f > 0)(copies[0].wait_recv)
        pl.when(f < nf - 1)(copies[1].wait_recv)
        pl.when(w > 0)(copies[2].wait_recv)
        pl.when(w < nw - 1)(copies[3].wait_recv)

    def wait_halo_sent(copies):
        pl.when(f < nf - 1)(copies[0].wait_send)
        pl.when(f > 0)(copies[1].wait_send)
        pl.when(w < nw - 1)(copies[2].wait_send)
        pl.when(w > 0)(copies[3].wait_send)

    halo = halo_copies(
        flow.at[:, 0], vp.at[:, 0, TOP:END, :], flow.at[:, CX - 1], vp.at[:, CX + 1, TOP:END, :], zo, zl, zh, hs, hr)
    start_z(halo)
    start_x(halo)

    lane32 = iota((CY, TW), 1)
    first_lane = lane32 == 0
    last_lane = lane32 == TW - 1

    def forward_plane(x, carry, last):
        low_flux, low_p = carry[:3], carry[3]
        cur = [vp[c, x + 1, TOP:END, :] for c in range(4)]
        if last:
            flux_x = [jnp.zeros((CY, TW), F32) for _ in range(3)]
            high_p = jnp.zeros((CY, TW), F32)
        else:
            jump = [vp[c, x + 2, TOP:END, :] - cur[c] for c in range(3)]
            nu = viscosity(jump)
            nux[x + 1] = nu
            flux_x = [nu * j for j in jump]
            high_p = vp[3, x + 2, TOP:END, :]
        jump = [vp[c, x + 1, TOP:ROWS, :] - vp[c, x + 1, TOP - 1 : ROWS - 1, :] for c in range(3)]
        nu = viscosity(jump)
        nuy[x] = nu
        flux_y = [nu * j for j in jump]
        jump = [cur[c] - pltpu.roll(cur[c], 1, 1) for c in range(3)]
        nu = jnp.where(first_lane, 0.0, viscosity(jump))
        nuz[x] = nu
        flux_z = [nu * j for j in jump]
        grad = [
            high_p - low_p,
            vp[3, x + 1, TOP + 1 : END + 1, :] - vp[3, x + 1, TOP - 1 : END - 1, :],
            jnp.where(last_lane, 0.0, pltpu.roll(cur[3], TW - 1, 1)) - jnp.where(first_lane, 0.0, pltpu.roll(cur[3], 1, 1)),
        ]
        for c in range(3):
            div = (flux_x[c] - low_flux[c]) + (flux_y[c][1 : CY + 1] - flux_y[c][0:CY])
            div = div + (pltpu.roll(flux_z[c], TW - 1, 1) - flux_z[c])
            vn[c, x] = cur[c] + time_step * (div - 0.5 * grad[c])
        return (*flux_x, cur[3])

    start = tuple(jnp.zeros((CY, TW), F32) for _ in range(4))
    carry = lax.fori_loop(0, CX - 1, lambda x, carry: forward_plane(x, carry, False), start)
    forward_plane(CX - 1, carry, True)

    wait_halo(halo)
    for plane, ghost, face, sign in ((0, 0, 0, 1.0), (CX - 1, CX + 1, CX, -1.0)):
        jump = [vp[c, ghost, TOP:END, :] - vp[c, plane + 1, TOP:END, :] for c in range(3)]
        nu = viscosity(jump)
        nux[face] = nu
        for c in range(3):
            add = nu * jump[c]
            if c == 0:
                add = add + (0.5 * sign) * vp[3, ghost, TOP:END, :]
            vn[c, plane] = vn[c, plane] + time_step * add
    halo_p = packed_halo(zl[3], zh[3])
    jump = [packed_halo(zl[c], zh[c]) - zo[c] for c in range(3)]
    nu = viscosity(jump)
    nup[...] = nu
    even = iota((8, TW), 1) % 2 == 0
    fix = [time_step * nu * j for j in jump]
    fix[2] = fix[2] + jnp.where(even, 0.5 * time_step, -0.5 * time_step) * halo_p

    def finish_forward(x, _):
        at = pl.ds(pl.multiple_of(x * CY, CY), CY)
        for c in range(3):
            value = vn[c, x] + unpack_edges(fix[c], x)
            vn[c, x] = value
            obsv[at, c * TW : (c + 1) * TW] = value.astype(BF16)
        return 0

    lax.fori_loop(0, CX, finish_forward, 0)

    vn_store = pltpu.make_async_copy(vn, vn_out, store_sem.at[0])

    picked = jnp.dot(gat[...], obsv[...], preferred_element_type=F32)
    comp = iota((nf * MSG, TW), 0) % CAP
    message = jnp.where(
        comp == 0, picked[:, 0:TW],
        jnp.where(comp == 1, picked[:, TW : 2 * TW], jnp.where(comp == 2, picked[:, 2 * TW : 3 * TW], 0.0)),
    ).astype(BF16)
    sb[...] = message.reshape(nf, MSG, TW)

    def exchange(src, dst, ss, rr):
        def copy(peer, at):
            return pltpu.make_async_remote_copy(
                src_ref=src.at[peer], dst_ref=dst.at[at], send_sem=ss.at[peer], recv_sem=rr.at[at],
                device_id={"fluid": peer, "wall": w}, device_id_type=MESH)

        def send():
            def one(d, _):
                copy(lax.rem(f + d, nf), f).start()
                return 0

            lax.fori_loop(1, nf, one, 0)

        def receive():
            def one(d, _):
                peer = lax.rem(f + d, nf)
                copy(peer, peer).wait_recv()
                return 0

            lax.fori_loop(1, nf, one, 0)

        def sent():
            def one(d, _):
                peer = lax.rem(f + d, nf)
                copy(peer, peer).wait_send()
                return 0

            lax.fori_loop(1, nf, one, 0)

        return send, receive, sent

    send1, receive1, sent1 = exchange(sb, rb, as1, ar1)
    send2, receive2, sent2 = exchange(sb2, rb2, as2, ar2)
    send1()
    vn_store.start()
    rb[f] = sb[f]

    dest_lane = jnp.full((MSG, TW), -1, jnp.int32)
    for t in range(tiles):
        dest_lane = jnp.where(lane16 == t, dest[t], dest_lane)
    for t in range(tiles):
        earlier = jnp.where((dest_lane == dest[t]) & (lane16 < t), 1.0, 0.0)
        rank = jnp.sum(earlier, axis=1, keepdims=True)
        mask16[t] = jnp.where((slot16.astype(F32) == rank) & (comp16 < 3), 1.0, 0.0)
        rows = meas[t].astype(F32)
        meas16[t] = jnp.where(
            comp16 == 0, rows[0:1], jnp.where(comp16 == 1, rows[1:2], jnp.where(comp16 == 2, rows[2:3], 0.0)))
    own_row = (lane16 % MSG) == row16
    dest_of = []
    for q in range(tiles * MSG // TW):
        ids = jnp.full((MSG, TW), -1, jnp.int32)
        for u in range(TW // MSG):
            ids = jnp.where(own_row & (lane16 // MSG == u), dest[q * (TW // MSG) + u], ids)
        dest_of.append(ids)

    def build_route(b, _):
        at = pl.ds(pl.multiple_of(b * MSG, MSG), MSG)
        for q, ids in enumerate(dest_of):
            route[at, q * TW : (q + 1) * TW] = jnp.where(ids == b, 1.0, 0.0).astype(BF16)
        return 0

    lax.fori_loop(0, nf, build_route, 0)
    cell_of = []
    for q in range(nf * MSG // TW):
        ids = jnp.full((MSG, TW), -1, jnp.int32)
        for u in range(TW // MSG):
            for k in range(CAP):
                ids = jnp.where(lane16 // CAP == u * CAP + k, cells[q * (TW // MSG) + u, k], ids)
        cell_of.append(ids)

    def build_scatter(i, _):
        at = pl.ds(pl.multiple_of(i * MSG, MSG), MSG)
        for q, ids in enumerate(cell_of):
            gatt[at, q * TW : (q + 1) * TW] = jnp.where(ids == row16 + i * MSG, 1.0, 0.0).astype(BF16)
        return 0

    lax.fori_loop(0, CELLS // MSG, build_scatter, 0)

    obs_load.wait()
    receive1()
    for t in range(tiles):
        predicted = lax.dot_general(
            rb[dest[t]], wts[t], (((1,), (1,)), ((), ())), preferred_element_type=F32)
        mis[t] = ((predicted - meas16[t]) * mask16[t]).astype(BF16)
    for t in range(tiles):
        contrib[t * MSG : (t + 1) * MSG, :] = jnp.dot(mis[t], wts[t], preferred_element_type=F32).astype(BF16)
    sb2[...] = jnp.dot(route[...], contrib[...], preferred_element_type=F32).astype(BF16).reshape(nf, MSG, TW)
    send2()
    rb2[f] = sb2[f]

    reg_load.wait()
    row8 = iota((8, TW), 0)

    def build_regions(x, _):
        for y in range(CY):
            ids = jnp.broadcast_to(reg[x, y : y + 1, :], (MSG, TW))
            group = 2 * x + y // 16
            half, g = (y // 8) % 2, y % 8
            low = pl.multiple_of(group * TW + g * MSG, MSG)
            onelo[pl.ds(low, MSG), half * TW : (half + 1) * TW] = jnp.where(ids % REG_DEV == row16, 1.0, 0.0).astype(BF16)
            maskhi[x * CY + y] = jnp.where(ids[0:8] // REG_DEV == row8, 1.0, 0.0)
        return 0

    lax.fori_loop(0, CX, build_regions, 0)

    receive2()
    back = rb2[...].reshape(nf * MSG, TW).astype(F32)
    for c in range(3):
        rhs[:, c * TW : (c + 1) * TW] = jnp.where(comp == c, back, 0.0).astype(BF16)

    def force_rows(first, last):
        force = jnp.dot(gatt[first * CY : last * CY, :], rhs[...], preferred_element_type=F32)
        for x in range(first, last):
            for c in range(3):
                fp[c, x + 1, TOP:END, :] = force[(x - first) * CY : (x - first + 1) * CY, c * TW : (c + 1) * TW]

    force_rows(0, 1)
    force_rows(CX - 1, CX)
    halo2 = halo_copies(
        fp.at[:, 1, TOP:END, :], fp.at[:, 0, TOP:END, :], fp.at[:, CX, TOP:END, :], fp.at[:, CX + 1, TOP:END, :],
        fo, fl, fh, hs2, hr2)
    start_x(halo2)
    force_rows(1, CX - 1)
    pack_edges(fp, 3, fo)
    start_z(halo2)

    def adjoint_plane(x, carry, last):
        cur = [fp[c, x + 1, TOP:END, :] for c in range(3)]
        flux_x = []
        for c in range(3):
            if last:
                flux = jnp.zeros((CY, TW), F32)
            else:
                flux = nux[x + 1] * (fp[c, x + 2, TOP:END, :] - cur[c])
            flux_x.append(flux)
            flux_y = nuy[x] * (fp[c, x + 1, TOP:ROWS, :] - fp[c, x + 1, TOP - 1 : ROWS - 1, :])
            flux_z = nuz[x] * (cur[c] - pltpu.roll(cur[c], 1, 1))
            div = (flux - carry[c]) + (flux_y[1 : CY + 1] - flux_y[0:CY])
            div = div + (pltpu.roll(flux_z, TW - 1, 1) - flux_z)
            adj[c, x] = cur[c] + time_step * div
        return tuple(flux_x)

    carry = lax.fori_loop(0, CX - 1, lambda x, carry: adjoint_plane(x, carry, False), start[:3])
    adjoint_plane(CX - 1, carry, True)

    wait_halo(halo2)
    for plane, ghost, face in ((0, 0, 0), (CX - 1, CX + 1, CX)):
        for c in range(3):
            jump = fp[c, ghost, TOP:END, :] - fp[c, plane + 1, TOP:END, :]
            adj[c, plane] = adj[c, plane] + time_step * (nux[face] * jump)
    fix2 = [time_step * nup[...] * (packed_halo(fl[c], fh[c]) - fo[c]) for c in range(3)]

    def finish_adjoint(x, sums):
        total = jnp.zeros((CY, TW), F32)
        for c in range(3):
            value = adj[c, x] + unpack_edges(fix2[c], x)
            adj[c, x] = value
            total = total + value * vn[c, x]
        prod[...] = total
        for y in range(CY):
            half, g = (y // 8) % 2, y % 8
            row = (y // 16) * TW + g * MSG
            part = maskhi[x * CY + y] * jnp.broadcast_to(prod[y : y + 1, :], (8, TW))
            coarse = part.astype(BF16).astype(F32)
            lhs[row : row + MSG, half * TW : (half + 1) * TW] = jnp.concatenate(
                [coarse, part - coarse], axis=0).astype(BF16)
        for h in range(2):
            at = pl.ds(pl.multiple_of((2 * x + h) * TW, TW), TW)
            sums = sums + lax.dot_general(
                lhs[h * TW : (h + 1) * TW, :], onelo[at, :], (((1,), (1,)), ((), ())), preferred_element_type=F32)
        return sums

    sums = lax.fori_loop(0, CX, finish_adjoint, jnp.zeros((TW, TW), F32))
    adj_store = pltpu.make_async_copy(adj, adj_out, store_sem.at[1])
    adj_store.start()
    sums = jnp.where(iota((TW, TW), 0) // MSG == iota((TW, TW), 1) // MSG, sums, 0.0)
    short = sums[0:MSG]
    for g in range(1, TW // MSG):
        short = short + sums[g * MSG : (g + 1) * MSG]
    for shift in (64, 32, 16):
        short = short + pltpu.roll(short, shift, 1)
    owned = short[0:8] + short[8:16]
    ps[...] = owned

    def wall_copy(peer, at):
        return pltpu.make_async_remote_copy(
            src_ref=ps, dst_ref=pr.at[at], send_sem=ws.at[peer], recv_sem=wr.at[at],
            device_id={"fluid": f, "wall": peer}, device_id_type=MESH)

    for d in range(1, nw):
        wall_copy(lax.rem(w + d, nw), w).start()
    pr[w] = owned
    wait_halo_sent(halo)
    wait_halo_sent(halo2)
    sent1()
    sent2()
    for d in range(1, nw):
        peer = lax.rem(w + d, nw)
        wall_copy(peer, peer).wait_recv()
    total = pr[0]
    for p in range(1, nw):
        total = total + pr[p]
    mine = jnp.sum(jnp.where(row8 == w, total, 0.0), axis=0, keepdims=True)
    sens_out[...] = sens_scale * mine[:, 0:REG_DEV]
    for d in range(1, nw):
        peer = lax.rem(w + d, nw)
        wall_copy(peer, peer).wait_send()
    vn_store.wait()
    adj_store.wait()


def solution(mesh):
    nf, nw = mesh.shape["fluid"], mesh.shape["wall"]

    def body(flow_state, regions, obs_tiles, measured, tile_dest, cell_list):
        tiles = obs_tiles.shape[2]
        anywhere = pl.BlockSpec(memory_space=pl.ANY)
        in_vmem = pl.BlockSpec(memory_space=pltpu.VMEM)
        in_smem = pl.BlockSpec(memory_space=pltpu.SMEM)
        dma = pltpu.SemaphoreType.DMA
        msgs = nf * MSG
        vn, adj, sens = pl.pallas_call(
            functools.partial(kernel, nf, nw, tiles),
            out_shape=(
                jax.ShapeDtypeStruct((3, CX, CY, TW), F32),
                jax.ShapeDtypeStruct((3, CX, CY, TW), F32),
                jax.ShapeDtypeStruct((1, REG_DEV), F32),
            ),
            in_specs=[anywhere, anywhere, anywhere, in_vmem, in_smem, in_smem],
            out_specs=(anywhere, anywhere, in_vmem),
            scratch_shapes=[
                pltpu.VMEM((4, CX + 2, ROWS, TW), F32),
                pltpu.VMEM((3, CX + 2, ROWS, TW), F32),
                pltpu.VMEM((3, CX, CY, TW), F32),
                pltpu.VMEM((3, CX, CY, TW), F32),
                pltpu.VMEM((CX + 1, CY, TW), F32),
                pltpu.VMEM((CX, ROWS - TOP, TW), F32),
                pltpu.VMEM((CX, CY, TW), F32),
                pltpu.VMEM((8, TW), F32),
                pltpu.VMEM((4, 8, TW), F32),
                pltpu.VMEM((4, 8, TW), F32),
                pltpu.VMEM((4, 8, TW), F32),
                pltpu.VMEM((3, 8, TW), F32),
                pltpu.VMEM((3, 8, TW), F32),
                pltpu.VMEM((3, 8, TW), F32),
                pltpu.VMEM((tiles, TW, TW), BF16),
                pltpu.VMEM((CX, CY, TW), jnp.int32),
                pltpu.VMEM((tiles, MSG, TW), F32),
                pltpu.VMEM((tiles, MSG, TW), F32),
                pltpu.VMEM((msgs, CELLS), BF16),
                pltpu.VMEM((CELLS, msgs), BF16),
                pltpu.VMEM((msgs, tiles * MSG), BF16),
                pltpu.VMEM((CELLS, 3 * TW), BF16),
                pltpu.VMEM((nf, MSG, TW), BF16),
                pltpu.VMEM((nf, MSG, TW), BF16),
                pltpu.VMEM((tiles, MSG, TW), BF16),
                pltpu.VMEM((tiles * MSG, TW), BF16),
                pltpu.VMEM((nf, MSG, TW), BF16),
                pltpu.VMEM((nf, MSG, TW), BF16),
                pltpu.VMEM((msgs, 3 * TW), BF16),
                pltpu.VMEM((2 * CX * TW, 2 * TW), BF16),
                pltpu.VMEM((CELLS, 8, TW), F32),
                pltpu.VMEM((CY, TW), F32),
                pltpu.VMEM((2 * TW, 2 * TW), BF16),
                pltpu.VMEM((8, TW), F32),
                pltpu.VMEM((nw, 8, TW), F32),
                dma((6,)),
                dma((2,)),
                dma((4,)),
                dma((4,)),
                dma((4,)),
                dma((4,)),
                dma((nf,)),
                dma((nf,)),
                dma((nf,)),
                dma((nf,)),
                dma((nw,)),
                dma((nw,)),
            ],
            compiler_params=pltpu.CompilerParams(collective_id=0, has_side_effects=True),
        )(flow_state, regions, obs_tiles[0, 0], measured[0, 0], tile_dest[0, 0], cell_list[0, 0])
        return vn, adj, sens.reshape(REG_DEV)

    in_specs = (
        P(None, "fluid", None, "wall"),
        P("fluid", None, "wall"),
        P("fluid", "wall", None, None, None),
        P("fluid", "wall", None, None, None),
        P("fluid", "wall", None),
        P("fluid", "wall", None, None),
    )
    out_specs = (
        P(None, "fluid", None, "wall"),
        P(None, "fluid", None, "wall"),
        P(("fluid", "wall")),
    )
    return jax.shard_map(body, mesh=mesh, in_specs=in_specs, out_specs=out_specs, check_vma=False)
```

```python
import functools

import jax
import jax.numpy as jnp
from jax import lax
from jax.experimental import pallas as pl
from jax.experimental.pallas import tpu as pltpu
from jax.sharding import PartitionSpec as P

CX, CY, TW = 16, 32, 128
CAP = 4
REG_DEV = 16
CELLS = CX * CY
TOP = 8
END = TOP + CY
ROWS = END + 8
MSG = 16

time_step = 0.12
nu_floor = 0.1
nu_spread = 0.9
relax_sq = 4.0
sens_scale = 0.03

MESH = pl.DeviceIdType.MESH
F32 = jnp.float32
BF16 = jnp.bfloat16


def iota(shape, dim):
    return lax.broadcasted_iota(jnp.int32, shape, dim)


def viscosity(jumps):
    base = 1.0 + relax_sq * (jumps[0] * jumps[0] + jumps[1] * jumps[1] + jumps[2] * jumps[2])
    root = lax.rsqrt(base)
    return nu_floor + nu_spread * (root * lax.rsqrt(root))


def pack_edges(rows_of, zero):
    half = ((iota((8, TW), 1) + 1) % TW) // 2
    total = None
    for k in range(4):
        packed = zero
        for x in range(CX):
            slot = 4 * x + k
            rows = rows_of(x, k)
            if slot:
                rows = pltpu.roll(rows, 2 * slot, 1)
            packed = jnp.where(half == slot, rows, packed)
        total = packed if total is None else total + packed
    return total


def packed_halo(low, high):
    even = iota((8, TW), 1) % 2 == 0
    return jnp.where(even, pltpu.roll(low, 1, 1), pltpu.roll(high, TW - 1, 1))


def unpack_edges(packed, x):
    rolled = [pltpu.roll(packed, TW - 2 * (4 * x + k), 1) if x + k else packed for k in range(4)]
    lane = iota((CY, TW), 1)
    return jnp.where((lane == 0) | (lane == TW - 1), jnp.concatenate(rolled, axis=0), 0.0)


def region_terms(values, masks):
    parts = []
    for value in values:
        coarse = value.astype(BF16).astype(F32)
        parts.append(jnp.concatenate([coarse, value - coarse], axis=0).astype(BF16))
    rows = []
    for h in range(8):
        rows.append(jnp.concatenate([masks(k, h) * part for k, part in enumerate(parts)], axis=1))
    return jnp.concatenate(rows, axis=0)


def fine_labels(ids, store):
    fine = ids % REG_DEV
    for pair in range(REG_DEV // 2):
        both = [jnp.where(fine == 2 * pair + i, 1.0, 0.0) for i in range(2)]
        store(pair, jnp.concatenate(both, axis=0).astype(BF16))


def coarse_mask(ids, h):
    mask = jnp.where(ids // REG_DEV == h, 1.0, 0.0)
    return jnp.concatenate([mask, mask], axis=0).astype(BF16)


def contract_lanes(a, b):
    return lax.dot_general(a, b, (((1,), (1,)), ((), ())), preferred_element_type=F32)


def kernel(
    nf, nw, tiles,
    flow, regions, obs, meas_in, dest_in, cells_in,
    vn, adj, sens_out,
    vp, fp, nux, nuy, nuz, nuzu, nup, vnp, zo, zl, zh, fo, fl, fh,
    wts, reg, meas16, mask16, gat, gatt, route, obsv, sb, rb, mis, contrib, sb2, rb2, rhs,
    onelo, maskhi, onez, maskz, ps, pr, meas, dest, cells,
    load_sem, hs, hr, hs2, hr2, as1, ar1, as2, ar2, ws, wr,
):
    f = lax.axis_index("fluid")
    w = lax.axis_index("wall")
    barrier = pltpu.get_barrier_semaphore()
    for d in range(1, nf):
        pl.semaphore_signal(barrier, inc=1, device_id={"fluid": lax.rem(f + d, nf), "wall": w}, device_id_type=MESH)
    for d in range(1, nw):
        pl.semaphore_signal(barrier, inc=1, device_id={"fluid": f, "wall": lax.rem(w + d, nw)}, device_id_type=MESH)

    flow_loads = [
        pltpu.make_async_copy(flow.at[c], vp.at[c, 1 : CX + 1, TOP:END, :], load_sem.at[c]) for c in range(4)
    ]
    for load in flow_loads:
        load.start()
    reg_load = pltpu.make_async_copy(regions, reg, load_sem.at[4])
    reg_load.start()
    obs_load = pltpu.make_async_copy(obs, wts, load_sem.at[5])
    table_loads = [
        pltpu.make_async_copy(cells_in, cells, load_sem.at[6]),
        pltpu.make_async_copy(dest_in, dest, load_sem.at[7]),
        pltpu.make_async_copy(meas_in, meas, load_sem.at[8]),
    ]
    for load in table_loads:
        load.start()
    obs_load.start()

    pl.semaphore_wait(barrier, nf - 1 + nw - 1)

    def halo_copies(low_src, low_dst, high_src, high_dst, packed, from_low, from_high, ss, rr):
        up = pltpu.make_async_remote_copy(
            src_ref=high_src, dst_ref=low_dst, send_sem=ss.at[0], recv_sem=rr.at[0],
            device_id={"fluid": lax.rem(f + 1, nf), "wall": w}, device_id_type=MESH)
        down = pltpu.make_async_remote_copy(
            src_ref=low_src, dst_ref=high_dst, send_sem=ss.at[1], recv_sem=rr.at[1],
            device_id={"fluid": lax.rem(f + nf - 1, nf), "wall": w}, device_id_type=MESH)
        right = pltpu.make_async_remote_copy(
            src_ref=packed, dst_ref=from_low, send_sem=ss.at[2], recv_sem=rr.at[2],
            device_id={"fluid": f, "wall": lax.rem(w + 1, nw)}, device_id_type=MESH)
        left = pltpu.make_async_remote_copy(
            src_ref=packed, dst_ref=from_high, send_sem=ss.at[3], recv_sem=rr.at[3],
            device_id={"fluid": f, "wall": lax.rem(w + nw - 1, nw)}, device_id_type=MESH)
        return up, down, right, left

    def start_x(copies):
        pl.when(f < nf - 1)(copies[0].start)
        pl.when(f > 0)(copies[1].start)

    def start_z(copies):
        pl.when(w < nw - 1)(copies[2].start)
        pl.when(w > 0)(copies[3].start)

    def wait_halo(copies):
        pl.when(f > 0)(copies[0].wait_recv)
        pl.when(f < nf - 1)(copies[1].wait_recv)
        pl.when(w > 0)(copies[2].wait_recv)
        pl.when(w < nw - 1)(copies[3].wait_recv)

    def wait_halo_sent(copies):
        pl.when(f < nf - 1)(copies[0].wait_send)
        pl.when(f > 0)(copies[1].wait_send)
        pl.when(w < nw - 1)(copies[2].wait_send)
        pl.when(w > 0)(copies[3].wait_send)

    halo = halo_copies(
        flow.at[:, 0], vp.at[:, 0, TOP:END, :], flow.at[:, CX - 1], vp.at[:, CX + 1, TOP:END, :], zo, zl, zh, hs, hr)
    start_x(halo)
    for load in flow_loads:
        load.wait()
    for c in range(4):
        zo[c] = pack_edges(lambda x, k: vp[c, x + 1, TOP + 8 * k : TOP + 8 * k + 8, :], jnp.zeros((8, TW), F32))
    start_z(halo)

    @pl.when(f == 0)
    def _():
        vp[:, 0, TOP:END, :] = jnp.zeros((4, CY, TW), F32)
        fp[:, 0, TOP:END, :] = jnp.zeros((3, CY, TW), F32)

    @pl.when(f == nf - 1)
    def _():
        vp[:, CX + 1, TOP:END, :] = jnp.zeros((4, CY, TW), F32)
        fp[:, CX + 1, TOP:END, :] = jnp.zeros((3, CY, TW), F32)

    @pl.when(w == 0)
    def _():
        zl[...] = jnp.zeros((4, 8, TW), F32)
        fl[...] = jnp.zeros((3, 8, TW), F32)

    @pl.when(w == nw - 1)
    def _():
        zh[...] = jnp.zeros((4, 8, TW), F32)
        fh[...] = jnp.zeros((3, 8, TW), F32)

    def zero_pads(x, _):
        for c in range(4):
            vp[c, x + 1, 0:TOP, :] = jnp.zeros((TOP, TW), F32)
            vp[c, x + 1, END:ROWS, :] = jnp.zeros((ROWS - END, TW), F32)
        for c in range(3):
            fp[c, x + 1, 0:TOP, :] = jnp.zeros((TOP, TW), F32)
            fp[c, x + 1, END:ROWS, :] = jnp.zeros((ROWS - END, TW), F32)
        return 0

    lax.fori_loop(0, CX, zero_pads, 0)

    row16 = iota((MSG, TW), 0)
    lane16 = iota((MSG, TW), 1)
    slot16 = row16 // CAP
    comp16 = row16 % CAP

    def build_gather(p, _):
        ids = jnp.where(
            slot16 == 0, cells[0, p], jnp.where(slot16 == 1, cells[1, p], jnp.where(slot16 == 2, cells[2, p], cells[3, p]))
        )
        at = pl.ds(pl.multiple_of(p * MSG, MSG), MSG)
        for q in range(CELLS // TW):
            gat[at, q * TW : (q + 1) * TW] = jnp.where(ids == lane16 + q * TW, 1.0, 0.0).astype(BF16)
        return 0

    for load in table_loads:
        load.wait()
    lax.fori_loop(0, nf, build_gather, 0)

    lane32 = iota((CY, TW), 1)
    first_lane = lane32 == 0
    last_lane = lane32 == TW - 1

    def forward_plane(x, carry, last):
        low_flux, low_p = carry[:3], carry[3]
        cur = [vp[c, x + 1, TOP:END, :] for c in range(4)]
        if last:
            flux_x = [jnp.zeros((CY, TW), F32) for _ in range(3)]
            high_p = jnp.zeros((CY, TW), F32)
        else:
            jump = [vp[c, x + 2, TOP:END, :] - cur[c] for c in range(3)]
            nu = viscosity(jump)
            nux[x + 1] = nu
            flux_x = [nu * j for j in jump]
            high_p = vp[3, x + 2, TOP:END, :]
        jump = [vp[c, x + 1, TOP:ROWS, :] - vp[c, x + 1, TOP - 1 : ROWS - 1, :] for c in range(3)]
        nu = viscosity(jump)
        nuy[x] = nu
        flux_y = [nu * j for j in jump]
        jump = [cur[c] - pltpu.roll(cur[c], 1, 1) for c in range(3)]
        nu = jnp.where(first_lane, 0.0, viscosity(jump))
        nuz[x] = nu
        nu_up = pltpu.roll(nu, TW - 1, 1)
        nuzu[x] = nu_up
        flux_z = [nu_up * (pltpu.roll(cur[c], TW - 1, 1) - cur[c]) - nu * jump[c] for c in range(3)]
        grad = [
            high_p - low_p,
            vp[3, x + 1, TOP + 1 : END + 1, :] - vp[3, x + 1, TOP - 1 : END - 1, :],
            jnp.where(last_lane, 0.0, pltpu.roll(cur[3], TW - 1, 1)) - jnp.where(first_lane, 0.0, pltpu.roll(cur[3], 1, 1)),
        ]
        for c in range(3):
            div = (flux_x[c] - low_flux[c]) + (flux_y[c][1 : CY + 1] - flux_y[c][0:CY])
            div = div + flux_z[c]
            vn[c, x] = cur[c] + time_step * (div - 0.5 * grad[c])
        return (*flux_x, cur[3])

    start = tuple(jnp.zeros((CY, TW), F32) for _ in range(4))
    carry = lax.fori_loop(0, CX - 1, lambda x, carry: forward_plane(x, carry, False), start, unroll=3)
    forward_plane(CX - 1, carry, True)

    wait_halo(halo)
    for plane, ghost, face, sign in ((0, 0, 0, 1.0), (CX - 1, CX + 1, CX, -1.0)):
        jump = [vp[c, ghost, TOP:END, :] - vp[c, plane + 1, TOP:END, :] for c in range(3)]
        nu = viscosity(jump)
        nux[face] = nu
        for c in range(3):
            add = nu * jump[c]
            if c == 0:
                add = add + (0.5 * sign) * vp[3, ghost, TOP:END, :]
            vn[c, plane] = vn[c, plane] + time_step * add
    halo_p = packed_halo(zl[3], zh[3])
    jump = [packed_halo(zl[c], zh[c]) - zo[c] for c in range(3)]
    nu = viscosity(jump)
    nup[...] = nu
    even = iota((8, TW), 1) % 2 == 0
    fix = [time_step * nu * j for j in jump]
    fix[2] = fix[2] + jnp.where(even, 0.5 * time_step, -0.5 * time_step) * halo_p

    for x in range(CX):
        for c in range(3):
            value = vn[c, x] + unpack_edges(fix[c], x)
            vn[c, x] = value
            obsv[x * CY : (x + 1) * CY, c * TW : (c + 1) * TW] = value.astype(BF16)

    picked = jnp.dot(gat[...], obsv[...], preferred_element_type=F32)
    comp = iota((nf * MSG, TW), 0) % CAP
    message = jnp.where(
        comp == 0, picked[:, 0:TW],
        jnp.where(comp == 1, picked[:, TW : 2 * TW], jnp.where(comp == 2, picked[:, 2 * TW : 3 * TW], 0.0)),
    ).astype(BF16)
    sb[...] = message.reshape(nf, MSG, TW)

    def hops(d):
        chip, side = d // 2, 4
        return sum(min(at, side - at) for at in (chip % side, chip // side % side))

    far_first = sorted(range(1, nf), key=lambda d: -hops(d))

    def exchange(src, dst, ss, rr):
        def copy(peer, at):
            return pltpu.make_async_remote_copy(
                src_ref=src.at[peer], dst_ref=dst.at[at], send_sem=ss.at[peer], recv_sem=rr.at[at],
                device_id={"fluid": peer, "wall": w}, device_id_type=MESH)

        def send():
            for d in far_first:
                copy(lax.rem(f + d, nf), f).start()

        def receive():
            def one(d, _):
                peer = lax.rem(f + d, nf)
                copy(peer, peer).wait_recv()
                return 0

            lax.fori_loop(1, nf, one, 0)

        def sent():
            def one(d, _):
                peer = lax.rem(f + d, nf)
                copy(peer, peer).wait_send()
                return 0

            lax.fori_loop(1, nf, one, 0)

        return send, receive, sent

    send1, receive1, sent1 = exchange(sb, rb, as1, ar1)
    send2, receive2, sent2 = exchange(sb2, rb2, as2, ar2)
    send1()
    rb[f] = sb[f]

    by_tile = [meas[c].astype(F32) for c in range(3)]
    dest_lane = jnp.full((MSG, TW), -1, jnp.int32)
    for t in range(tiles):
        dest_lane = jnp.where(lane16 == t, dest[t], dest_lane)
    for t in range(tiles):
        earlier = jnp.where((dest_lane == dest[t]) & (lane16 < t), 1.0, 0.0)
        rank = jnp.sum(earlier, axis=1, keepdims=True)
        mask16[t] = jnp.where((slot16.astype(F32) == rank) & (comp16 < 3), 1.0, 0.0)
        meas16[t] = jnp.where(
            comp16 == 0, by_tile[0][t : t + 1],
            jnp.where(comp16 == 1, by_tile[1][t : t + 1], jnp.where(comp16 == 2, by_tile[2][t : t + 1], 0.0)))
    own_row = (lane16 % MSG) == row16
    dest_of = []
    for q in range(tiles * MSG // TW):
        ids = jnp.full((MSG, TW), -1, jnp.int32)
        for u in range(TW // MSG):
            ids = jnp.where(own_row & (lane16 // MSG == u), dest[q * (TW // MSG) + u], ids)
        dest_of.append(ids)

    def build_route(b, _):
        at = pl.ds(pl.multiple_of(b * MSG, MSG), MSG)
        for q, ids in enumerate(dest_of):
            route[at, q * TW : (q + 1) * TW] = jnp.where(ids == b, 1.0, 0.0).astype(BF16)
        return 0

    lax.fori_loop(0, nf, build_route, 0)
    cell_of = []
    for q in range(nf * MSG // TW):
        ids = jnp.full((MSG, TW), -1, jnp.int32)
        for u in range(TW // MSG):
            for k in range(CAP):
                ids = jnp.where(lane16 // CAP == u * CAP + k, cells[k, q * (TW // MSG) + u], ids)
        cell_of.append(ids)

    def build_scatter(i, _):
        at = pl.ds(pl.multiple_of(i * MSG, MSG), MSG)
        for q, ids in enumerate(cell_of):
            gatt[at, q * TW : (q + 1) * TW] = jnp.where(ids == row16 + i * MSG, 1.0, 0.0).astype(BF16)
        return 0

    lax.fori_loop(0, CELLS // MSG, build_scatter, 0)

    reg_load.wait()

    def build_regions(x, _):
        at = pl.multiple_of(x * TW, TW)
        for k in range(4):
            ids = reg[x, 8 * k : 8 * k + 8, :]

            def store(pair, rows, k=k):
                onelo[pl.ds(at + MSG * pair, MSG), k * TW : (k + 1) * TW] = rows

            fine_labels(ids, store)
            for h in range(8):
                maskhi[x, k, h] = coarse_mask(ids, h)
        return 0

    lax.fori_loop(0, CX, build_regions, 0)
    packed_ids = pack_edges(lambda x, k: reg[x, 8 * k : 8 * k + 8, :], jnp.zeros((8, TW), jnp.int32))

    def store_z(pair, rows):
        onez[MSG * pair : MSG * pair + MSG, :] = rows

    fine_labels(packed_ids, store_z)
    for h in range(8):
        maskz[h] = coarse_mask(packed_ids, h)
    obs_load.wait()
    receive1()
    for t in range(tiles):
        predicted = lax.dot_general(
            rb[dest[t]], wts[t], (((1,), (1,)), ((), ())), preferred_element_type=F32)
        mis[t] = ((predicted - meas16[t]) * mask16[t]).astype(BF16)
    for t in range(tiles):
        contrib[t * MSG : (t + 1) * MSG, :] = jnp.dot(mis[t], wts[t], preferred_element_type=F32).astype(BF16)
    sb2[...] = jnp.dot(route[...], contrib[...], preferred_element_type=F32).astype(BF16).reshape(nf, MSG, TW)
    send2()
    rb2[f] = sb2[f]

    for c in range(3):
        vnp[c] = pack_edges(lambda x, k: vn[c, x, 8 * k : 8 * k + 8, :], jnp.zeros((8, TW), F32))
    receive2()
    back = rb2[...].reshape(nf * MSG, TW).astype(F32)
    for c in range(3):
        rhs[:, c * TW : (c + 1) * TW] = jnp.where(comp == c, back, 0.0).astype(BF16)

    def force_rows(first, last):
        force = jnp.dot(gatt[first * CY : last * CY, :], rhs[...], preferred_element_type=F32)
        for x in range(first, last):
            for c in range(3):
                fp[c, x + 1, TOP:END, :] = force[(x - first) * CY : (x - first + 1) * CY, c * TW : (c + 1) * TW]

    force_rows(0, 1)
    force_rows(CX - 1, CX)
    halo2 = halo_copies(
        fp.at[:, 1, TOP:END, :], fp.at[:, 0, TOP:END, :], fp.at[:, CX, TOP:END, :], fp.at[:, CX + 1, TOP:END, :],
        fo, fl, fh, hs2, hr2)
    start_x(halo2)
    force_rows(1, CX - 1)
    for c in range(3):
        fo[c] = pack_edges(lambda x, k: fp[c, x + 1, TOP + 8 * k : TOP + 8 * k + 8, :], jnp.zeros((8, TW), F32))
    start_z(halo2)

    def plane_sums(x, total):
        at = pl.ds(pl.multiple_of(x * TW, TW), TW)
        terms = region_terms([total[8 * k : 8 * k + 8] for k in range(4)], lambda k, h: maskhi[x, k, h])
        return contract_lanes(terms, onelo[at, :])

    def adjoint_plane(x, carry, last):
        flux_x = []
        total = None
        for c in range(3):
            cur = fp[c, x + 1, TOP:END, :]
            if last:
                flux = jnp.zeros((CY, TW), F32)
            else:
                flux = nux[x + 1] * (fp[c, x + 2, TOP:END, :] - cur)
            flux_x.append(flux)
            div = flux - carry[c]
            div = div + nuy[x, 1 : CY + 1, :] * (fp[c, x + 1, TOP + 1 : END + 1, :] - cur)
            div = div - nuy[x, 0:CY, :] * (cur - fp[c, x + 1, TOP - 1 : END - 1, :])
            div = div + nuzu[x] * (pltpu.roll(cur, TW - 1, 1) - cur)
            div = div - nuz[x] * (cur - pltpu.roll(cur, 1, 1))
            value = cur + time_step * div
            adj[c, x] = value
            part = value * vn[c, x]
            total = part if total is None else total + part
        return (*flux_x, carry[3] + plane_sums(x, total))

    carry = lax.fori_loop(
        0, CX - 1, lambda x, carry: adjoint_plane(x, carry, False), (*start[:3], jnp.zeros((TW, TW), F32)), unroll=3)
    sums = adjoint_plane(CX - 1, carry, True)[3]

    wait_halo(halo2)
    fix2 = [time_step * nup[...] * (packed_halo(fl[c], fh[c]) - fo[c]) for c in range(3)]
    total = fix2[0] * vnp[0] + fix2[1] * vnp[1] + fix2[2] * vnp[2]
    sums = sums + contract_lanes(region_terms([total], lambda k, h: maskz[h]), onez[...])
    for plane, ghost, face in ((0, 0, 0), (CX - 1, CX + 1, CX)):
        total = None
        for c in range(3):
            jump = fp[c, ghost, TOP:END, :] - fp[c, plane + 1, TOP:END, :]
            value = time_step * (nux[face] * jump)
            adj[c, plane] = adj[c, plane] + value
            part = value * vn[c, plane]
            total = part if total is None else total + part
        sums = sums + plane_sums(plane, total)

    sums = jnp.where(iota((TW, TW), 0) % 8 == iota((TW, TW), 1) % 8, sums, 0.0)
    coarse_rows = [jnp.sum(sums[MSG * h : MSG * h + MSG], axis=0, keepdims=True) for h in range(8)]
    pick = jnp.where(iota((TW, TW), 0) // 8 == iota((TW, TW), 1), 1.0, 0.0)
    owned = jnp.dot(
        jnp.concatenate(coarse_rows, axis=0), pick, precision=lax.Precision.HIGHEST, preferred_element_type=F32)
    ps[...] = owned

    def wall_copy(peer, at):
        return pltpu.make_async_remote_copy(
            src_ref=ps, dst_ref=pr.at[at], send_sem=ws.at[peer], recv_sem=wr.at[at],
            device_id={"fluid": f, "wall": peer}, device_id_type=MESH)

    for d in range(1, nw):
        wall_copy(lax.rem(w + d, nw), w).start()
    pr[w] = owned
    for x in range(CX):
        for c in range(3):
            adj[c, x] = adj[c, x] + unpack_edges(fix2[c], x)
    wait_halo_sent(halo)
    wait_halo_sent(halo2)
    sent1()
    sent2()
    for d in range(1, nw):
        peer = lax.rem(w + d, nw)
        wall_copy(peer, peer).wait_recv()
    total = pr[0]
    for p in range(1, nw):
        total = total + pr[p]
    mine = jnp.sum(jnp.where(iota((8, TW), 0) == w, total, 0.0), axis=0, keepdims=True)
    sens_out[...] = sens_scale * mine[:, 0:REG_DEV]
    for d in range(1, nw):
        peer = lax.rem(w + d, nw)
        wall_copy(peer, peer).wait_send()


def write_out(vn, adj, sens, vn_out, adj_out, sens_out, sems):
    copies = [
        pltpu.make_async_copy(src, dst, sems.at[i])
        for i, (src, dst) in enumerate(((vn, vn_out), (adj, adj_out), (sens, sens_out)))
    ]
    for copy in copies:
        copy.start()
    for copy in copies:
        copy.wait()


def solution(mesh):
    nf, nw = mesh.shape["fluid"], mesh.shape["wall"]

    def body(flow_state, regions, obs_tiles, measured, tile_dest, cell_list):
        tiles = obs_tiles.shape[2]
        in_hbm = pl.BlockSpec(memory_space=pltpu.HBM)
        in_vmem = pl.BlockSpec(memory_space=pltpu.VMEM)
        dma = pltpu.SemaphoreType.DMA
        msgs = nf * MSG
        vn, adj, sens = pl.pallas_call(
            functools.partial(kernel, nf, nw, tiles),
            out_shape=(
                pltpu.VMEM((3, CX, CY, TW), F32),
                pltpu.VMEM((3, CX, CY, TW), F32),
                pltpu.VMEM((1, REG_DEV), F32),
            ),
            in_specs=[in_hbm] * 6,
            out_specs=(in_vmem, in_vmem, in_vmem),
            scratch_shapes=[
                pltpu.VMEM((4, CX + 2, ROWS, TW), F32),
                pltpu.VMEM((3, CX + 2, ROWS, TW), F32),
                pltpu.VMEM((CX + 1, CY, TW), F32),
                pltpu.VMEM((CX, ROWS - TOP, TW), F32),
                pltpu.VMEM((CX, CY, TW), F32),
                pltpu.VMEM((CX, CY, TW), F32),
                pltpu.VMEM((8, TW), F32),
                pltpu.VMEM((3, 8, TW), F32),
                pltpu.VMEM((4, 8, TW), F32),
                pltpu.VMEM((4, 8, TW), F32),
                pltpu.VMEM((4, 8, TW), F32),
                pltpu.VMEM((3, 8, TW), F32),
                pltpu.VMEM((3, 8, TW), F32),
                pltpu.VMEM((3, 8, TW), F32),
                pltpu.VMEM((tiles, TW, TW), BF16),
                pltpu.VMEM((CX, CY, TW), jnp.int32),
                pltpu.VMEM((tiles, MSG, TW), F32),
                pltpu.VMEM((tiles, MSG, TW), F32),
                pltpu.VMEM((msgs, CELLS), BF16),
                pltpu.VMEM((CELLS, msgs), BF16),
                pltpu.VMEM((msgs, tiles * MSG), BF16),
                pltpu.VMEM((CELLS, 3 * TW), BF16),
                pltpu.VMEM((nf, MSG, TW), BF16),
                pltpu.VMEM((nf, MSG, TW), BF16),
                pltpu.VMEM((tiles, MSG, TW), BF16),
                pltpu.VMEM((tiles * MSG, TW), BF16),
                pltpu.VMEM((nf, MSG, TW), BF16),
                pltpu.VMEM((nf, MSG, TW), BF16),
                pltpu.VMEM((msgs, 3 * TW), BF16),
                pltpu.VMEM((CX * TW, 4 * TW), BF16),
                pltpu.VMEM((CX, 4, 8, MSG, TW), BF16),
                pltpu.VMEM((TW, TW), BF16),
                pltpu.VMEM((8, MSG, TW), BF16),
                pltpu.VMEM((8, TW), F32),
                pltpu.VMEM((nw, 8, TW), F32),
                pltpu.VMEM((3, tiles, TW), BF16),
                pltpu.SMEM((tiles,), jnp.int32),
                pltpu.SMEM((CAP, nf), jnp.int32),
                dma((9,)),
                dma((4,)),
                dma((4,)),
                dma((4,)),
                dma((4,)),
                dma((nf,)),
                dma((nf,)),
                dma((nf,)),
                dma((nf,)),
                dma((nw,)),
                dma((nw,)),
            ],
            compiler_params=pltpu.CompilerParams(collective_id=0, has_side_effects=True, vmem_limit_bytes=60 * 1024 * 1024),
        )(
            flow_state, regions, obs_tiles[0, 0], measured[0, 0].transpose(1, 0, 2), tile_dest[0, 0],
            cell_list[0, 0].T,
        )
        vn, adj, sens = pl.pallas_call(
            write_out,
            out_shape=tuple(jax.ShapeDtypeStruct(a.shape, a.dtype) for a in (vn, adj, sens)),
            in_specs=[in_vmem, in_vmem, in_vmem],
            out_specs=(in_hbm, in_hbm, in_hbm),
            scratch_shapes=[dma((3,))],
            compiler_params=pltpu.CompilerParams(vmem_limit_bytes=8 << 20),
        )(vn, adj, sens)
        return vn, adj, sens.reshape(REG_DEV)

    in_specs = (
        P(None, "fluid", None, "wall"),
        P("fluid", None, "wall"),
        P("fluid", "wall", None, None, None),
        P("fluid", "wall", None, None, None),
        P("fluid", "wall", None),
        P("fluid", "wall", None, None),
    )
    out_specs = (
        P(None, "fluid", None, "wall"),
        P(None, "fluid", None, "wall"),
        P(("fluid", "wall")),
    )
    return jax.shard_map(body, mesh=mesh, in_specs=in_specs, out_specs=out_specs, check_vma=False)
```

```python
import functools

import jax
import jax.numpy as jnp
from jax import lax
from jax.experimental import pallas as pl
from jax.experimental.pallas import tpu as pltpu
from jax.sharding import PartitionSpec as P

CX, CY, TW = 16, 32, 128
CAP = 4
REG_DEV = 16
CELLS = CX * CY
TOP = 8
END = TOP + CY
ROWS = END + 8
MSG = 16
ROW = 8

time_step = 0.12
nu_floor = 0.1
nu_spread = 0.9
relax_sq = 4.0
sens_scale = 0.03

MESH = pl.DeviceIdType.MESH
F32 = jnp.float32
BF16 = jnp.bfloat16


def iota(shape, dim):
    return lax.broadcasted_iota(jnp.int32, shape, dim)


def viscosity(jumps):
    base = 1.0 + relax_sq * (jumps[0] * jumps[0] + jumps[1] * jumps[1] + jumps[2] * jumps[2])
    root = lax.rsqrt(base)
    return nu_floor + nu_spread * (root * lax.rsqrt(root))


def pack_edges(rows_of, zero):
    half = ((iota((8, TW), 1) + 1) % TW) // 2
    total = None
    for k in range(4):
        packed = zero
        for x in range(CX):
            slot = 4 * x + k
            rows = rows_of(x, k)
            if slot:
                rows = pltpu.roll(rows, 2 * slot, 1)
            packed = jnp.where(half == slot, rows, packed)
        total = packed if total is None else total + packed
    return total


def packed_halo(low, high):
    even = iota((8, TW), 1) % 2 == 0
    return jnp.where(even, pltpu.roll(low, 1, 1), pltpu.roll(high, TW - 1, 1))


def unpack_edges(packed, x):
    rolled = [pltpu.roll(packed, TW - 2 * (4 * x + k), 1) if x + k else packed for k in range(4)]
    lane = iota((CY, TW), 1)
    return jnp.where((lane == 0) | (lane == TW - 1), jnp.concatenate(rolled, axis=0), 0.0)


def region_terms(values, masks):
    twice = [jnp.concatenate([value, value], axis=0).astype(BF16) for value in values]
    rows = [jnp.concatenate([masks(k, pair) * v for k, v in enumerate(twice)], axis=1) for pair in range(4)]
    return jnp.concatenate(rows, axis=0)


def label_pairs(labels, count, store):
    for pair in range(count // 2):
        both = [jnp.where(labels == 2 * pair + i, 1.0, 0.0) for i in range(2)]
        store(pair, jnp.concatenate(both, axis=0).astype(BF16))


def contract_lanes(a, b):
    return lax.dot_general(a, b, (((1,), (1,)), ((), ())), preferred_element_type=F32)


def kernel(
    nf, nw, tiles,
    flow, regions, obs, meas_in, dest_in, cells_in,
    vn, adj, sens_out,
    vp, fp, nux, nuy, nuz, nuzu, nup, vnp, zo, zl, zh, fo, fl, fh,
    wts, reg, meas16, mask16, gat, gatt, route, obsv, big, sb, rb, mis, contrib, sb2, rb2, rhs,
    onelo, maskhi, onez, maskz, ps, pr, meas, dest, cells,
    row_sem, wall_sem, load_sem, hs, hr, hs2, hr2, as1, ar1, as2, ar2, ws, wr,
):
    f = lax.axis_index("fluid")
    w = lax.axis_index("wall")
    flow_loads = [
        pltpu.make_async_copy(flow.at[c], vp.at[c, 1 : CX + 1, TOP:END, :], load_sem.at[c]) for c in range(4)
    ]
    for load in flow_loads:
        load.start()
    table_loads = [
        pltpu.make_async_copy(cells_in, cells, load_sem.at[6]),
        pltpu.make_async_copy(dest_in, dest, load_sem.at[7]),
        pltpu.make_async_copy(meas_in, meas, load_sem.at[8]),
    ]
    for load in table_loads:
        load.start()

    def signal(sem, to_f, to_w):
        pl.semaphore_signal(
            sem, inc=1, device_id={"fluid": lax.rem(to_f + nf, nf), "wall": lax.rem(to_w + nw, nw)}, device_id_type=MESH)

    barrier = pltpu.get_barrier_semaphore()
    many_rows = nf > ROW
    row_start = (f // ROW) * ROW
    near = [(f + 1, w), (f - 1, w), (f, w + 1), (f, w - 1)]
    if many_rows:
        near += [(f + ROW, w), (f - ROW, w)]
    near += [(row_start + lax.rem(f + d, ROW), w) for d in range(1, ROW)]
    for to_f, to_w in near:
        signal(barrier, to_f, to_w)

    def pass_rows(stage):
        if many_rows:
            signal(row_sem.at[stage], f + ROW, w)
            signal(row_sem.at[stage], f - ROW, w)

    def wait_rows(stage):
        if many_rows:
            pl.semaphore_wait(row_sem.at[stage], 2)

    def pass_walls(stage):
        signal(wall_sem.at[stage], f, w + 1)
        signal(wall_sem.at[stage], f, w - 1)

    def wait_walls(stage):
        pl.semaphore_wait(wall_sem.at[stage], 2)

    def halo_copies(low_src, low_dst, high_src, high_dst, packed, from_low, from_high, ss, rr):
        up = pltpu.make_async_remote_copy(
            src_ref=high_src, dst_ref=low_dst, send_sem=ss.at[0], recv_sem=rr.at[0],
            device_id={"fluid": lax.rem(f + 1, nf), "wall": w}, device_id_type=MESH)
        down = pltpu.make_async_remote_copy(
            src_ref=low_src, dst_ref=high_dst, send_sem=ss.at[1], recv_sem=rr.at[1],
            device_id={"fluid": lax.rem(f + nf - 1, nf), "wall": w}, device_id_type=MESH)
        right = pltpu.make_async_remote_copy(
            src_ref=packed, dst_ref=from_low, send_sem=ss.at[2], recv_sem=rr.at[2],
            device_id={"fluid": f, "wall": lax.rem(w + 1, nw)}, device_id_type=MESH)
        left = pltpu.make_async_remote_copy(
            src_ref=packed, dst_ref=from_high, send_sem=ss.at[3], recv_sem=rr.at[3],
            device_id={"fluid": f, "wall": lax.rem(w + nw - 1, nw)}, device_id_type=MESH)
        return up, down, right, left

    def start_x(copies):
        pl.when(f < nf - 1)(copies[0].start)
        pl.when(f > 0)(copies[1].start)

    def start_z(copies):
        pl.when(w < nw - 1)(copies[2].start)
        pl.when(w > 0)(copies[3].start)

    def wait_halo(copies):
        pl.when(f > 0)(copies[0].wait_recv)
        pl.when(f < nf - 1)(copies[1].wait_recv)
        pl.when(w > 0)(copies[2].wait_recv)
        pl.when(w < nw - 1)(copies[3].wait_recv)

    def wait_halo_sent(copies):
        pl.when(f < nf - 1)(copies[0].wait_send)
        pl.when(f > 0)(copies[1].wait_send)
        pl.when(w < nw - 1)(copies[2].wait_send)
        pl.when(w > 0)(copies[3].wait_send)

    @pl.when(f == 0)
    def _():
        vp[:, 0, TOP:END, :] = jnp.zeros((4, CY, TW), F32)
        fp[:, 0, TOP:END, :] = jnp.zeros((3, CY, TW), F32)

    @pl.when(f == nf - 1)
    def _():
        vp[:, CX + 1, TOP:END, :] = jnp.zeros((4, CY, TW), F32)
        fp[:, CX + 1, TOP:END, :] = jnp.zeros((3, CY, TW), F32)

    @pl.when(w == 0)
    def _():
        zl[...] = jnp.zeros((4, 8, TW), F32)
        fl[...] = jnp.zeros((3, 8, TW), F32)

    @pl.when(w == nw - 1)
    def _():
        zh[...] = jnp.zeros((4, 8, TW), F32)
        fh[...] = jnp.zeros((3, 8, TW), F32)

    def zero_pads(x, _):
        for c in range(4):
            vp[c, x + 1, 0:TOP, :] = jnp.zeros((TOP, TW), F32)
            vp[c, x + 1, END:ROWS, :] = jnp.zeros((ROWS - END, TW), F32)
        for c in range(3):
            fp[c, x + 1, 0:TOP, :] = jnp.zeros((TOP, TW), F32)
            fp[c, x + 1, END:ROWS, :] = jnp.zeros((ROWS - END, TW), F32)
        return 0

    lax.fori_loop(0, CX, zero_pads, 0)

    row16 = iota((MSG, TW), 0)
    lane16 = iota((MSG, TW), 1)
    slot16 = row16 // CAP
    comp16 = row16 % CAP

    def build_gather(i, _):
        ids = jnp.full((MSG, TW), -1, jnp.int32)
        for u in range(MSG):
            ids = jnp.where(row16 == u, cells[u % CAP, 4 * i + u // CAP], ids)
        at = pl.ds(pl.multiple_of(i * MSG, MSG), MSG)
        for q in range(CELLS // TW):
            gat[at, q * TW : (q + 1) * TW] = jnp.where(ids == lane16 + q * TW, 1.0, 0.0).astype(BF16)
        return 0

    big[...] = jnp.zeros((nf * MSG, TW), F32)
    for load in table_loads:
        load.wait()
    lax.fori_loop(0, nf // 4, build_gather, 0)

    for load in flow_loads:
        load.wait()
    for c in range(4):
        zo[c] = pack_edges(lambda x, k: vp[c, x + 1, TOP + 8 * k : TOP + 8 * k + 8, :], jnp.zeros((8, TW), F32))

    reg_load = pltpu.make_async_copy(regions, reg, load_sem.at[4])
    reg_load.start()
    obs_load = pltpu.make_async_copy(obs, wts, load_sem.at[5])
    obs_load.start()
    halo = halo_copies(
        vp.at[:, 1, TOP:END, :], vp.at[:, 0, TOP:END, :], vp.at[:, CX, TOP:END, :], vp.at[:, CX + 1, TOP:END, :],
        zo, zl, zh, hs, hr)
    pl.semaphore_wait(barrier, len(near))
    start_x(halo)
    start_z(halo)
    pass_rows(0)
    pass_walls(0)

    lane32 = iota((CY, TW), 1)
    first_lane = lane32 == 0
    last_lane = lane32 == TW - 1

    def forward_plane(x, carry, last):
        low_flux, low_p = carry[:3], carry[3]
        cur = [vp[c, x + 1, TOP:END, :] for c in range(4)]
        if last:
            flux_x = [jnp.zeros((CY, TW), F32) for _ in range(3)]
            high_p = jnp.zeros((CY, TW), F32)
        else:
            jump = [vp[c, x + 2, TOP:END, :] - cur[c] for c in range(3)]
            nu = viscosity(jump)
            nux[x + 1] = nu
            flux_x = [nu * j for j in jump]
            high_p = vp[3, x + 2, TOP:END, :]
        jump = [vp[c, x + 1, TOP:ROWS, :] - vp[c, x + 1, TOP - 1 : ROWS - 1, :] for c in range(3)]
        nu = viscosity(jump)
        nuy[x] = nu
        flux_y = [nu * j for j in jump]
        jump = [cur[c] - pltpu.roll(cur[c], 1, 1) for c in range(3)]
        nu = jnp.where(first_lane, 0.0, viscosity(jump))
        nuz[x] = nu
        nu_up = pltpu.roll(nu, TW - 1, 1)
        nuzu[x] = nu_up
        flux_z = [nu_up * (pltpu.roll(cur[c], TW - 1, 1) - cur[c]) - nu * jump[c] for c in range(3)]
        grad = [
            high_p - low_p,
            vp[3, x + 1, TOP + 1 : END + 1, :] - vp[3, x + 1, TOP - 1 : END - 1, :],
            jnp.where(last_lane, 0.0, pltpu.roll(cur[3], TW - 1, 1)) - jnp.where(first_lane, 0.0, pltpu.roll(cur[3], 1, 1)),
        ]
        for c in range(3):
            div = (flux_x[c] - low_flux[c]) + (flux_y[c][1 : CY + 1] - flux_y[c][0:CY])
            div = div + flux_z[c]
            vn[c, x] = cur[c] + time_step * (div - 0.5 * grad[c])
        return (*flux_x, cur[3])

    start = tuple(jnp.zeros((CY, TW), F32) for _ in range(4))
    carry = lax.fori_loop(0, CX - 1, lambda x, carry: forward_plane(x, carry, False), start, unroll=3)
    forward_plane(CX - 1, carry, True)

    wait_rows(0)
    pass_rows(1)
    wait_walls(0)
    pass_walls(1)
    wait_halo(halo)
    for plane, ghost, face, sign in ((0, 0, 0, 1.0), (CX - 1, CX + 1, CX, -1.0)):
        jump = [vp[c, ghost, TOP:END, :] - vp[c, plane + 1, TOP:END, :] for c in range(3)]
        nu = viscosity(jump)
        nux[face] = nu
        for c in range(3):
            add = nu * jump[c]
            if c == 0:
                add = add + (0.5 * sign) * vp[3, ghost, TOP:END, :]
            vn[c, plane] = vn[c, plane] + time_step * add
    halo_p = packed_halo(zl[3], zh[3])
    jump = [packed_halo(zl[c], zh[c]) - zo[c] for c in range(3)]
    nu = viscosity(jump)
    nup[...] = nu
    even = iota((8, TW), 1) % 2 == 0
    fix = [time_step * nu * j for j in jump]
    fix[2] = fix[2] + jnp.where(even, 0.5 * time_step, -0.5 * time_step) * halo_p

    for x in range(CX):
        for c in range(3):
            value = vn[c, x] + unpack_edges(fix[c], x)
            vn[c, x] = value
            obsv[x * CY : (x + 1) * CY, c * TW : (c + 1) * TW] = value.astype(BF16)

    picked = jnp.dot(gat[...], obsv[...], preferred_element_type=F32)
    for c in range(3):
        big[pl.ds(c, nf * CAP, stride=CAP), :] = picked[:, c * TW : (c + 1) * TW]
    sb[...] = big[...].astype(BF16).reshape(nf, MSG, TW)

    def hops(d):
        chip, side = d // 2, 4
        return sum(min(at, side - at) for at in (chip % side, chip // side % side))

    far_first = sorted(range(1, nf), key=lambda d: -hops(d))

    def exchange(src, dst, ss, rr):
        def copy(peer, at):
            return pltpu.make_async_remote_copy(
                src_ref=src.at[peer], dst_ref=dst.at[at], send_sem=ss.at[peer], recv_sem=rr.at[at],
                device_id={"fluid": peer, "wall": w}, device_id_type=MESH)

        def send():
            for d in far_first:
                copy(lax.rem(f + d, nf), f).start()

        def receive():
            for d in reversed(far_first):
                peer = lax.rem(f + d, nf)
                copy(peer, peer).wait_recv()

        def sent():
            def one(d, _):
                peer = lax.rem(f + d, nf)
                copy(peer, peer).wait_send()
                return 0

            lax.fori_loop(1, nf, one, 0)

        return send, receive, sent

    send1, receive1, sent1 = exchange(sb, rb, as1, ar1)
    send2, receive2, sent2 = exchange(sb2, rb2, as2, ar2)
    wait_rows(1)
    send1()
    wait_walls(1)
    pass_walls(2)
    rb[f] = sb[f]

    by_tile = [meas[c].astype(F32) for c in range(3)]
    dest_lane = jnp.full((MSG, TW), -1, jnp.int32)
    for t in range(tiles):
        dest_lane = jnp.where(lane16 == t, dest[t], dest_lane)
    for t in range(tiles):
        earlier = jnp.where((dest_lane == dest[t]) & (lane16 < t), 1.0, 0.0)
        rank = jnp.sum(earlier, axis=1, keepdims=True)
        at_row, at_lane = MSG * (t % 2), TW * (t % 2)
        blank = jnp.zeros((MSG, TW), F32)
        mask16[t // 2, at_row : at_row + MSG, at_lane : at_lane + TW] = jnp.where(
            (slot16.astype(F32) == rank) & (comp16 < 3), 1.0, 0.0)
        mask16[t // 2, at_row : at_row + MSG, TW - at_lane : 2 * TW - at_lane] = blank
        meas16[t // 2, at_row : at_row + MSG, TW - at_lane : 2 * TW - at_lane] = blank
        meas16[t // 2, at_row : at_row + MSG, at_lane : at_lane + TW] = jnp.where(
            comp16 == 0, by_tile[0][t : t + 1],
            jnp.where(comp16 == 1, by_tile[1][t : t + 1], jnp.where(comp16 == 2, by_tile[2][t : t + 1], 0.0)))
    route[...] = jnp.where(jnp.broadcast_to(dest_lane[0:1], (nf, TW)) == iota((nf, TW), 0), 1.0, 0.0).astype(BF16)
    cell_of = jnp.full((MSG, TW), -1, jnp.int32)
    for p in range(nf):
        for k in range(CAP):
            cell_of = jnp.where(lane16 == p * CAP + k, cells[k, p], cell_of)

    def build_scatter(i, _):
        at = pl.ds(pl.multiple_of(i * MSG, MSG), MSG)
        gatt[at, :] = jnp.where(cell_of == row16 + i * MSG, 1.0, 0.0).astype(BF16)
        return 0

    lax.fori_loop(0, CELLS // MSG, build_scatter, 0, unroll=4)
    if nf * CAP < TW:
        rhs[...] = jnp.zeros((TW, 3 * TW), BF16)
    reg_load.wait()

    def build_regions(x, _):
        at = pl.multiple_of(x * TW, TW)
        for k in range(4):
            ids = reg[x, 8 * k : 8 * k + 8, :]

            def store(pair, rows, k=k):
                onelo[pl.ds(at + MSG * pair, MSG), k * TW : (k + 1) * TW] = rows

            label_pairs(ids % REG_DEV, REG_DEV, store)

            def store_mask(pair, rows, k=k):
                maskhi[x, k, pair] = rows

            label_pairs(ids // REG_DEV, 8, store_mask)
        return 0

    lax.fori_loop(0, CX, build_regions, 0)
    packed_ids = pack_edges(lambda x, k: reg[x, 8 * k : 8 * k + 8, :], jnp.zeros((8, TW), jnp.int32))

    def store_z(pair, rows):
        onez[MSG * pair : MSG * pair + MSG, :] = rows

    label_pairs(packed_ids % REG_DEV, REG_DEV, store_z)

    def store_zmask(pair, rows):
        maskz[pair] = rows

    label_pairs(packed_ids // REG_DEV, 8, store_zmask)
    obs_load.wait()
    receive1()
    for p in range(tiles // 2):
        pair = wts[2 * p : 2 * p + 2].reshape(2 * TW, TW)
        predicted = contract_lanes(jnp.concatenate([rb[dest[2 * p]], rb[dest[2 * p + 1]]], axis=0), pair)
        mis[p] = ((predicted - meas16[p]) * mask16[p]).astype(BF16)
    for p in range(tiles // 2):
        pair = wts[2 * p : 2 * p + 2].reshape(2 * TW, TW)
        contrib[2 * p * MSG : 2 * (p + 1) * MSG, :] = jnp.dot(mis[p], pair, preferred_element_type=F32)
    used = [r for r in range(MSG) if r % CAP < 3]
    flat = jnp.concatenate([contrib[pl.ds(r, tiles, stride=MSG), :].astype(BF16) for r in used], axis=1)
    routed = jnp.dot(route[:, 0:tiles], flat, preferred_element_type=F32)
    for i, r in enumerate(used):
        big[pl.ds(r, nf, stride=MSG), :] = routed[:, i * TW : (i + 1) * TW]
    sb2[...] = big[...].astype(BF16).reshape(nf, MSG, TW)
    send2()
    wait_walls(2)
    rb2[f] = sb2[f]

    for c in range(3):
        vnp[c] = pack_edges(lambda x, k: vn[c, x, 8 * k : 8 * k + 8, :], jnp.zeros((8, TW), F32))
    receive2()
    big[...] = rb2[...].reshape(nf * MSG, TW).astype(F32)
    for c in range(3):
        rhs[0 : nf * CAP, c * TW : (c + 1) * TW] = big[pl.ds(c, nf * CAP, stride=CAP), :].astype(BF16)

    def force_rows(first, last):
        force = jnp.dot(gatt[first * CY : last * CY, :], rhs[...], preferred_element_type=F32)
        for x in range(first, last):
            for c in range(3):
                fp[c, x + 1, TOP:END, :] = force[(x - first) * CY : (x - first + 1) * CY, c * TW : (c + 1) * TW]

    force_rows(0, 1)
    force_rows(CX - 1, CX)
    halo2 = halo_copies(
        fp.at[:, 1, TOP:END, :], fp.at[:, 0, TOP:END, :], fp.at[:, CX, TOP:END, :], fp.at[:, CX + 1, TOP:END, :],
        fo, fl, fh, hs2, hr2)
    start_x(halo2)
    force_rows(1, CX - 1)
    for c in range(3):
        fo[c] = pack_edges(lambda x, k: fp[c, x + 1, TOP + 8 * k : TOP + 8 * k + 8, :], jnp.zeros((8, TW), F32))
    start_z(halo2)

    def plane_sums(x, total):
        at = pl.ds(pl.multiple_of(x * TW, TW), TW)
        terms = region_terms([total[8 * k : 8 * k + 8] for k in range(4)], lambda k, h: maskhi[x, k, h])
        return contract_lanes(terms, onelo[at, :])

    def adjoint_plane(x, carry, last):
        flux_x = []
        total = None
        for c in range(3):
            cur = fp[c, x + 1, TOP:END, :]
            if last:
                flux = jnp.zeros((CY, TW), F32)
            else:
                flux = nux[x + 1] * (fp[c, x + 2, TOP:END, :] - cur)
            flux_x.append(flux)
            div = flux - carry[c]
            div = div + nuy[x, 1 : CY + 1, :] * (fp[c, x + 1, TOP + 1 : END + 1, :] - cur)
            div = div - nuy[x, 0:CY, :] * (cur - fp[c, x + 1, TOP - 1 : END - 1, :])
            div = div + nuzu[x] * (pltpu.roll(cur, TW - 1, 1) - cur)
            div = div - nuz[x] * (cur - pltpu.roll(cur, 1, 1))
            value = cur + time_step * div
            adj[c, x] = value
            part = value * vn[c, x]
            total = part if total is None else total + part
        return (*flux_x, carry[3] + plane_sums(x, total))

    carry = lax.fori_loop(
        0, CX - 1, lambda x, carry: adjoint_plane(x, carry, False), (*start[:3], jnp.zeros((TW // 2, TW), F32)), unroll=3)
    sums = adjoint_plane(CX - 1, carry, True)[3]

    wait_halo(halo2)
    fix2 = [time_step * nup[...] * (packed_halo(fl[c], fh[c]) - fo[c]) for c in range(3)]
    total = fix2[0] * vnp[0] + fix2[1] * vnp[1] + fix2[2] * vnp[2]
    sums = sums + contract_lanes(region_terms([total], lambda k, h: maskz[h]), onez[...])
    for plane, ghost, face in ((0, 0, 0), (CX - 1, CX + 1, CX)):
        total = None
        for c in range(3):
            jump = fp[c, ghost, TOP:END, :] - fp[c, plane + 1, TOP:END, :]
            value = time_step * (nux[face] * jump)
            adj[c, plane] = adj[c, plane] + value
            part = value * vn[c, plane]
            total = part if total is None else total + part
        sums = sums + plane_sums(plane, total)

    sums = jnp.where(iota((TW // 2, TW), 0) % 8 == iota((TW // 2, TW), 1) % 8, sums, 0.0)
    coarse_rows = [jnp.sum(sums[8 * h : 8 * h + 8], axis=0, keepdims=True) for h in range(8)]
    pick = jnp.where(iota((TW, TW), 0) // 8 == iota((TW, TW), 1), 1.0, 0.0)
    owned = jnp.dot(
        jnp.concatenate(coarse_rows, axis=0), pick, precision=lax.Precision.HIGHEST, preferred_element_type=F32)
    ps[...] = owned

    def wall_copy(peer, at):
        return pltpu.make_async_remote_copy(
            src_ref=ps, dst_ref=pr.at[at], send_sem=ws.at[peer], recv_sem=wr.at[at],
            device_id={"fluid": f, "wall": peer}, device_id_type=MESH)

    for d in range(1, nw):
        wall_copy(lax.rem(w + d, nw), w).start()
    pr[w] = owned
    for x in range(CX):
        for c in range(3):
            adj[c, x] = adj[c, x] + unpack_edges(fix2[c], x)
    wait_halo_sent(halo)
    wait_halo_sent(halo2)
    sent1()
    sent2()
    for d in range(1, nw):
        peer = lax.rem(w + d, nw)
        wall_copy(peer, peer).wait_recv()
    total = pr[0]
    for p in range(1, nw):
        total = total + pr[p]
    mine = jnp.sum(jnp.where(iota((8, TW), 0) == w, total, 0.0), axis=0, keepdims=True)
    sens_out[...] = sens_scale * mine[:, 0:REG_DEV]
    for d in range(1, nw):
        peer = lax.rem(w + d, nw)
        wall_copy(peer, peer).wait_send()


def write_out(vn, adj, sens, vn_out, adj_out, sens_out, sems):
    copies = [
        pltpu.make_async_copy(src, dst, sems.at[i])
        for i, (src, dst) in enumerate(((vn, vn_out), (adj, adj_out), (sens, sens_out)))
    ]
    for copy in copies:
        copy.start()
    for copy in copies:
        copy.wait()


def solution(mesh):
    nf, nw = mesh.shape["fluid"], mesh.shape["wall"]

    def body(flow_state, regions, obs_tiles, measured, tile_dest, cell_list):
        tiles = obs_tiles.shape[2]
        in_hbm = pl.BlockSpec(memory_space=pltpu.HBM)
        in_vmem = pl.BlockSpec(memory_space=pltpu.VMEM)
        dma = pltpu.SemaphoreType.DMA
        vn, adj, sens = pl.pallas_call(
            functools.partial(kernel, nf, nw, tiles),
            out_shape=(
                pltpu.VMEM((3, CX, CY, TW), F32),
                pltpu.VMEM((3, CX, CY, TW), F32),
                pltpu.VMEM((1, REG_DEV), F32),
            ),
            in_specs=[in_hbm] * 6,
            out_specs=(in_vmem, in_vmem, in_vmem),
            scratch_shapes=[
                pltpu.VMEM((4, CX + 2, ROWS, TW), F32),
                pltpu.VMEM((3, CX + 2, ROWS, TW), F32),
                pltpu.VMEM((CX + 1, CY, TW), F32),
                pltpu.VMEM((CX, ROWS - TOP, TW), F32),
                pltpu.VMEM((CX, CY, TW), F32),
                pltpu.VMEM((CX, CY, TW), F32),
                pltpu.VMEM((8, TW), F32),
                pltpu.VMEM((3, 8, TW), F32),
                pltpu.VMEM((4, 8, TW), F32),
                pltpu.VMEM((4, 8, TW), F32),
                pltpu.VMEM((4, 8, TW), F32),
                pltpu.VMEM((3, 8, TW), F32),
                pltpu.VMEM((3, 8, TW), F32),
                pltpu.VMEM((3, 8, TW), F32),
                pltpu.VMEM((tiles, TW, TW), BF16),
                pltpu.VMEM((CX, CY, TW), jnp.int32),
                pltpu.VMEM((tiles // 2, 2 * MSG, 2 * TW), F32),
                pltpu.VMEM((tiles // 2, 2 * MSG, 2 * TW), F32),
                pltpu.VMEM((nf * CAP, CELLS), BF16),
                pltpu.VMEM((CELLS, TW), BF16),
                pltpu.VMEM((nf, TW), BF16),
                pltpu.VMEM((CELLS, 3 * TW), BF16),
                pltpu.VMEM((nf * MSG, TW), F32),
                pltpu.VMEM((nf, MSG, TW), BF16),
                pltpu.VMEM((nf, MSG, TW), BF16),
                pltpu.VMEM((tiles // 2, 2 * MSG, 2 * TW), BF16),
                pltpu.VMEM((tiles * MSG, TW), F32),
                pltpu.VMEM((nf, MSG, TW), BF16),
                pltpu.VMEM((nf, MSG, TW), BF16),
                pltpu.VMEM((TW, 3 * TW), BF16),
                pltpu.VMEM((CX * TW, 4 * TW), BF16),
                pltpu.VMEM((CX, 4, 4, MSG, TW), BF16),
                pltpu.VMEM((TW, TW), BF16),
                pltpu.VMEM((4, MSG, TW), BF16),
                pltpu.VMEM((8, TW), F32),
                pltpu.VMEM((nw, 8, TW), F32),
                pltpu.VMEM((3, tiles, TW), BF16),
                pltpu.SMEM((tiles,), jnp.int32),
                pltpu.SMEM((CAP, nf), jnp.int32),
                pltpu.SemaphoreType.REGULAR((2,)),
                pltpu.SemaphoreType.REGULAR((3,)),
                dma((9,)),
                dma((4,)),
                dma((4,)),
                dma((4,)),
                dma((4,)),
                dma((nf,)),
                dma((nf,)),
                dma((nf,)),
                dma((nf,)),
                dma((nw,)),
                dma((nw,)),
            ],
            compiler_params=pltpu.CompilerParams(collective_id=0, has_side_effects=True, vmem_limit_bytes=60 * 1024 * 1024),
        )(
            flow_state, regions, obs_tiles[0, 0], measured[0, 0].transpose(1, 0, 2), tile_dest[0, 0],
            cell_list[0, 0].T,
        )
        vn, adj, sens = pl.pallas_call(
            write_out,
            out_shape=tuple(jax.ShapeDtypeStruct(a.shape, a.dtype) for a in (vn, adj, sens)),
            in_specs=[in_vmem, in_vmem, in_vmem],
            out_specs=(in_hbm, in_hbm, in_hbm),
            scratch_shapes=[dma((3,))],
            compiler_params=pltpu.CompilerParams(vmem_limit_bytes=8 << 20),
        )(vn, adj, sens)
        return vn, adj, sens.reshape(REG_DEV)

    in_specs = (
        P(None, "fluid", None, "wall"),
        P("fluid", None, "wall"),
        P("fluid", "wall", None, None, None),
        P("fluid", "wall", None, None, None),
        P("fluid", "wall", None),
        P("fluid", "wall", None, None),
    )
    out_specs = (
        P(None, "fluid", None, "wall"),
        P(None, "fluid", None, "wall"),
        P(("fluid", "wall")),
    )
    return jax.shard_map(body, mesh=mesh, in_specs=in_specs, out_specs=out_specs, check_vma=False)
```

```python
import functools

import jax
import jax.numpy as jnp
from jax import lax
from jax.experimental import pallas as pl
from jax.experimental.pallas import tpu as pltpu
from jax.sharding import PartitionSpec as P

CX, CY, TW = 16, 32, 128
CAP = 4
REG_DEV = 16
CELLS = CX * CY
TOP = 8
END = TOP + CY
ROWS = END + 8
MSG = 16
ROW = 8

time_step = 0.12
nu_floor = 0.1
nu_spread = 0.9
relax_sq = 4.0
sens_scale = 0.03

MESH = pl.DeviceIdType.MESH
F32 = jnp.float32
BF16 = jnp.bfloat16


def iota(shape, dim):
    return lax.broadcasted_iota(jnp.int32, shape, dim)


def viscosity(jumps):
    base = 1.0 + relax_sq * (jumps[0] * jumps[0] + jumps[1] * jumps[1] + jumps[2] * jumps[2])
    root = lax.rsqrt(base)
    return nu_floor + nu_spread * (root * lax.rsqrt(root))


def pack_edges(rows_of, zero):
    half = ((iota((8, TW), 1) + 1) % TW) // 2
    total = None
    for k in range(4):
        packed = zero
        for x in range(CX):
            slot = 4 * x + k
            rows = rows_of(x, k)
            if slot:
                rows = pltpu.roll(rows, 2 * slot, 1)
            packed = jnp.where(half == slot, rows, packed)
        total = packed if total is None else total + packed
    return total


def packed_halo(low, high):
    even = iota((8, TW), 1) % 2 == 0
    return jnp.where(even, pltpu.roll(low, 1, 1), pltpu.roll(high, TW - 1, 1))


def unpack_edges(packed, x):
    rolled = [pltpu.roll(packed, TW - 2 * (4 * x + k), 1) if x + k else packed for k in range(4)]
    lane = iota((CY, TW), 1)
    return jnp.where((lane == 0) | (lane == TW - 1), jnp.concatenate(rolled, axis=0), 0.0)


def region_terms(values, masks):
    twice = [jnp.concatenate([value, value], axis=0).astype(BF16) for value in values]
    rows = [jnp.concatenate([masks(k, pair) * v for k, v in enumerate(twice)], axis=1) for pair in range(4)]
    return jnp.concatenate(rows, axis=0)


def label_pairs(labels, count, store):
    for pair in range(count // 2):
        both = [jnp.where(labels == 2 * pair + i, 1.0, 0.0) for i in range(2)]
        store(pair, jnp.concatenate(both, axis=0).astype(BF16))


def contract_lanes(a, b):
    return lax.dot_general(a, b, (((1,), (1,)), ((), ())), preferred_element_type=F32)


def kernel(
    nf, nw, tiles,
    flow, regions, obs, meas_in, dest_in, cells_in,
    vn, adj, sens_out,
    vp, fp, hxs, hxr, fxs, fxr, nux, nuy, nuz, nuzu, nup, vnp, zo, zl, zh, fo, fl, fh,
    wts, reg, meas16, mask16, gat, gatt, route, obsv, big, sb, rb, mis, contrib, sb2, rb2, rhs,
    onelo, maskhi, onez, maskz, pick, lhs, inner, ps, pr, meas, dest, cells,
    row_sem, wall_sem, load_sem, hs, hr, hs2, hr2, as1, ar1, as2, ar2, ws, wr,
):
    f = lax.axis_index("fluid")
    w = lax.axis_index("wall")
    flow_loads = [
        pltpu.make_async_copy(flow.at[c], vp.at[c, 1 : CX + 1, TOP:END, :], load_sem.at[c]) for c in range(4)
    ]
    for load in flow_loads:
        load.start()
    table_loads = [
        pltpu.make_async_copy(cells_in, cells, load_sem.at[6]),
        pltpu.make_async_copy(dest_in, dest, load_sem.at[7]),
        pltpu.make_async_copy(meas_in, meas, load_sem.at[8]),
    ]
    for load in table_loads:
        load.start()

    def signal(sem, to_f, to_w):
        pl.semaphore_signal(
            sem, inc=1, device_id={"fluid": lax.rem(to_f + nf, nf), "wall": lax.rem(to_w + nw, nw)}, device_id_type=MESH)

    barrier = pltpu.get_barrier_semaphore()
    many_rows = nf > ROW
    row_start = (f // ROW) * ROW
    in_row = lax.rem(f, ROW)
    flip = 1 - 2 * lax.rem(f, 2)
    beside = [row_start + lax.rem(in_row + d, ROW) for d in (2, ROW - 2)]
    near = [(f + 1, w), (f - 1, w), (f, w + 1), (f, w - 1)]
    near += [(at, w) for at in beside] + [(at + flip, w) for at in beside] + [(f + flip, w)]
    if many_rows:
        near += [(f + ROW, w), (f - ROW, w)]
    for to_f, to_w in near:
        signal(barrier, to_f, to_w)

    def pass_rows(stage):
        if stage == 0:
            for at in beside:
                signal(row_sem.at[0], at, w)
        elif many_rows:
            signal(row_sem.at[stage], f + ROW, w)
            signal(row_sem.at[stage], f - ROW, w)

    def wait_rows(stage):
        if stage == 0 or many_rows:
            pl.semaphore_wait(row_sem.at[stage], 2)

    def pass_walls(stage):
        signal(wall_sem.at[stage], f, w + 1)
        signal(wall_sem.at[stage], f, w - 1)

    def wait_walls(stage):
        pl.semaphore_wait(wall_sem.at[stage], 2)

    def halo_copies(low_src, low_dst, high_src, high_dst, packed, from_low, from_high, ss, rr):
        up = pltpu.make_async_remote_copy(
            src_ref=high_src, dst_ref=low_dst, send_sem=ss.at[0], recv_sem=rr.at[0],
            device_id={"fluid": lax.rem(f + 1, nf), "wall": w}, device_id_type=MESH)
        down = pltpu.make_async_remote_copy(
            src_ref=low_src, dst_ref=high_dst, send_sem=ss.at[1], recv_sem=rr.at[1],
            device_id={"fluid": lax.rem(f + nf - 1, nf), "wall": w}, device_id_type=MESH)
        right = pltpu.make_async_remote_copy(
            src_ref=packed, dst_ref=from_low, send_sem=ss.at[2], recv_sem=rr.at[2],
            device_id={"fluid": f, "wall": lax.rem(w + 1, nw)}, device_id_type=MESH)
        left = pltpu.make_async_remote_copy(
            src_ref=packed, dst_ref=from_high, send_sem=ss.at[3], recv_sem=rr.at[3],
            device_id={"fluid": f, "wall": lax.rem(w + nw - 1, nw)}, device_id_type=MESH)
        return up, down, right, left

    def start_x(copies):
        pl.when(f < nf - 1)(copies[0].start)
        pl.when(f > 0)(copies[1].start)

    def start_z(copies):
        pl.when(w < nw - 1)(copies[2].start)
        pl.when(w > 0)(copies[3].start)

    def wait_halo(copies):
        pl.when(f > 0)(copies[0].wait_recv)
        pl.when(f < nf - 1)(copies[1].wait_recv)
        pl.when(w > 0)(copies[2].wait_recv)
        pl.when(w < nw - 1)(copies[3].wait_recv)

    def wait_halo_sent(copies):
        pl.when(f < nf - 1)(copies[0].wait_send)
        pl.when(f > 0)(copies[1].wait_send)
        pl.when(w < nw - 1)(copies[2].wait_send)
        pl.when(w > 0)(copies[3].wait_send)

    @pl.when(f == 0)
    def _():
        hxr[0] = jnp.zeros((4, CY, TW), BF16)
        fxr[0] = jnp.zeros((3, CY, TW), BF16)

    @pl.when(f == nf - 1)
    def _():
        hxr[1] = jnp.zeros((4, CY, TW), BF16)
        fxr[1] = jnp.zeros((3, CY, TW), BF16)

    @pl.when(w == 0)
    def _():
        zl[...] = jnp.zeros((4, 8, TW), F32)
        fl[...] = jnp.zeros((3, 8, TW), F32)

    @pl.when(w == nw - 1)
    def _():
        zh[...] = jnp.zeros((4, 8, TW), F32)
        fh[...] = jnp.zeros((3, 8, TW), F32)

    row16 = iota((MSG, TW), 0)
    lane16 = iota((MSG, TW), 1)
    slot16 = row16 // CAP
    comp16 = row16 % CAP

    def build_gather(i, _):
        ids = jnp.full((MSG, TW), -1, jnp.int32)
        for u in range(MSG):
            ids = jnp.where(row16 == u, cells[u % CAP, 4 * i + u // CAP], ids)
        at = pl.ds(pl.multiple_of(i * MSG, MSG), MSG)
        for q in range(CELLS // TW):
            gat[at, q * TW : (q + 1) * TW] = jnp.where(ids == lane16 + q * TW, 1.0, 0.0).astype(BF16)
        return 0

    def zero_pads(x, _):
        for c in range(4):
            vp[c, x + 1, 0:TOP, :] = jnp.zeros((TOP, TW), F32)
            vp[c, x + 1, END:ROWS, :] = jnp.zeros((ROWS - END, TW), F32)
        for c in range(3):
            fp[c, x + 1, 0:TOP, :] = jnp.zeros((TOP, TW), F32)
            fp[c, x + 1, END:ROWS, :] = jnp.zeros((ROWS - END, TW), F32)
        return 0

    lax.fori_loop(0, CX, zero_pads, 0)

    for c in range(4):
        flow_loads[c].wait()
        hxs[0, c] = vp[c, 1, TOP:END, :].astype(BF16)
        hxs[1, c] = vp[c, CX, TOP:END, :].astype(BF16)
        zo[c] = pack_edges(lambda x, k: vp[c, x + 1, TOP + 8 * k : TOP + 8 * k + 8, :], jnp.zeros((8, TW), F32))
    halo = halo_copies(
        hxs.at[0], hxr.at[0], hxs.at[1], hxr.at[1], zo, zl, zh, hs, hr)
    pl.semaphore_wait(barrier, len(near))
    start_x(halo)
    start_z(halo)
    pass_rows(0)
    pass_walls(0)
    reg_load = pltpu.make_async_copy(regions, reg, load_sem.at[4])
    reg_load.start()
    obs_load = pltpu.make_async_copy(obs, wts, load_sem.at[5])
    obs_load.start()
    big[...] = jnp.zeros((nf * MSG, TW), F32)
    for load in table_loads:
        load.wait()
    lax.fori_loop(0, nf // 4, build_gather, 0)

    lane32 = iota((CY, TW), 1)
    first_lane = lane32 == 0
    last_lane = lane32 == TW - 1

    def forward_plane(x, carry, last):
        low_flux, low_p = carry[:3], carry[3]
        cur = [vp[c, x + 1, TOP:END, :] for c in range(4)]
        if last:
            flux_x = [jnp.zeros((CY, TW), F32) for _ in range(3)]
            high_p = jnp.zeros((CY, TW), F32)
        else:
            jump = [vp[c, x + 2, TOP:END, :] - cur[c] for c in range(3)]
            nu = viscosity(jump)
            nux[x + 1] = nu
            flux_x = [nu * j for j in jump]
            high_p = vp[3, x + 2, TOP:END, :]
        jump = [vp[c, x + 1, TOP:ROWS, :] - vp[c, x + 1, TOP - 1 : ROWS - 1, :] for c in range(3)]
        nu = viscosity(jump)
        nuy[x] = nu
        flux_y = [nu * j for j in jump]
        jump = [cur[c] - pltpu.roll(cur[c], 1, 1) for c in range(3)]
        nu = jnp.where(first_lane, 0.0, viscosity(jump))
        nuz[x] = nu
        nu_up = pltpu.roll(nu, TW - 1, 1)
        nuzu[x] = nu_up
        flux_z = [nu_up * (pltpu.roll(cur[c], TW - 1, 1) - cur[c]) - nu * jump[c] for c in range(3)]
        grad = [
            high_p - low_p,
            vp[3, x + 1, TOP + 1 : END + 1, :] - vp[3, x + 1, TOP - 1 : END - 1, :],
            jnp.where(last_lane, 0.0, pltpu.roll(cur[3], TW - 1, 1)) - jnp.where(first_lane, 0.0, pltpu.roll(cur[3], 1, 1)),
        ]
        for c in range(3):
            div = (flux_x[c] - low_flux[c]) + (flux_y[c][1 : CY + 1] - flux_y[c][0:CY])
            div = div + flux_z[c]
            vn[c, x] = cur[c] + time_step * (div - 0.5 * grad[c])
        return (*flux_x, cur[3])

    start = tuple(jnp.zeros((CY, TW), F32) for _ in range(4))
    carry = lax.fori_loop(0, 9, lambda x, carry: forward_plane(x, carry, False), start, unroll=3)
    wait_rows(0)
    pass_rows(1)
    carry = lax.fori_loop(9, CX - 1, lambda x, carry: forward_plane(x, carry, False), carry, unroll=3)
    forward_plane(CX - 1, carry, True)

    wait_rows(1)
    pass_rows(2)
    wait_walls(0)
    pass_walls(1)
    wait_halo(halo)
    for plane, side, face, sign in ((0, 0, 0, 1.0), (CX - 1, 1, CX, -1.0)):
        ghost = [hxr[side, c].astype(F32) for c in range(4)]
        jump = [ghost[c] - vp[c, plane + 1, TOP:END, :] for c in range(3)]
        nu = viscosity(jump)
        nux[face] = nu
        for c in range(3):
            add = nu * jump[c]
            if c == 0:
                add = add + (0.5 * sign) * ghost[3]
            vn[c, plane] = vn[c, plane] + time_step * add
    halo_p = packed_halo(zl[3], zh[3])
    jump = [packed_halo(zl[c], zh[c]) - zo[c] for c in range(3)]
    nu = viscosity(jump)
    nup[...] = nu
    even = iota((8, TW), 1) % 2 == 0
    fix = [time_step * nu * j for j in jump]
    fix[2] = fix[2] + jnp.where(even, 0.5 * time_step, -0.5 * time_step) * halo_p

    for x in range(CX):
        for c in range(3):
            value = vn[c, x] + unpack_edges(fix[c], x)
            vn[c, x] = value
            obsv[x * CY : (x + 1) * CY, c * TW : (c + 1) * TW] = value.astype(BF16)

    picked = jnp.dot(gat[...], obsv[...], preferred_element_type=F32)
    for c in range(3):
        big[pl.ds(c, nf * CAP, stride=CAP), :] = picked[:, c * TW : (c + 1) * TW]
    sb[...] = big[...].astype(BF16).reshape(nf, MSG, TW)

    def hops(d):
        chip, side = d // 2, 4
        return sum(min(at, side - at) for at in (chip % side, chip // side % side))

    far_first = sorted(range(1, nf), key=lambda d: -hops(d))

    def exchange(src, dst, ss, rr):
        def copy(peer, at):
            return pltpu.make_async_remote_copy(
                src_ref=src.at[peer], dst_ref=dst.at[at], send_sem=ss.at[peer], recv_sem=rr.at[at],
                device_id={"fluid": peer, "wall": w}, device_id_type=MESH)

        def send():
            for d in far_first:
                copy(lax.rem(f + d, nf), f).start()

        def receive():
            for d in reversed(far_first):
                peer = lax.rem(f + d, nf)
                copy(peer, peer).wait_recv()

        def sent():
            def one(d, _):
                peer = lax.rem(f + d, nf)
                copy(peer, peer).wait_send()
                return 0

            lax.fori_loop(1, nf, one, 0)

        return send, receive, sent

    send1, receive1, sent1 = exchange(sb, rb, as1, ar1)
    send2, receive2, sent2 = exchange(sb2, rb2, as2, ar2)
    wait_rows(2)
    send1()
    wait_walls(1)
    pass_walls(2)
    rb[f] = sb[f]

    by_tile = [meas[c].astype(F32) for c in range(3)]
    dest_lane = jnp.full((MSG, TW), -1, jnp.int32)
    for t in range(tiles):
        dest_lane = jnp.where(lane16 == t, dest[t], dest_lane)
    for t in range(tiles):
        earlier = jnp.where((dest_lane == dest[t]) & (lane16 < t), 1.0, 0.0)
        rank = jnp.sum(earlier, axis=1, keepdims=True)
        at_row, at_lane = MSG * (t % 2), TW * (t % 2)
        blank = jnp.zeros((MSG, TW), F32)
        mask16[t // 2, at_row : at_row + MSG, at_lane : at_lane + TW] = jnp.where(
            (slot16.astype(F32) == rank) & (comp16 < 3), 1.0, 0.0)
        mask16[t // 2, at_row : at_row + MSG, TW - at_lane : 2 * TW - at_lane] = blank
        meas16[t // 2, at_row : at_row + MSG, TW - at_lane : 2 * TW - at_lane] = blank
        meas16[t // 2, at_row : at_row + MSG, at_lane : at_lane + TW] = jnp.where(
            comp16 == 0, by_tile[0][t : t + 1],
            jnp.where(comp16 == 1, by_tile[1][t : t + 1], jnp.where(comp16 == 2, by_tile[2][t : t + 1], 0.0)))
    route[...] = jnp.where(jnp.broadcast_to(dest_lane[0:1], (nf, TW)) == iota((nf, TW), 0), 1.0, 0.0).astype(BF16)
    cell_of = jnp.full((MSG, TW), -1, jnp.int32)
    for p in range(nf):
        for k in range(CAP):
            cell_of = jnp.where(lane16 == p * CAP + k, cells[k, p], cell_of)

    def build_scatter(i, _):
        at = pl.ds(pl.multiple_of(i * MSG, MSG), MSG)
        gatt[at, :] = jnp.where(cell_of == row16 + i * MSG, 1.0, 0.0).astype(BF16)
        return 0

    lax.fori_loop(0, CELLS // MSG, build_scatter, 0, unroll=4)
    if nf * CAP < TW:
        rhs[...] = jnp.zeros((TW, 3 * TW), BF16)
    reg_load.wait()

    label_of_lane = iota((TW, TW), 1) // 8

    def by_fine_label(ids):
        fine = jnp.concatenate([(ids % REG_DEV).astype(F32)] * REG_DEV, axis=0)
        return jnp.where(fine.T == label_of_lane.astype(F32), 1.0, 0.0).astype(BF16)

    def build_regions(x, _):
        for k in range(4):
            ids = reg[x, 8 * k : 8 * k + 8, :]
            onelo[pl.ds(pl.multiple_of((4 * x + k) * TW, TW), TW), :] = by_fine_label(ids)

            def store_mask(pair, rows, k=k):
                maskhi[x, k, pair] = rows

            label_pairs(ids // REG_DEV, 8, store_mask)
        return 0

    lax.fori_loop(0, CX, build_regions, 0)
    packed_ids = pack_edges(lambda x, k: reg[x, 8 * k : 8 * k + 8, :], jnp.zeros((8, TW), jnp.int32))

    onez[...] = by_fine_label(packed_ids)

    def store_zmask(pair, rows):
        maskz[pair] = rows

    label_pairs(packed_ids // REG_DEV, 8, store_zmask)
    pick[...] = jnp.where(iota((TW, TW), 0) // 8 == iota((TW, TW), 1), 1.0, 0.0).astype(BF16)
    obs_load.wait()
    receive1()
    for p in range(tiles // 2):
        pair = wts[2 * p : 2 * p + 2].reshape(2 * TW, TW)
        predicted = contract_lanes(jnp.concatenate([rb[dest[2 * p]], rb[dest[2 * p + 1]]], axis=0), pair)
        mis[p] = ((predicted - meas16[p]) * mask16[p]).astype(BF16)
    for p in range(tiles // 2):
        pair = wts[2 * p : 2 * p + 2].reshape(2 * TW, TW)
        contrib[2 * p * MSG : 2 * (p + 1) * MSG, :] = jnp.dot(mis[p], pair, preferred_element_type=F32)
    used = [r for r in range(MSG) if r % CAP < 3]
    flat = jnp.concatenate([contrib[pl.ds(r, tiles, stride=MSG), :].astype(BF16) for r in used], axis=1)
    routed = jnp.dot(route[:, 0:tiles], flat, preferred_element_type=F32)
    for i, r in enumerate(used):
        big[pl.ds(r, nf, stride=MSG), :] = routed[:, i * TW : (i + 1) * TW]
    sb2[...] = big[...].astype(BF16).reshape(nf, MSG, TW)
    send2()
    wait_walls(2)
    rb2[f] = sb2[f]

    for c in range(3):
        vnp[c] = pack_edges(lambda x, k: vn[c, x, 8 * k : 8 * k + 8, :], jnp.zeros((8, TW), F32))
    receive2()
    big[...] = rb2[...].reshape(nf * MSG, TW).astype(F32)
    for c in range(3):
        rhs[0 : nf * CAP, c * TW : (c + 1) * TW] = big[pl.ds(c, nf * CAP, stride=CAP), :].astype(BF16)

    def force_rows(first, last):
        force = jnp.dot(gatt[first * CY : last * CY, :], rhs[...], preferred_element_type=F32)
        for x in range(first, last):
            for c in range(3):
                fp[c, x + 1, TOP:END, :] = force[(x - first) * CY : (x - first + 1) * CY, c * TW : (c + 1) * TW]

    force_rows(0, 1)
    force_rows(CX - 1, CX)
    for c in range(3):
        fxs[0, c] = fp[c, 1, TOP:END, :].astype(BF16)
        fxs[1, c] = fp[c, CX, TOP:END, :].astype(BF16)
    halo2 = halo_copies(
        fxs.at[0], fxr.at[0], fxs.at[1], fxr.at[1], fo, fl, fh, hs2, hr2)
    start_x(halo2)
    force_rows(1, CX - 1)
    for c in range(3):
        fo[c] = pack_edges(lambda x, k: fp[c, x + 1, TOP + 8 * k : TOP + 8 * k + 8, :], jnp.zeros((8, TW), F32))
    start_z(halo2)

    def plane_sums(x, total):
        at = pl.ds(pl.multiple_of(x * 4 * TW, TW), 4 * TW)
        terms = region_terms([total[8 * k : 8 * k + 8] for k in range(4)], lambda k, h: maskhi[x, k, h])
        return jnp.dot(terms, onelo[at, :], preferred_element_type=F32)

    def adjoint_plane(x, carry, last):
        flux_x = []
        total = None
        for c in range(3):
            cur = fp[c, x + 1, TOP:END, :]
            if last:
                flux = jnp.zeros((CY, TW), F32)
            else:
                flux = nux[x + 1] * (fp[c, x + 2, TOP:END, :] - cur)
            flux_x.append(flux)
            div = flux - carry[c]
            div = div + nuy[x, 1 : CY + 1, :] * (fp[c, x + 1, TOP + 1 : END + 1, :] - cur)
            div = div - nuy[x, 0:CY, :] * (cur - fp[c, x + 1, TOP - 1 : END - 1, :])
            div = div + nuzu[x] * (pltpu.roll(cur, TW - 1, 1) - cur)
            div = div - nuz[x] * (cur - pltpu.roll(cur, 1, 1))
            value = cur + time_step * div
            adj[c, x] = value
            part = value * vn[c, x]
            total = part if total is None else total + part
        at = pl.ds(pl.multiple_of(x * 4 * TW, 4 * TW), 4 * TW)
        lhs[:, at] = region_terms([total[8 * k : 8 * k + 8] for k in range(4)], lambda k, h: maskhi[x, k, h])
        return tuple(flux_x)

    carry = lax.fori_loop(0, CX - 1, lambda x, carry: adjoint_plane(x, carry, False), start[:3], unroll=3)
    adjoint_plane(CX - 1, carry, True)
    inner[...] = jnp.dot(lhs[...], onelo[...], preferred_element_type=F32)

    wait_halo(halo2)
    fix2 = [time_step * nup[...] * (packed_halo(fl[c], fh[c]) - fo[c]) for c in range(3)]
    total = fix2[0] * vnp[0] + fix2[1] * vnp[1] + fix2[2] * vnp[2]
    terms = region_terms([total], lambda k, h: maskz[h])
    sums = inner[...] + jnp.dot(terms, onez[...], preferred_element_type=F32)
    for plane, side, face in ((0, 0, 0), (CX - 1, 1, CX)):
        total = None
        for c in range(3):
            jump = fxr[side, c].astype(F32) - fp[c, plane + 1, TOP:END, :]
            value = time_step * (nux[face] * jump)
            adj[c, plane] = adj[c, plane] + value
            part = value * vn[c, plane]
            total = part if total is None else total + part
        sums = sums + plane_sums(plane, total)

    sums = jnp.where(iota((TW // 2, TW), 0) % 8 == iota((TW // 2, TW), 1) % 8, sums, 0.0)
    coarse_rows = [jnp.sum(sums[8 * h : 8 * h + 8], axis=0, keepdims=True) for h in range(8)]
    by_label = jnp.concatenate(coarse_rows, axis=0)
    parts = []
    for _ in range(3):
        part = by_label.astype(BF16)
        parts.append(part)
        by_label = by_label - part.astype(F32)
    owned = jnp.dot(jnp.concatenate(parts, axis=0), pick[...], preferred_element_type=F32)
    owned = owned[0:8] + owned[8:16] + owned[16:24]
    ps[...] = owned

    def wall_copy(peer, at):
        return pltpu.make_async_remote_copy(
            src_ref=ps, dst_ref=pr.at[at], send_sem=ws.at[peer], recv_sem=wr.at[at],
            device_id={"fluid": f, "wall": peer}, device_id_type=MESH)

    for d in sorted(range(1, nw), key=lambda d: -min(d, nw - d)):
        wall_copy(lax.rem(w + d, nw), w).start()
    pr[w] = owned
    for x in range(CX):
        for c in range(3):
            adj[c, x] = adj[c, x] + unpack_edges(fix2[c], x)
    wait_halo_sent(halo)
    wait_halo_sent(halo2)
    sent1()
    sent2()
    for d in range(1, nw):
        peer = lax.rem(w + d, nw)
        wall_copy(peer, peer).wait_recv()
    total = pr[0]
    for p in range(1, nw):
        total = total + pr[p]
    mine = jnp.sum(jnp.where(iota((8, TW), 0) == w, total, 0.0), axis=0, keepdims=True)
    sens_out[...] = sens_scale * mine[:, 0:REG_DEV]
    for d in range(1, nw):
        peer = lax.rem(w + d, nw)
        wall_copy(peer, peer).wait_send()


def write_out(vn, adj, sens, vn_out, adj_out, sens_out, sems):
    copies = [pltpu.make_async_copy(sens, sens_out, sems.at[0])]
    for c in range(3):
        copies.append(pltpu.make_async_copy(vn.at[c], vn_out.at[c], sems.at[1 + c]))
        copies.append(pltpu.make_async_copy(adj.at[c], adj_out.at[c], sems.at[4 + c]))
    for copy in copies:
        copy.start()
    for copy in copies:
        copy.wait()


def solution(mesh):
    nf, nw = mesh.shape["fluid"], mesh.shape["wall"]

    def body(flow_state, regions, obs_tiles, measured, tile_dest, cell_list):
        tiles = obs_tiles.shape[2]
        in_hbm = pl.BlockSpec(memory_space=pltpu.HBM)
        in_vmem = pl.BlockSpec(memory_space=pltpu.VMEM)
        dma = pltpu.SemaphoreType.DMA
        vn, adj, sens = pl.pallas_call(
            functools.partial(kernel, nf, nw, tiles),
            out_shape=(
                pltpu.VMEM((3, CX, CY, TW), F32),
                pltpu.VMEM((3, CX, CY, TW), F32),
                pltpu.VMEM((1, REG_DEV), F32),
            ),
            in_specs=[in_hbm] * 6,
            out_specs=(in_vmem, in_vmem, in_vmem),
            scratch_shapes=[
                pltpu.VMEM((4, CX + 2, ROWS, TW), F32),
                pltpu.VMEM((3, CX + 2, ROWS, TW), F32),
                pltpu.VMEM((2, 4, CY, TW), BF16),
                pltpu.VMEM((2, 4, CY, TW), BF16),
                pltpu.VMEM((2, 3, CY, TW), BF16),
                pltpu.VMEM((2, 3, CY, TW), BF16),
                pltpu.VMEM((CX + 1, CY, TW), F32),
                pltpu.VMEM((CX, ROWS - TOP, TW), F32),
                pltpu.VMEM((CX, CY, TW), F32),
                pltpu.VMEM((CX, CY, TW), F32),
                pltpu.VMEM((8, TW), F32),
                pltpu.VMEM((3, 8, TW), F32),
                pltpu.VMEM((4, 8, TW), F32),
                pltpu.VMEM((4, 8, TW), F32),
                pltpu.VMEM((4, 8, TW), F32),
                pltpu.VMEM((3, 8, TW), F32),
                pltpu.VMEM((3, 8, TW), F32),
                pltpu.VMEM((3, 8, TW), F32),
                pltpu.VMEM((tiles, TW, TW), BF16),
                pltpu.VMEM((CX, CY, TW), jnp.int32),
                pltpu.VMEM((tiles // 2, 2 * MSG, 2 * TW), F32),
                pltpu.VMEM((tiles // 2, 2 * MSG, 2 * TW), F32),
                pltpu.VMEM((nf * CAP, CELLS), BF16),
                pltpu.VMEM((CELLS, TW), BF16),
                pltpu.VMEM((nf, TW), BF16),
                pltpu.VMEM((CELLS, 3 * TW), BF16),
                pltpu.VMEM((nf * MSG, TW), F32),
                pltpu.VMEM((nf, MSG, TW), BF16),
                pltpu.VMEM((nf, MSG, TW), BF16),
                pltpu.VMEM((tiles // 2, 2 * MSG, 2 * TW), BF16),
                pltpu.VMEM((tiles * MSG, TW), F32),
                pltpu.VMEM((nf, MSG, TW), BF16),
                pltpu.VMEM((nf, MSG, TW), BF16),
                pltpu.VMEM((TW, 3 * TW), BF16),
                pltpu.VMEM((CX * 4 * TW, TW), BF16),
                pltpu.VMEM((CX, 4, 4, MSG, TW), BF16),
                pltpu.VMEM((TW, TW), BF16),
                pltpu.VMEM((4, MSG, TW), BF16),
                pltpu.VMEM((TW, TW), BF16),
                pltpu.VMEM((TW // 2, CX * 4 * TW), BF16),
                pltpu.VMEM((TW // 2, TW), F32),
                pltpu.VMEM((8, TW), F32),
                pltpu.VMEM((nw, 8, TW), F32),
                pltpu.VMEM((3, tiles, TW), BF16),
                pltpu.SMEM((tiles,), jnp.int32),
                pltpu.SMEM((CAP, nf), jnp.int32),
                pltpu.SemaphoreType.REGULAR((3,)),
                pltpu.SemaphoreType.REGULAR((3,)),
                dma((9,)),
                dma((4,)),
                dma((4,)),
                dma((4,)),
                dma((4,)),
                dma((nf,)),
                dma((nf,)),
                dma((nf,)),
                dma((nf,)),
                dma((nw,)),
                dma((nw,)),
            ],
            compiler_params=pltpu.CompilerParams(collective_id=0, has_side_effects=True, vmem_limit_bytes=60 * 1024 * 1024),
        )(
            flow_state, regions, obs_tiles[0, 0], measured[0, 0].transpose(1, 0, 2), tile_dest[0, 0],
            cell_list[0, 0].T,
        )
        vn, adj, sens = pl.pallas_call(
            write_out,
            out_shape=tuple(jax.ShapeDtypeStruct(a.shape, a.dtype) for a in (vn, adj, sens)),
            in_specs=[in_vmem, in_vmem, in_vmem],
            out_specs=(in_hbm, in_hbm, in_hbm),
            scratch_shapes=[dma((7,))],
            compiler_params=pltpu.CompilerParams(vmem_limit_bytes=8 << 20),
        )(vn, adj, sens)
        return vn, adj, sens.reshape(REG_DEV)

    in_specs = (
        P(None, "fluid", None, "wall"),
        P("fluid", None, "wall"),
        P("fluid", "wall", None, None, None),
        P("fluid", "wall", None, None, None),
        P("fluid", "wall", None),
        P("fluid", "wall", None, None),
    )
    out_specs = (
        P(None, "fluid", None, "wall"),
        P(None, "fluid", None, "wall"),
        P(("fluid", "wall")),
    )
    return jax.shard_map(body, mesh=mesh, in_specs=in_specs, out_specs=out_specs, check_vma=False)
```

```python
import functools

import jax
import jax.numpy as jnp
from jax import lax
from jax.experimental import pallas as pl
from jax.experimental.pallas import tpu as pltpu
from jax.sharding import PartitionSpec as P

CX, CY, TW = 16, 32, 128
CAP = 4
REG_DEV = 16
CELLS = CX * CY
TOP = 8
END = TOP + CY
ROWS = END + 8
MSG = 16
ROW = 8

time_step = 0.12
nu_floor = 0.1
nu_spread = 0.9
relax_sq = 4.0
sens_scale = 0.03

MESH = pl.DeviceIdType.MESH
F32 = jnp.float32
BF16 = jnp.bfloat16


def iota(shape, dim):
    return lax.broadcasted_iota(jnp.int32, shape, dim)


def viscosity(jumps):
    base = 1.0 + relax_sq * (jumps[0] * jumps[0] + jumps[1] * jumps[1] + jumps[2] * jumps[2])
    root = lax.rsqrt(base)
    return nu_floor + nu_spread * (root * lax.rsqrt(root))


def pack_edges(rows_of, zero):
    half = ((iota((8, TW), 1) + 1) % TW) // 2
    total = None
    for k in range(4):
        packed = zero
        for x in range(CX):
            slot = 4 * x + k
            rows = rows_of(x, k)
            if slot:
                rows = pltpu.roll(rows, 2 * slot, 1)
            packed = jnp.where(half == slot, rows, packed)
        total = packed if total is None else total + packed
    return total


def packed_halo(low, high):
    even = iota((8, TW), 1) % 2 == 0
    return jnp.where(even, pltpu.roll(low, 1, 1), pltpu.roll(high, TW - 1, 1))


def unpack_edges(packed, x):
    rolled = [pltpu.roll(packed, TW - 2 * (4 * x + k), 1) if x + k else packed for k in range(4)]
    lane = iota((CY, TW), 1)
    return jnp.where((lane == 0) | (lane == TW - 1), jnp.concatenate(rolled, axis=0), 0.0)


def region_terms(values, masks):
    twice = [jnp.concatenate([value, value], axis=0).astype(BF16) for value in values]
    rows = [jnp.concatenate([masks(k, pair) * v for k, v in enumerate(twice)], axis=1) for pair in range(4)]
    return jnp.concatenate(rows, axis=0)


def label_pairs(labels, count, store):
    for pair in range(count // 2):
        both = [jnp.where(labels == 2 * pair + i, 1.0, 0.0) for i in range(2)]
        store(pair, jnp.concatenate(both, axis=0).astype(BF16))


def contract_lanes(a, b):
    return lax.dot_general(a, b, (((1,), (1,)), ((), ())), preferred_element_type=F32)


def kernel(
    nf, nw, tiles,
    flow, regions, obs, meas_in, dest_in, cells_in,
    vn, adj, sens_out,
    vp, fp, hxs, hxr, fxs, fxr, nux, nuy, nuz, nuzu, nup, vnp, zo, zl, zh, fo, fl, fh,
    wts, reg, meas16, mask16, gat, gatt, route, obsv, big, sb, rb, mis, contrib, sb2, rb2, rhs,
    onelo, maskhi, onez, maskz, pick, lhs, inner, ps, pr, meas, dest, cells,
    row_sem, wall_sem, load_sem, hs, hr, hs2, hr2, as1, ar1, as2, ar2, ws, wr,
):
    f = lax.axis_index("fluid")
    w = lax.axis_index("wall")
    flow_loads = [
        pltpu.make_async_copy(flow.at[c], vp.at[c, 1 : CX + 1, TOP:END, :], load_sem.at[c]) for c in range(4)
    ]
    for load in flow_loads:
        load.start()
    table_loads = [
        pltpu.make_async_copy(cells_in, cells, load_sem.at[6]),
        pltpu.make_async_copy(dest_in, dest, load_sem.at[7]),
        pltpu.make_async_copy(meas_in, meas, load_sem.at[8]),
    ]
    for load in table_loads:
        load.start()

    def signal(sem, to_f, to_w):
        pl.semaphore_signal(
            sem, inc=1, device_id={"fluid": lax.rem(to_f + nf, nf), "wall": lax.rem(to_w + nw, nw)}, device_id_type=MESH)

    barrier = pltpu.get_barrier_semaphore()
    many_rows = nf > ROW
    in_row = lax.rem(f, ROW)
    flip = 1 - 2 * lax.rem(f, 2)

    def away(dx, dy):
        return lax.rem((f // ROW + dy) * ROW + nf, nf) + lax.rem(in_row + 2 * dx + ROW, ROW)

    beside = [away(1, 0), away(-1, 0)]
    beyond = [away(2, 0)]
    if many_rows:
        beside += [away(0, 1), away(0, -1)]
        beyond += [away(0, 2), away(1, 1), away(1, -1), away(-1, 1), away(-1, -1)]
    near = [(f + 1, w), (f - 1, w), (f, w + 1), (f, w - 1), (f + flip, w)]
    near += [(at, w) for at in beside] + [(at + flip, w) for at in beside]
    for to_f, to_w in near:
        signal(barrier, to_f, to_w)
    rounds = (beside, beyond)

    def pass_rows(stage):
        for at in rounds[stage]:
            signal(row_sem.at[stage], at, w)

    def wait_rows(stage):
        pl.semaphore_wait(row_sem.at[stage], len(rounds[stage]))

    def pass_walls(stage):
        signal(wall_sem.at[stage], f, w + 1)
        signal(wall_sem.at[stage], f, w - 1)

    def wait_walls(stage):
        pl.semaphore_wait(wall_sem.at[stage], 2)

    def halo_copies(low_src, low_dst, high_src, high_dst, packed, from_low, from_high, ss, rr):
        up = pltpu.make_async_remote_copy(
            src_ref=high_src, dst_ref=low_dst, send_sem=ss.at[0], recv_sem=rr.at[0],
            device_id={"fluid": lax.rem(f + 1, nf), "wall": w}, device_id_type=MESH)
        down = pltpu.make_async_remote_copy(
            src_ref=low_src, dst_ref=high_dst, send_sem=ss.at[1], recv_sem=rr.at[1],
            device_id={"fluid": lax.rem(f + nf - 1, nf), "wall": w}, device_id_type=MESH)
        right = pltpu.make_async_remote_copy(
            src_ref=packed, dst_ref=from_low, send_sem=ss.at[2], recv_sem=rr.at[2],
            device_id={"fluid": f, "wall": lax.rem(w + 1, nw)}, device_id_type=MESH)
        left = pltpu.make_async_remote_copy(
            src_ref=packed, dst_ref=from_high, send_sem=ss.at[3], recv_sem=rr.at[3],
            device_id={"fluid": f, "wall": lax.rem(w + nw - 1, nw)}, device_id_type=MESH)
        return up, down, right, left

    def start_x(copies):
        pl.when(f < nf - 1)(copies[0].start)
        pl.when(f > 0)(copies[1].start)

    def start_z(copies):
        pl.when(w < nw - 1)(copies[2].start)
        pl.when(w > 0)(copies[3].start)

    def wait_halo(copies):
        pl.when(f > 0)(copies[0].wait_recv)
        pl.when(f < nf - 1)(copies[1].wait_recv)
        pl.when(w > 0)(copies[2].wait_recv)
        pl.when(w < nw - 1)(copies[3].wait_recv)

    def wait_halo_sent(copies):
        pl.when(f < nf - 1)(copies[0].wait_send)
        pl.when(f > 0)(copies[1].wait_send)
        pl.when(w < nw - 1)(copies[2].wait_send)
        pl.when(w > 0)(copies[3].wait_send)

    @pl.when(f == 0)
    def _():
        hxr[0] = jnp.zeros((4, CY, TW), BF16)
        fxr[0] = jnp.zeros((3, CY, TW), BF16)

    @pl.when(f == nf - 1)
    def _():
        hxr[1] = jnp.zeros((4, CY, TW), BF16)
        fxr[1] = jnp.zeros((3, CY, TW), BF16)

    @pl.when(w == 0)
    def _():
        zl[...] = jnp.zeros((4, 8, TW), F32)
        fl[...] = jnp.zeros((3, 8, TW), F32)

    @pl.when(w == nw - 1)
    def _():
        zh[...] = jnp.zeros((4, 8, TW), F32)
        fh[...] = jnp.zeros((3, 8, TW), F32)

    row16 = iota((MSG, TW), 0)
    lane16 = iota((MSG, TW), 1)
    slot16 = row16 // CAP
    comp16 = row16 % CAP

    def build_gather(i, _):
        ids = jnp.full((MSG, TW), -1, jnp.int32)
        for u in range(MSG):
            ids = jnp.where(row16 == u, cells[u % CAP, 4 * i + u // CAP], ids)
        at = pl.ds(pl.multiple_of(i * MSG, MSG), MSG)
        for q in range(CELLS // TW):
            gat[at, q * TW : (q + 1) * TW] = jnp.where(ids == lane16 + q * TW, 1.0, 0.0).astype(BF16)
        return 0

    def zero_pads(x, _):
        for c in range(4):
            vp[c, x + 1, 0:TOP, :] = jnp.zeros((TOP, TW), F32)
            vp[c, x + 1, END:ROWS, :] = jnp.zeros((ROWS - END, TW), F32)
        for c in range(3):
            fp[c, x + 1, 0:TOP, :] = jnp.zeros((TOP, TW), F32)
            fp[c, x + 1, END:ROWS, :] = jnp.zeros((ROWS - END, TW), F32)
        return 0

    lax.fori_loop(0, CX, zero_pads, 0)

    for c in range(4):
        flow_loads[c].wait()
        hxs[0, c] = vp[c, 1, TOP:END, :].astype(BF16)
        hxs[1, c] = vp[c, CX, TOP:END, :].astype(BF16)
        zo[c] = pack_edges(lambda x, k: vp[c, x + 1, TOP + 8 * k : TOP + 8 * k + 8, :], jnp.zeros((8, TW), F32))
    halo = halo_copies(
        hxs.at[0], hxr.at[0], hxs.at[1], hxr.at[1], zo, zl, zh, hs, hr)
    pl.semaphore_wait(barrier, len(near))
    start_x(halo)
    start_z(halo)
    pass_rows(0)
    pass_walls(0)
    reg_load = pltpu.make_async_copy(regions, reg, load_sem.at[4])
    reg_load.start()
    obs_load = pltpu.make_async_copy(obs, wts, load_sem.at[5])
    obs_load.start()
    big[...] = jnp.zeros((nf * MSG, TW), F32)
    for load in table_loads:
        load.wait()
    lax.fori_loop(0, nf // 4, build_gather, 0)

    lane32 = iota((CY, TW), 1)
    first_lane = lane32 == 0
    last_lane = lane32 == TW - 1

    def forward_plane(x, carry, last):
        low_flux, low_p = carry[:3], carry[3]
        cur = [vp[c, x + 1, TOP:END, :] for c in range(4)]
        if last:
            flux_x = [jnp.zeros((CY, TW), F32) for _ in range(3)]
            high_p = jnp.zeros((CY, TW), F32)
        else:
            jump = [vp[c, x + 2, TOP:END, :] - cur[c] for c in range(3)]
            nu = viscosity(jump)
            nux[x + 1] = nu
            flux_x = [nu * j for j in jump]
            high_p = vp[3, x + 2, TOP:END, :]
        jump = [vp[c, x + 1, TOP:ROWS, :] - vp[c, x + 1, TOP - 1 : ROWS - 1, :] for c in range(3)]
        nu = viscosity(jump)
        nuy[x] = nu
        flux_y = [nu * j for j in jump]
        jump = [cur[c] - pltpu.roll(cur[c], 1, 1) for c in range(3)]
        nu = jnp.where(first_lane, 0.0, viscosity(jump))
        nuz[x] = nu
        nu_up = pltpu.roll(nu, TW - 1, 1)
        nuzu[x] = nu_up
        flux_z = [nu_up * (pltpu.roll(cur[c], TW - 1, 1) - cur[c]) - nu * jump[c] for c in range(3)]
        grad = [
            high_p - low_p,
            vp[3, x + 1, TOP + 1 : END + 1, :] - vp[3, x + 1, TOP - 1 : END - 1, :],
            jnp.where(last_lane, 0.0, pltpu.roll(cur[3], TW - 1, 1)) - jnp.where(first_lane, 0.0, pltpu.roll(cur[3], 1, 1)),
        ]
        for c in range(3):
            div = (flux_x[c] - low_flux[c]) + (flux_y[c][1 : CY + 1] - flux_y[c][0:CY])
            div = div + flux_z[c]
            vn[c, x] = cur[c] + time_step * (div - 0.5 * grad[c])
        return (*flux_x, cur[3])

    start = tuple(jnp.zeros((CY, TW), F32) for _ in range(4))
    carry = lax.fori_loop(0, 9, lambda x, carry: forward_plane(x, carry, False), start, unroll=3)
    wait_rows(0)
    pass_rows(1)
    carry = lax.fori_loop(9, CX - 1, lambda x, carry: forward_plane(x, carry, False), carry, unroll=3)
    forward_plane(CX - 1, carry, True)

    wait_walls(0)
    pass_walls(1)
    wait_halo(halo)
    for plane, side, face, sign in ((0, 0, 0, 1.0), (CX - 1, 1, CX, -1.0)):
        ghost = [hxr[side, c].astype(F32) for c in range(4)]
        jump = [ghost[c] - vp[c, plane + 1, TOP:END, :] for c in range(3)]
        nu = viscosity(jump)
        nux[face] = nu
        for c in range(3):
            add = nu * jump[c]
            if c == 0:
                add = add + (0.5 * sign) * ghost[3]
            vn[c, plane] = vn[c, plane] + time_step * add
    halo_p = packed_halo(zl[3], zh[3])
    jump = [packed_halo(zl[c], zh[c]) - zo[c] for c in range(3)]
    nu = viscosity(jump)
    nup[...] = nu
    even = iota((8, TW), 1) % 2 == 0
    fix = [time_step * nu * j for j in jump]
    fix[2] = fix[2] + jnp.where(even, 0.5 * time_step, -0.5 * time_step) * halo_p

    for x in range(CX):
        for c in range(3):
            value = vn[c, x] + unpack_edges(fix[c], x)
            vn[c, x] = value
            obsv[x * CY : (x + 1) * CY, c * TW : (c + 1) * TW] = value.astype(BF16)

    picked = jnp.dot(gat[...], obsv[...], preferred_element_type=F32)
    for c in range(3):
        big[pl.ds(c, nf * CAP, stride=CAP), :] = picked[:, c * TW : (c + 1) * TW]
    sb[...] = big[...].astype(BF16).reshape(nf, MSG, TW)

    def hops(d):
        chip, side = d // 2, 4
        return sum(min(at, side - at) for at in (chip % side, chip // side % side))

    far_first = sorted(range(1, nf), key=lambda d: -hops(d))

    def exchange(src, dst, ss, rr):
        def send():
            for d in far_first:
                peer = lax.rem(f + d, nf)
                pltpu.make_async_remote_copy(
                    src_ref=src.at[peer], dst_ref=dst.at[f], send_sem=ss, recv_sem=rr,
                    device_id={"fluid": peer, "wall": w}, device_id_type=MESH).start()

        every = pltpu.make_async_remote_copy(
            src_ref=src.at[0 : nf - 1], dst_ref=dst.at[0 : nf - 1], send_sem=ss, recv_sem=rr,
            device_id={"fluid": lax.rem(f + 1, nf), "wall": w}, device_id_type=MESH)
        return send, every.wait_recv, every.wait_send

    send1, receive1, sent1 = exchange(sb, rb, as1, ar1)
    send2, receive2, sent2 = exchange(sb2, rb2, as2, ar2)
    wait_rows(1)
    send1()
    wait_walls(1)
    pass_walls(2)
    rb[f] = sb[f]

    by_tile = [meas[c].astype(F32) for c in range(3)]
    dest_lane = jnp.full((MSG, TW), -1, jnp.int32)
    for t in range(tiles):
        dest_lane = jnp.where(lane16 == t, dest[t], dest_lane)
    for t in range(tiles):
        earlier = jnp.where((dest_lane == dest[t]) & (lane16 < t), 1.0, 0.0)
        rank = jnp.sum(earlier, axis=1, keepdims=True)
        at_row, at_lane = MSG * (t % 2), TW * (t % 2)
        blank = jnp.zeros((MSG, TW), F32)
        mask16[t // 2, at_row : at_row + MSG, at_lane : at_lane + TW] = jnp.where(
            (slot16.astype(F32) == rank) & (comp16 < 3), 1.0, 0.0)
        mask16[t // 2, at_row : at_row + MSG, TW - at_lane : 2 * TW - at_lane] = blank
        meas16[t // 2, at_row : at_row + MSG, TW - at_lane : 2 * TW - at_lane] = blank
        meas16[t // 2, at_row : at_row + MSG, at_lane : at_lane + TW] = jnp.where(
            comp16 == 0, by_tile[0][t : t + 1],
            jnp.where(comp16 == 1, by_tile[1][t : t + 1], jnp.where(comp16 == 2, by_tile[2][t : t + 1], 0.0)))
    route[...] = jnp.where(jnp.broadcast_to(dest_lane[0:1], (nf, TW)) == iota((nf, TW), 0), 1.0, 0.0).astype(BF16)
    cell_of = jnp.full((MSG, TW), -1, jnp.int32)
    for p in range(nf):
        for k in range(CAP):
            cell_of = jnp.where(lane16 == p * CAP + k, cells[k, p], cell_of)

    def build_scatter(i, _):
        at = pl.ds(pl.multiple_of(i * MSG, MSG), MSG)
        first = jnp.where(i < 2, i * MSG, jnp.where(i < 4, (i + 2 * CX - 4) * MSG, (i - 2) * MSG))
        gatt[at, :] = jnp.where(cell_of == row16 + first, 1.0, 0.0).astype(BF16)
        return 0

    lax.fori_loop(0, CELLS // MSG, build_scatter, 0, unroll=4)
    if nf * CAP < TW:
        rhs[...] = jnp.zeros((TW, 3 * TW), BF16)
    reg_load.wait()

    label_of_lane = iota((TW, TW), 1) // 8

    def by_fine_label(ids):
        fine = jnp.concatenate([(ids % REG_DEV).astype(F32)] * REG_DEV, axis=0)
        return jnp.where(fine.T == label_of_lane.astype(F32), 1.0, 0.0).astype(BF16)

    def build_regions(x, _):
        for k in range(4):
            ids = reg[x, 8 * k : 8 * k + 8, :]
            onelo[pl.ds(pl.multiple_of((4 * x + k) * TW, TW), TW), :] = by_fine_label(ids)

            def store_mask(pair, rows, k=k):
                maskhi[x, k, pair] = rows

            label_pairs(ids // REG_DEV, 8, store_mask)
        return 0

    lax.fori_loop(0, CX, build_regions, 0)
    packed_ids = pack_edges(lambda x, k: reg[x, 8 * k : 8 * k + 8, :], jnp.zeros((8, TW), jnp.int32))

    onez[...] = by_fine_label(packed_ids)

    def store_zmask(pair, rows):
        maskz[pair] = rows

    label_pairs(packed_ids // REG_DEV, 8, store_zmask)
    pick[...] = jnp.where(iota((TW, TW), 0) // 8 == iota((TW, TW), 1), 1.0, 0.0).astype(BF16)
    obs_load.wait()
    receive1()
    for p in range(tiles // 2):
        pair = wts[2 * p : 2 * p + 2].reshape(2 * TW, TW)
        predicted = contract_lanes(jnp.concatenate([rb[dest[2 * p]], rb[dest[2 * p + 1]]], axis=0), pair)
        mis[p] = ((predicted - meas16[p]) * mask16[p]).astype(BF16)
    for p in range(tiles // 2):
        pair = wts[2 * p : 2 * p + 2].reshape(2 * TW, TW)
        contrib[2 * p * MSG : 2 * (p + 1) * MSG, :] = jnp.dot(mis[p], pair, preferred_element_type=F32)
    used = [r for r in range(MSG) if r % CAP < 3]
    flat = jnp.concatenate([contrib[pl.ds(r, tiles, stride=MSG), :].astype(BF16) for r in used], axis=1)
    routed = jnp.dot(route[:, 0:tiles], flat, preferred_element_type=F32)
    for i, r in enumerate(used):
        big[pl.ds(r, nf, stride=MSG), :] = routed[:, i * TW : (i + 1) * TW]
    sb2[...] = big[...].astype(BF16).reshape(nf, MSG, TW)
    send2()
    wait_walls(2)
    rb2[f] = sb2[f]

    for c in range(3):
        vnp[c] = pack_edges(lambda x, k: vn[c, x, 8 * k : 8 * k + 8, :], jnp.zeros((8, TW), F32))
    receive2()
    big[...] = rb2[...].reshape(nf * MSG, TW).astype(F32)
    for c in range(3):
        rhs[0 : nf * CAP, c * TW : (c + 1) * TW] = big[pl.ds(c, nf * CAP, stride=CAP), :].astype(BF16)

    def force_rows(first, planes):
        rows = gatt[first * CY : (first + len(planes)) * CY, :]
        force = jnp.dot(rows, rhs[...], preferred_element_type=F32)
        for i, x in enumerate(planes):
            for c in range(3):
                fp[c, x + 1, TOP:END, :] = force[i * CY : (i + 1) * CY, c * TW : (c + 1) * TW]

    force_rows(0, (0, CX - 1))
    for c in range(3):
        fxs[0, c] = fp[c, 1, TOP:END, :].astype(BF16)
        fxs[1, c] = fp[c, CX, TOP:END, :].astype(BF16)
    halo2 = halo_copies(
        fxs.at[0], fxr.at[0], fxs.at[1], fxr.at[1], fo, fl, fh, hs2, hr2)
    start_x(halo2)
    force_rows(2, range(1, CX - 1))
    for c in range(3):
        fo[c] = pack_edges(lambda x, k: fp[c, x + 1, TOP + 8 * k : TOP + 8 * k + 8, :], jnp.zeros((8, TW), F32))
    start_z(halo2)

    def plane_sums(x, total):
        at = pl.ds(pl.multiple_of(x * 4 * TW, TW), 4 * TW)
        terms = region_terms([total[8 * k : 8 * k + 8] for k in range(4)], lambda k, h: maskhi[x, k, h])
        return jnp.dot(terms, onelo[at, :], preferred_element_type=F32)

    def adjoint_plane(x, carry, last):
        flux_x = []
        total = None
        for c in range(3):
            cur = fp[c, x + 1, TOP:END, :]
            if last:
                flux = jnp.zeros((CY, TW), F32)
            else:
                flux = nux[x + 1] * (fp[c, x + 2, TOP:END, :] - cur)
            flux_x.append(flux)
            div = flux - carry[c]
            div = div + nuy[x, 1 : CY + 1, :] * (fp[c, x + 1, TOP + 1 : END + 1, :] - cur)
            div = div - nuy[x, 0:CY, :] * (cur - fp[c, x + 1, TOP - 1 : END - 1, :])
            div = div + nuzu[x] * (pltpu.roll(cur, TW - 1, 1) - cur)
            div = div - nuz[x] * (cur - pltpu.roll(cur, 1, 1))
            value = cur + time_step * div
            adj[c, x] = value
            part = value * vn[c, x]
            total = part if total is None else total + part
        at = pl.ds(pl.multiple_of(x * 4 * TW, 4 * TW), 4 * TW)
        lhs[:, at] = region_terms([total[8 * k : 8 * k + 8] for k in range(4)], lambda k, h: maskhi[x, k, h])
        return tuple(flux_x)

    carry = lax.fori_loop(0, CX - 1, lambda x, carry: adjoint_plane(x, carry, False), start[:3], unroll=3)
    adjoint_plane(CX - 1, carry, True)
    inner[...] = jnp.dot(lhs[...], onelo[...], preferred_element_type=F32)

    wait_halo(halo2)
    fix2 = [time_step * nup[...] * (packed_halo(fl[c], fh[c]) - fo[c]) for c in range(3)]
    total = fix2[0] * vnp[0] + fix2[1] * vnp[1] + fix2[2] * vnp[2]
    terms = region_terms([total], lambda k, h: maskz[h])
    sums = inner[...] + jnp.dot(terms, onez[...], preferred_element_type=F32)
    for plane, side, face in ((0, 0, 0), (CX - 1, 1, CX)):
        total = None
        for c in range(3):
            jump = fxr[side, c].astype(F32) - fp[c, plane + 1, TOP:END, :]
            value = time_step * (nux[face] * jump)
            adj[c, plane] = adj[c, plane] + value
            part = value * vn[c, plane]
            total = part if total is None else total + part
        sums = sums + plane_sums(plane, total)

    sums = jnp.where(iota((TW // 2, TW), 0) % 8 == iota((TW // 2, TW), 1) % 8, sums, 0.0)
    coarse_rows = [jnp.sum(sums[8 * h : 8 * h + 8], axis=0, keepdims=True) for h in range(8)]
    by_label = jnp.concatenate(coarse_rows, axis=0)
    parts = []
    for _ in range(3):
        part = by_label.astype(BF16)
        parts.append(part)
        by_label = by_label - part.astype(F32)
    owned = jnp.dot(jnp.concatenate(parts, axis=0), pick[...], preferred_element_type=F32)
    owned = owned[0:8] + owned[8:16] + owned[16:24]
    for p in range(nw):
        ps[p] = owned

    def wall_copy(peer, src, dst):
        return pltpu.make_async_remote_copy(
            src_ref=src, dst_ref=dst, send_sem=ws, recv_sem=wr,
            device_id={"fluid": f, "wall": peer}, device_id_type=MESH)

    every_wall = wall_copy(lax.rem(w + 1, nw), ps.at[0 : nw - 1], pr.at[0 : nw - 1])
    for d in sorted(range(1, nw), key=lambda d: -min(d, nw - d)):
        peer = lax.rem(w + d, nw)
        wall_copy(peer, ps.at[peer], pr.at[w]).start()
    pr[w] = owned
    for x in range(CX):
        for c in range(3):
            adj[c, x] = adj[c, x] + unpack_edges(fix2[c], x)
    wait_halo_sent(halo)
    wait_halo_sent(halo2)
    sent1()
    sent2()
    every_wall.wait_recv()
    total = pr[0]
    for p in range(1, nw):
        total = total + pr[p]
    mine = jnp.sum(jnp.where(iota((8, TW), 0) == w, total, 0.0), axis=0, keepdims=True)
    sens_out[...] = sens_scale * mine[:, 0:REG_DEV]
    every_wall.wait_send()


def write_out(vn, adj, sens, vn_out, adj_out, sens_out, sems):
    copies = [pltpu.make_async_copy(sens, sens_out, sems.at[0])]
    for c in range(3):
        copies.append(pltpu.make_async_copy(vn.at[c], vn_out.at[c], sems.at[1 + c]))
        copies.append(pltpu.make_async_copy(adj.at[c], adj_out.at[c], sems.at[4 + c]))
    for copy in copies:
        copy.start()
    for copy in copies:
        copy.wait()


def solution(mesh):
    nf, nw = mesh.shape["fluid"], mesh.shape["wall"]

    def body(flow_state, regions, obs_tiles, measured, tile_dest, cell_list):
        tiles = obs_tiles.shape[2]
        in_hbm = pl.BlockSpec(memory_space=pltpu.HBM)
        in_vmem = pl.BlockSpec(memory_space=pltpu.VMEM)
        dma = pltpu.SemaphoreType.DMA
        vn, adj, sens = pl.pallas_call(
            functools.partial(kernel, nf, nw, tiles),
            out_shape=(
                pltpu.VMEM((3, CX, CY, TW), F32),
                pltpu.VMEM((3, CX, CY, TW), F32),
                pltpu.VMEM((1, REG_DEV), F32),
            ),
            in_specs=[in_hbm] * 6,
            out_specs=(in_vmem, in_vmem, in_vmem),
            scratch_shapes=[
                pltpu.VMEM((4, CX + 2, ROWS, TW), F32),
                pltpu.VMEM((3, CX + 2, ROWS, TW), F32),
                pltpu.VMEM((2, 4, CY, TW), BF16),
                pltpu.VMEM((2, 4, CY, TW), BF16),
                pltpu.VMEM((2, 3, CY, TW), BF16),
                pltpu.VMEM((2, 3, CY, TW), BF16),
                pltpu.VMEM((CX + 1, CY, TW), F32),
                pltpu.VMEM((CX, ROWS - TOP, TW), F32),
                pltpu.VMEM((CX, CY, TW), F32),
                pltpu.VMEM((CX, CY, TW), F32),
                pltpu.VMEM((8, TW), F32),
                pltpu.VMEM((3, 8, TW), F32),
                pltpu.VMEM((4, 8, TW), F32),
                pltpu.VMEM((4, 8, TW), F32),
                pltpu.VMEM((4, 8, TW), F32),
                pltpu.VMEM((3, 8, TW), F32),
                pltpu.VMEM((3, 8, TW), F32),
                pltpu.VMEM((3, 8, TW), F32),
                pltpu.VMEM((tiles, TW, TW), BF16),
                pltpu.VMEM((CX, CY, TW), jnp.int32),
                pltpu.VMEM((tiles // 2, 2 * MSG, 2 * TW), F32),
                pltpu.VMEM((tiles // 2, 2 * MSG, 2 * TW), F32),
                pltpu.VMEM((nf * CAP, CELLS), BF16),
                pltpu.VMEM((CELLS, TW), BF16),
                pltpu.VMEM((nf, TW), BF16),
                pltpu.VMEM((CELLS, 3 * TW), BF16),
                pltpu.VMEM((nf * MSG, TW), F32),
                pltpu.VMEM((nf, MSG, TW), BF16),
                pltpu.VMEM((nf, MSG, TW), BF16),
                pltpu.VMEM((tiles // 2, 2 * MSG, 2 * TW), BF16),
                pltpu.VMEM((tiles * MSG, TW), F32),
                pltpu.VMEM((nf, MSG, TW), BF16),
                pltpu.VMEM((nf, MSG, TW), BF16),
                pltpu.VMEM((TW, 3 * TW), BF16),
                pltpu.VMEM((CX * 4 * TW, TW), BF16),
                pltpu.VMEM((CX, 4, 4, MSG, TW), BF16),
                pltpu.VMEM((TW, TW), BF16),
                pltpu.VMEM((4, MSG, TW), BF16),
                pltpu.VMEM((TW, TW), BF16),
                pltpu.VMEM((TW // 2, CX * 4 * TW), BF16),
                pltpu.VMEM((TW // 2, TW), F32),
                pltpu.VMEM((nw, 8, TW), F32),
                pltpu.VMEM((nw, 8, TW), F32),
                pltpu.VMEM((3, tiles, TW), BF16),
                pltpu.SMEM((tiles,), jnp.int32),
                pltpu.SMEM((CAP, nf), jnp.int32),
                pltpu.SemaphoreType.REGULAR((2,)),
                pltpu.SemaphoreType.REGULAR((3,)),
                dma((9,)),
                dma((4,)),
                dma((4,)),
                dma((4,)),
                dma((4,)),
                dma(()),
                dma(()),
                dma(()),
                dma(()),
                dma(()),
                dma(()),
            ],
            compiler_params=pltpu.CompilerParams(collective_id=0, has_side_effects=True, vmem_limit_bytes=60 * 1024 * 1024),
        )(
            flow_state, regions, obs_tiles[0, 0], measured[0, 0].transpose(1, 0, 2), tile_dest[0, 0],
            cell_list[0, 0].T,
        )
        vn, adj, sens = pl.pallas_call(
            write_out,
            out_shape=tuple(jax.ShapeDtypeStruct(a.shape, a.dtype) for a in (vn, adj, sens)),
            in_specs=[in_vmem, in_vmem, in_vmem],
            out_specs=(in_hbm, in_hbm, in_hbm),
            scratch_shapes=[dma((7,))],
            compiler_params=pltpu.CompilerParams(vmem_limit_bytes=8 << 20),
        )(vn, adj, sens)
        return vn, adj, sens.reshape(REG_DEV)

    in_specs = (
        P(None, "fluid", None, "wall"),
        P("fluid", None, "wall"),
        P("fluid", "wall", None, None, None),
        P("fluid", "wall", None, None, None),
        P("fluid", "wall", None),
        P("fluid", "wall", None, None),
    )
    out_specs = (
        P(None, "fluid", None, "wall"),
        P(None, "fluid", None, "wall"),
        P(("fluid", "wall")),
    )
    return jax.shard_map(body, mesh=mesh, in_specs=in_specs, out_specs=out_specs, check_vma=False)
```

```python
import functools

import jax
import jax.numpy as jnp
from jax import lax
from jax.experimental import pallas as pl
from jax.experimental.pallas import tpu as pltpu
from jax.sharding import PartitionSpec as P

CX, CY, TW = 16, 32, 128
CAP = 4
REG_DEV = 16
CELLS = CX * CY
TOP = 8
END = TOP + CY
ROWS = END + 8
MSG = 16
ROW = 8

time_step = 0.12
nu_floor = 0.1
nu_spread = 0.9
relax_sq = 4.0
sens_scale = 0.03

MESH = pl.DeviceIdType.MESH
F32 = jnp.float32
BF16 = jnp.bfloat16


def iota(shape, dim):
    return lax.broadcasted_iota(jnp.int32, shape, dim)


def viscosity(jumps):
    base = 1.0 + relax_sq * (jumps[0] * jumps[0] + jumps[1] * jumps[1] + jumps[2] * jumps[2])
    root = lax.rsqrt(base)
    return nu_floor + nu_spread * (root * lax.rsqrt(root))


def pack_edges(rows_of, zero):
    half = ((iota((8, TW), 1) + 1) % TW) // 2
    total = None
    for k in range(4):
        packed = zero
        for x in range(CX):
            slot = 4 * x + k
            rows = rows_of(x, k)
            if slot:
                rows = pltpu.roll(rows, 2 * slot, 1)
            packed = jnp.where(half == slot, rows, packed)
        total = packed if total is None else total + packed
    return total


def packed_halo(low, high):
    even = iota((8, TW), 1) % 2 == 0
    return jnp.where(even, pltpu.roll(low, 1, 1), pltpu.roll(high, TW - 1, 1))


def unpack_edges(packed, x):
    rolled = [pltpu.roll(packed, TW - 2 * (4 * x + k), 1) if x + k else packed for k in range(4)]
    lane = iota((CY, TW), 1)
    return jnp.where((lane == 0) | (lane == TW - 1), jnp.concatenate(rolled, axis=0), 0.0)


def region_terms(values, masks):
    twice = [jnp.concatenate([value, value], axis=0).astype(BF16) for value in values]
    rows = [jnp.concatenate([masks(k, pair) * v for k, v in enumerate(twice)], axis=1) for pair in range(4)]
    return jnp.concatenate(rows, axis=0)


def label_pairs(labels, count, store):
    for pair in range(count // 2):
        both = [jnp.where(labels == 2 * pair + i, 1.0, 0.0) for i in range(2)]
        store(pair, jnp.concatenate(both, axis=0).astype(BF16))


def contract_lanes(a, b):
    return lax.dot_general(a, b, (((1,), (1,)), ((), ())), preferred_element_type=F32)


def kernel(
    nf, nw, tiles,
    flow, regions, obs, meas_in, dest_in, cells_in,
    vn, adj, sens_out,
    vp, fp, hxs, hxr, fxs, fxr, nux, nuy, nuz, nuzu, nup, vnp, zo, zl, zh, fo, fl, fh,
    wts, reg, meas16, mask16, gat, gatt, route, obsv, big, sb, rb, mis, contrib, sb2, rb2, rhs,
    onelo, maskhi, onez, maskz, pick, lhs, inner, ps, pr, meas, dest, cells,
    row_sem, wall_sem, load_sem, hs, hr, hs2, hr2, as1, ar1, as2, ar2, ws, wr,
):
    f = lax.axis_index("fluid")
    w = lax.axis_index("wall")
    flow_loads = [
        pltpu.make_async_copy(flow.at[c], vp.at[c, 1 : CX + 1, TOP:END, :], load_sem.at[c]) for c in range(4)
    ]
    for load in flow_loads:
        load.start()
    table_loads = [
        pltpu.make_async_copy(cells_in, cells, load_sem.at[6]),
        pltpu.make_async_copy(dest_in, dest, load_sem.at[7]),
        pltpu.make_async_copy(meas_in, meas, load_sem.at[8]),
    ]
    for load in table_loads:
        load.start()

    def signal(sem, to_f, to_w):
        pl.semaphore_signal(
            sem, inc=1, device_id={"fluid": lax.rem(to_f + nf, nf), "wall": lax.rem(to_w + nw, nw)}, device_id_type=MESH)

    barrier = pltpu.get_barrier_semaphore()
    many_rows = nf > ROW
    in_row = lax.rem(f, ROW)
    flip = 1 - 2 * lax.rem(f, 2)

    def away(dx, dy):
        return lax.rem((f // ROW + dy) * ROW + nf, nf) + lax.rem(in_row + 2 * dx + ROW, ROW)

    beside = [away(1, 0), away(-1, 0)]
    beyond = [away(2, 0)]
    if many_rows:
        beside += [away(0, 1), away(0, -1)]
        beyond += [away(0, 2), away(1, 1), away(1, -1), away(-1, 1), away(-1, -1)]
    near = [(f, w + 1), (f, w - 1), (f + flip, w)]
    near += [(at, w) for at in beside] + [(at + flip, w) for at in beside]
    pl.when(f < nf - 1)(lambda: signal(barrier, f + 1, w))
    pl.when(f > 0)(lambda: signal(barrier, f - 1, w))
    for to_f, to_w in near:
        signal(barrier, to_f, to_w)
    expected = len(near) + (f + nf - 1) // nf + (2 * nf - 2 - f) // nf
    rounds = (beside, beyond)

    def pass_rows(stage):
        for at in rounds[stage]:
            signal(row_sem.at[stage], at, w)

    def wait_rows(stage):
        pl.semaphore_wait(row_sem.at[stage], len(rounds[stage]))

    def pass_walls(stage):
        signal(wall_sem.at[stage], f, w + 1)
        signal(wall_sem.at[stage], f, w - 1)

    def wait_walls(stage):
        pl.semaphore_wait(wall_sem.at[stage], 2)

    def halo_copies(low_src, low_dst, high_src, high_dst, packed, from_low, from_high, ss, rr):
        up = pltpu.make_async_remote_copy(
            src_ref=high_src, dst_ref=low_dst, send_sem=ss.at[0], recv_sem=rr.at[0],
            device_id={"fluid": lax.rem(f + 1, nf), "wall": w}, device_id_type=MESH)
        down = pltpu.make_async_remote_copy(
            src_ref=low_src, dst_ref=high_dst, send_sem=ss.at[1], recv_sem=rr.at[1],
            device_id={"fluid": lax.rem(f + nf - 1, nf), "wall": w}, device_id_type=MESH)
        right = pltpu.make_async_remote_copy(
            src_ref=packed, dst_ref=from_low, send_sem=ss.at[2], recv_sem=rr.at[2],
            device_id={"fluid": f, "wall": lax.rem(w + 1, nw)}, device_id_type=MESH)
        left = pltpu.make_async_remote_copy(
            src_ref=packed, dst_ref=from_high, send_sem=ss.at[3], recv_sem=rr.at[3],
            device_id={"fluid": f, "wall": lax.rem(w + nw - 1, nw)}, device_id_type=MESH)
        return up, down, right, left

    def start_x(copies):
        pl.when(f < nf - 1)(copies[0].start)
        pl.when(f > 0)(copies[1].start)

    def start_z(copies):
        pl.when(w < nw - 1)(copies[2].start)
        pl.when(w > 0)(copies[3].start)

    def wait_halo(copies):
        pl.when(f > 0)(copies[0].wait_recv)
        pl.when(f < nf - 1)(copies[1].wait_recv)
        pl.when(w > 0)(copies[2].wait_recv)
        pl.when(w < nw - 1)(copies[3].wait_recv)

    def wait_halo_sent(copies):
        pl.when(f < nf - 1)(copies[0].wait_send)
        pl.when(f > 0)(copies[1].wait_send)
        pl.when(w < nw - 1)(copies[2].wait_send)
        pl.when(w > 0)(copies[3].wait_send)

    @pl.when(f == 0)
    def _():
        hxr[0] = jnp.zeros((4, CY, TW), BF16)
        fxr[0] = jnp.zeros((3, CY, TW), BF16)

    @pl.when(f == nf - 1)
    def _():
        hxr[1] = jnp.zeros((4, CY, TW), BF16)
        fxr[1] = jnp.zeros((3, CY, TW), BF16)

    @pl.when(w == 0)
    def _():
        zl[...] = jnp.zeros((4, 8, TW), F32)
        fl[...] = jnp.zeros((3, 8, TW), F32)

    @pl.when(w == nw - 1)
    def _():
        zh[...] = jnp.zeros((4, 8, TW), F32)
        fh[...] = jnp.zeros((3, 8, TW), F32)

    row16 = iota((MSG, TW), 0)
    lane16 = iota((MSG, TW), 1)
    slot16 = row16 // CAP
    comp16 = row16 % CAP

    def build_gather(i, _):
        ids = jnp.full((MSG, TW), -1, jnp.int32)
        for u in range(MSG):
            ids = jnp.where(row16 == u, cells[u % CAP, 4 * i + u // CAP], ids)
        at = pl.ds(pl.multiple_of(i * MSG, MSG), MSG)
        for q in range(CELLS // TW):
            gat[at, q * TW : (q + 1) * TW] = jnp.where(ids == lane16 + q * TW, 1.0, 0.0).astype(BF16)
        return 0

    def zero_pads(x, _):
        for c in range(4):
            vp[c, x + 1, 0:TOP, :] = jnp.zeros((TOP, TW), F32)
            vp[c, x + 1, END:ROWS, :] = jnp.zeros((ROWS - END, TW), F32)
        for c in range(3):
            fp[c, x + 1, 0:TOP, :] = jnp.zeros((TOP, TW), F32)
            fp[c, x + 1, END:ROWS, :] = jnp.zeros((ROWS - END, TW), F32)
        return 0

    lax.fori_loop(0, CX, zero_pads, 0)

    for c in range(4):
        flow_loads[c].wait()
        hxs[0, c] = vp[c, 1, TOP:END, :].astype(BF16)
        hxs[1, c] = vp[c, CX, TOP:END, :].astype(BF16)
        zo[c] = pack_edges(lambda x, k: vp[c, x + 1, TOP + 8 * k : TOP + 8 * k + 8, :], jnp.zeros((8, TW), F32))
    halo = halo_copies(
        hxs.at[0], hxr.at[0], hxs.at[1], hxr.at[1], zo, zl, zh, hs, hr)
    pl.semaphore_wait(barrier, expected)
    start_x(halo)
    start_z(halo)
    pass_rows(0)
    pass_walls(0)
    reg_load = pltpu.make_async_copy(regions, reg, load_sem.at[4])
    reg_load.start()
    obs_load = pltpu.make_async_copy(obs, wts, load_sem.at[5])
    obs_load.start()
    big[...] = jnp.zeros((nf * MSG, TW), F32)
    for load in table_loads:
        load.wait()
    lax.fori_loop(0, nf // 4, build_gather, 0)

    lane32 = iota((CY, TW), 1)
    first_lane = lane32 == 0
    last_lane = lane32 == TW - 1

    def forward_plane(x, carry, last):
        low_flux, low_p = carry[:3], carry[3]
        cur = [vp[c, x + 1, TOP:END, :] for c in range(4)]
        if last:
            flux_x = [jnp.zeros((CY, TW), F32) for _ in range(3)]
            high_p = jnp.zeros((CY, TW), F32)
        else:
            jump = [vp[c, x + 2, TOP:END, :] - cur[c] for c in range(3)]
            nu = viscosity(jump)
            nux[x + 1] = nu
            flux_x = [nu * j for j in jump]
            high_p = vp[3, x + 2, TOP:END, :]
        jump = [vp[c, x + 1, TOP:ROWS, :] - vp[c, x + 1, TOP - 1 : ROWS - 1, :] for c in range(3)]
        nu = viscosity(jump)
        nuy[x] = nu
        flux_y = [nu * j for j in jump]
        jump = [cur[c] - pltpu.roll(cur[c], 1, 1) for c in range(3)]
        nu = jnp.where(first_lane, 0.0, viscosity(jump))
        nuz[x] = nu
        nu_up = pltpu.roll(nu, TW - 1, 1)
        nuzu[x] = nu_up
        flux_z = [nu_up * (pltpu.roll(cur[c], TW - 1, 1) - cur[c]) - nu * jump[c] for c in range(3)]
        grad = [
            high_p - low_p,
            vp[3, x + 1, TOP + 1 : END + 1, :] - vp[3, x + 1, TOP - 1 : END - 1, :],
            jnp.where(last_lane, 0.0, pltpu.roll(cur[3], TW - 1, 1)) - jnp.where(first_lane, 0.0, pltpu.roll(cur[3], 1, 1)),
        ]
        for c in range(3):
            div = (flux_x[c] - low_flux[c]) + (flux_y[c][1 : CY + 1] - flux_y[c][0:CY])
            div = div + flux_z[c]
            vn[c, x] = cur[c] + time_step * (div - 0.5 * grad[c])
        return (*flux_x, cur[3])

    start = tuple(jnp.zeros((CY, TW), F32) for _ in range(4))
    carry = lax.fori_loop(0, 9, lambda x, carry: forward_plane(x, carry, False), start, unroll=3)
    wait_rows(0)
    pass_rows(1)
    carry = lax.fori_loop(9, CX - 1, lambda x, carry: forward_plane(x, carry, False), carry, unroll=3)
    forward_plane(CX - 1, carry, True)

    wait_walls(0)
    pass_walls(1)
    wait_halo(halo)
    for plane, side, face, sign in ((0, 0, 0, 1.0), (CX - 1, 1, CX, -1.0)):
        ghost = [hxr[side, c].astype(F32) for c in range(4)]
        jump = [ghost[c] - vp[c, plane + 1, TOP:END, :] for c in range(3)]
        nu = viscosity(jump)
        nux[face] = nu
        for c in range(3):
            add = nu * jump[c]
            if c == 0:
                add = add + (0.5 * sign) * ghost[3]
            vn[c, plane] = vn[c, plane] + time_step * add
    halo_p = packed_halo(zl[3], zh[3])
    jump = [packed_halo(zl[c], zh[c]) - zo[c] for c in range(3)]
    nu = viscosity(jump)
    nup[...] = nu
    even = iota((8, TW), 1) % 2 == 0
    fix = [time_step * nu * j for j in jump]
    fix[2] = fix[2] + jnp.where(even, 0.5 * time_step, -0.5 * time_step) * halo_p

    for x in range(CX):
        for c in range(3):
            value = vn[c, x] + unpack_edges(fix[c], x)
            vn[c, x] = value
            obsv[x * CY : (x + 1) * CY, c * TW : (c + 1) * TW] = value.astype(BF16)

    picked = jnp.dot(gat[...], obsv[...], preferred_element_type=F32)
    for c in range(3):
        big[pl.ds(c, nf * CAP, stride=CAP), :] = picked[:, c * TW : (c + 1) * TW]
    sb[...] = big[...].astype(BF16).reshape(nf, MSG, TW)

    def hops(d):
        chip, side = d // 2, 4
        return sum(min(at, side - at) for at in (chip % side, chip // side % side))

    far_first = sorted(range(1, nf), key=lambda d: -hops(d))

    def exchange(src, dst, ss, rr):
        def send():
            for d in far_first:
                peer = lax.rem(f + d, nf)
                pltpu.make_async_remote_copy(
                    src_ref=src.at[peer], dst_ref=dst.at[f], send_sem=ss, recv_sem=rr,
                    device_id={"fluid": peer, "wall": w}, device_id_type=MESH).start()

        every = pltpu.make_async_remote_copy(
            src_ref=src.at[0 : nf - 1], dst_ref=dst.at[0 : nf - 1], send_sem=ss, recv_sem=rr,
            device_id={"fluid": lax.rem(f + 1, nf), "wall": w}, device_id_type=MESH)
        return send, every.wait_recv, every.wait_send

    send1, receive1, sent1 = exchange(sb, rb, as1, ar1)
    send2, receive2, sent2 = exchange(sb2, rb2, as2, ar2)
    wait_rows(1)
    send1()
    wait_walls(1)
    pass_walls(2)
    rb[f] = sb[f]

    by_tile = [meas[c].astype(F32) for c in range(3)]
    dest_lane = jnp.full((MSG, TW), -1, jnp.int32)
    for t in range(tiles):
        dest_lane = jnp.where(lane16 == t, dest[t], dest_lane)
    for t in range(tiles):
        earlier = jnp.where((dest_lane == dest[t]) & (lane16 < t), 1.0, 0.0)
        rank = jnp.sum(earlier, axis=1, keepdims=True)
        at_row, at_lane = MSG * (t % 2), TW * (t % 2)
        blank = jnp.zeros((MSG, TW), F32)
        mask16[t // 2, at_row : at_row + MSG, at_lane : at_lane + TW] = jnp.where(
            (slot16.astype(F32) == rank) & (comp16 < 3), 1.0, 0.0)
        mask16[t // 2, at_row : at_row + MSG, TW - at_lane : 2 * TW - at_lane] = blank
        meas16[t // 2, at_row : at_row + MSG, TW - at_lane : 2 * TW - at_lane] = blank
        meas16[t // 2, at_row : at_row + MSG, at_lane : at_lane + TW] = jnp.where(
            comp16 == 0, by_tile[0][t : t + 1],
            jnp.where(comp16 == 1, by_tile[1][t : t + 1], jnp.where(comp16 == 2, by_tile[2][t : t + 1], 0.0)))
    route[...] = jnp.where(jnp.broadcast_to(dest_lane[0:1], (nf, TW)) == iota((nf, TW), 0), 1.0, 0.0).astype(BF16)
    cell_of = jnp.full((MSG, TW), -1, jnp.int32)
    for p in range(nf):
        for k in range(CAP):
            cell_of = jnp.where(lane16 == p * CAP + k, cells[k, p], cell_of)

    def build_scatter(i, _):
        at = pl.ds(pl.multiple_of(i * MSG, MSG), MSG)
        first = jnp.where(i < 2, i * MSG, jnp.where(i < 4, (i + 2 * CX - 4) * MSG, (i - 2) * MSG))
        gatt[at, :] = jnp.where(cell_of == row16 + first, 1.0, 0.0).astype(BF16)
        return 0

    lax.fori_loop(0, CELLS // MSG, build_scatter, 0, unroll=4)
    if nf * CAP < TW:
        rhs[...] = jnp.zeros((TW, 3 * TW), BF16)
    reg_load.wait()

    label_of_lane = iota((TW, TW), 1) // 8

    def by_fine_label(ids):
        fine = jnp.concatenate([(ids % REG_DEV).astype(F32)] * REG_DEV, axis=0)
        return jnp.where(fine.T == label_of_lane.astype(F32), 1.0, 0.0).astype(BF16)

    def build_regions(x, _):
        for k in range(4):
            ids = reg[x, 8 * k : 8 * k + 8, :]
            onelo[pl.ds(pl.multiple_of((4 * x + k) * TW, TW), TW), :] = by_fine_label(ids)

            def store_mask(pair, rows, k=k):
                maskhi[x, k, pair] = rows

            label_pairs(ids // REG_DEV, 8, store_mask)
        return 0

    lax.fori_loop(0, CX, build_regions, 0)
    packed_ids = pack_edges(lambda x, k: reg[x, 8 * k : 8 * k + 8, :], jnp.zeros((8, TW), jnp.int32))

    onez[...] = by_fine_label(packed_ids)

    def store_zmask(pair, rows):
        maskz[pair] = rows

    label_pairs(packed_ids // REG_DEV, 8, store_zmask)
    pick[...] = jnp.where(iota((TW, TW), 0) // 8 == iota((TW, TW), 1), 1.0, 0.0).astype(BF16)
    obs_load.wait()
    receive1()
    for p in range(tiles // 2):
        pair = wts[2 * p : 2 * p + 2].reshape(2 * TW, TW)
        predicted = contract_lanes(jnp.concatenate([rb[dest[2 * p]], rb[dest[2 * p + 1]]], axis=0), pair)
        mis[p] = ((predicted - meas16[p]) * mask16[p]).astype(BF16)
    for p in range(tiles // 2):
        pair = wts[2 * p : 2 * p + 2].reshape(2 * TW, TW)
        contrib[2 * p * MSG : 2 * (p + 1) * MSG, :] = jnp.dot(mis[p], pair, preferred_element_type=F32)
    used = [r for r in range(MSG) if r % CAP < 3]
    flat = jnp.concatenate([contrib[pl.ds(r, tiles, stride=MSG), :].astype(BF16) for r in used], axis=1)
    routed = jnp.dot(route[:, 0:tiles], flat, preferred_element_type=F32)
    for i, r in enumerate(used):
        big[pl.ds(r, nf, stride=MSG), :] = routed[:, i * TW : (i + 1) * TW]
    sb2[...] = big[...].astype(BF16).reshape(nf, MSG, TW)
    send2()
    wait_walls(2)
    rb2[f] = sb2[f]

    for c in range(3):
        vnp[c] = pack_edges(lambda x, k: vn[c, x, 8 * k : 8 * k + 8, :], jnp.zeros((8, TW), F32))
    receive2()
    big[...] = rb2[...].reshape(nf * MSG, TW).astype(F32)
    for c in range(3):
        rhs[0 : nf * CAP, c * TW : (c + 1) * TW] = big[pl.ds(c, nf * CAP, stride=CAP), :].astype(BF16)

    def force_rows(first, planes):
        rows = gatt[first * CY : (first + len(planes)) * CY, :]
        force = jnp.dot(rows, rhs[...], preferred_element_type=F32)
        for i, x in enumerate(planes):
            for c in range(3):
                fp[c, x + 1, TOP:END, :] = force[i * CY : (i + 1) * CY, c * TW : (c + 1) * TW]

    force_rows(0, (0, CX - 1))
    for c in range(3):
        fxs[0, c] = fp[c, 1, TOP:END, :].astype(BF16)
        fxs[1, c] = fp[c, CX, TOP:END, :].astype(BF16)
    halo2 = halo_copies(
        fxs.at[0], fxr.at[0], fxs.at[1], fxr.at[1], fo, fl, fh, hs2, hr2)
    start_x(halo2)
    force_rows(2, range(1, CX - 1))
    for c in range(3):
        fo[c] = pack_edges(lambda x, k: fp[c, x + 1, TOP + 8 * k : TOP + 8 * k + 8, :], jnp.zeros((8, TW), F32))
    start_z(halo2)

    def plane_sums(x, total):
        at = pl.ds(pl.multiple_of(x * 4 * TW, TW), 4 * TW)
        terms = region_terms([total[8 * k : 8 * k + 8] for k in range(4)], lambda k, h: maskhi[x, k, h])
        return jnp.dot(terms, onelo[at, :], preferred_element_type=F32)

    def adjoint_plane(x, carry, last):
        flux_x = []
        total = None
        for c in range(3):
            cur = fp[c, x + 1, TOP:END, :]
            if last:
                flux = jnp.zeros((CY, TW), F32)
            else:
                flux = nux[x + 1] * (fp[c, x + 2, TOP:END, :] - cur)
            flux_x.append(flux)
            div = flux - carry[c]
            div = div + nuy[x, 1 : CY + 1, :] * (fp[c, x + 1, TOP + 1 : END + 1, :] - cur)
            div = div - nuy[x, 0:CY, :] * (cur - fp[c, x + 1, TOP - 1 : END - 1, :])
            div = div + nuzu[x] * (pltpu.roll(cur, TW - 1, 1) - cur)
            div = div - nuz[x] * (cur - pltpu.roll(cur, 1, 1))
            value = cur + time_step * div
            adj[c, x] = value
            part = value * vn[c, x]
            total = part if total is None else total + part
        at = pl.ds(pl.multiple_of(x * 4 * TW, 4 * TW), 4 * TW)
        lhs[:, at] = region_terms([total[8 * k : 8 * k + 8] for k in range(4)], lambda k, h: maskhi[x, k, h])
        return tuple(flux_x)

    carry = lax.fori_loop(0, CX - 1, lambda x, carry: adjoint_plane(x, carry, False), start[:3], unroll=3)
    adjoint_plane(CX - 1, carry, True)
    inner[...] = jnp.dot(lhs[...], onelo[...], preferred_element_type=F32)

    wait_halo(halo2)
    fix2 = [time_step * nup[...] * (packed_halo(fl[c], fh[c]) - fo[c]) for c in range(3)]
    total = fix2[0] * vnp[0] + fix2[1] * vnp[1] + fix2[2] * vnp[2]
    terms = region_terms([total], lambda k, h: maskz[h])
    sums = inner[...] + jnp.dot(terms, onez[...], preferred_element_type=F32)
    for plane, side, face in ((0, 0, 0), (CX - 1, 1, CX)):
        total = None
        for c in range(3):
            jump = fxr[side, c].astype(F32) - fp[c, plane + 1, TOP:END, :]
            value = time_step * (nux[face] * jump)
            adj[c, plane] = adj[c, plane] + value
            part = value * vn[c, plane]
            total = part if total is None else total + part
        sums = sums + plane_sums(plane, total)

    sums = jnp.where(iota((TW // 2, TW), 0) % 8 == iota((TW // 2, TW), 1) % 8, sums, 0.0)
    coarse_rows = [jnp.sum(sums[8 * h : 8 * h + 8], axis=0, keepdims=True) for h in range(8)]
    by_label = jnp.concatenate(coarse_rows, axis=0)
    parts = []
    for _ in range(3):
        part = by_label.astype(BF16)
        parts.append(part)
        by_label = by_label - part.astype(F32)
    owned = jnp.dot(jnp.concatenate(parts, axis=0), pick[...], preferred_element_type=F32)
    owned = owned[0:8] + owned[8:16] + owned[16:24]
    for p in range(nw):
        ps[p] = owned

    def wall_copy(peer, src, dst):
        return pltpu.make_async_remote_copy(
            src_ref=src, dst_ref=dst, send_sem=ws, recv_sem=wr,
            device_id={"fluid": f, "wall": peer}, device_id_type=MESH)

    every_wall = wall_copy(lax.rem(w + 1, nw), ps.at[0 : nw - 1], pr.at[0 : nw - 1])
    for d in sorted(range(1, nw), key=lambda d: -min(d, nw - d)):
        peer = lax.rem(w + d, nw)
        wall_copy(peer, ps.at[peer], pr.at[w]).start()
    pr[w] = owned
    for x in range(CX):
        for c in range(3):
            adj[c, x] = adj[c, x] + unpack_edges(fix2[c], x)
    wait_halo_sent(halo)
    wait_halo_sent(halo2)
    sent1()
    sent2()
    every_wall.wait_recv()
    total = pr[0]
    for p in range(1, nw):
        total = total + pr[p]
    mine = jnp.sum(jnp.where(iota((8, TW), 0) == w, total, 0.0), axis=0, keepdims=True)
    sens_out[...] = sens_scale * mine[:, 0:REG_DEV]
    every_wall.wait_send()


def write_out(vn, adj, sens, vn_out, adj_out, sens_out, sems):
    copies = [pltpu.make_async_copy(sens, sens_out, sems.at[0])]
    for c in range(3):
        copies.append(pltpu.make_async_copy(vn.at[c], vn_out.at[c], sems.at[1 + c]))
        copies.append(pltpu.make_async_copy(adj.at[c], adj_out.at[c], sems.at[4 + c]))
    for copy in copies:
        copy.start()
    for copy in copies:
        copy.wait()


def solution(mesh):
    nf, nw = mesh.shape["fluid"], mesh.shape["wall"]

    def body(flow_state, regions, obs_tiles, measured, tile_dest, cell_list):
        tiles = obs_tiles.shape[2]
        in_hbm = pl.BlockSpec(memory_space=pltpu.HBM)
        in_vmem = pl.BlockSpec(memory_space=pltpu.VMEM)
        dma = pltpu.SemaphoreType.DMA
        vn, adj, sens = pl.pallas_call(
            functools.partial(kernel, nf, nw, tiles),
            out_shape=(
                pltpu.VMEM((3, CX, CY, TW), F32),
                pltpu.VMEM((3, CX, CY, TW), F32),
                pltpu.VMEM((1, REG_DEV), F32),
            ),
            in_specs=[in_hbm] * 6,
            out_specs=(in_vmem, in_vmem, in_vmem),
            scratch_shapes=[
                pltpu.VMEM((4, CX + 2, ROWS, TW), F32),
                pltpu.VMEM((3, CX + 2, ROWS, TW), F32),
                pltpu.VMEM((2, 4, CY, TW), BF16),
                pltpu.VMEM((2, 4, CY, TW), BF16),
                pltpu.VMEM((2, 3, CY, TW), BF16),
                pltpu.VMEM((2, 3, CY, TW), BF16),
                pltpu.VMEM((CX + 1, CY, TW), F32),
                pltpu.VMEM((CX, ROWS - TOP, TW), F32),
                pltpu.VMEM((CX, CY, TW), F32),
                pltpu.VMEM((CX, CY, TW), F32),
                pltpu.VMEM((8, TW), F32),
                pltpu.VMEM((3, 8, TW), F32),
                pltpu.VMEM((4, 8, TW), F32),
                pltpu.VMEM((4, 8, TW), F32),
                pltpu.VMEM((4, 8, TW), F32),
                pltpu.VMEM((3, 8, TW), F32),
                pltpu.VMEM((3, 8, TW), F32),
                pltpu.VMEM((3, 8, TW), F32),
                pltpu.VMEM((tiles, TW, TW), BF16),
                pltpu.VMEM((CX, CY, TW), jnp.int32),
                pltpu.VMEM((tiles // 2, 2 * MSG, 2 * TW), F32),
                pltpu.VMEM((tiles // 2, 2 * MSG, 2 * TW), F32),
                pltpu.VMEM((nf * CAP, CELLS), BF16),
                pltpu.VMEM((CELLS, TW), BF16),
                pltpu.VMEM((nf, TW), BF16),
                pltpu.VMEM((CELLS, 3 * TW), BF16),
                pltpu.VMEM((nf * MSG, TW), F32),
                pltpu.VMEM((nf, MSG, TW), BF16),
                pltpu.VMEM((nf, MSG, TW), BF16),
                pltpu.VMEM((tiles // 2, 2 * MSG, 2 * TW), BF16),
                pltpu.VMEM((tiles * MSG, TW), F32),
                pltpu.VMEM((nf, MSG, TW), BF16),
                pltpu.VMEM((nf, MSG, TW), BF16),
                pltpu.VMEM((TW, 3 * TW), BF16),
                pltpu.VMEM((CX * 4 * TW, TW), BF16),
                pltpu.VMEM((CX, 4, 4, MSG, TW), BF16),
                pltpu.VMEM((TW, TW), BF16),
                pltpu.VMEM((4, MSG, TW), BF16),
                pltpu.VMEM((TW, TW), BF16),
                pltpu.VMEM((TW // 2, CX * 4 * TW), BF16),
                pltpu.VMEM((TW // 2, TW), F32),
                pltpu.VMEM((nw, 8, TW), F32),
                pltpu.VMEM((nw, 8, TW), F32),
                pltpu.VMEM((3, tiles, TW), BF16),
                pltpu.SMEM((tiles,), jnp.int32),
                pltpu.SMEM((CAP, nf), jnp.int32),
                pltpu.SemaphoreType.REGULAR((2,)),
                pltpu.SemaphoreType.REGULAR((3,)),
                dma((9,)),
                dma((4,)),
                dma((4,)),
                dma((4,)),
                dma((4,)),
                dma(()),
                dma(()),
                dma(()),
                dma(()),
                dma(()),
                dma(()),
            ],
            compiler_params=pltpu.CompilerParams(collective_id=0, has_side_effects=True, vmem_limit_bytes=60 * 1024 * 1024),
        )(
            flow_state, regions, obs_tiles[0, 0], measured[0, 0].transpose(1, 0, 2), tile_dest[0, 0],
            cell_list[0, 0].T,
        )
        vn, adj, sens = pl.pallas_call(
            write_out,
            out_shape=tuple(jax.ShapeDtypeStruct(a.shape, a.dtype) for a in (vn, adj, sens)),
            in_specs=[in_vmem, in_vmem, in_vmem],
            out_specs=(in_hbm, in_hbm, in_hbm),
            scratch_shapes=[dma((7,))],
            compiler_params=pltpu.CompilerParams(vmem_limit_bytes=8 << 20),
        )(vn, adj, sens)
        return vn, adj, sens.reshape(REG_DEV)

    in_specs = (
        P(None, "fluid", None, "wall"),
        P("fluid", None, "wall"),
        P("fluid", "wall", None, None, None),
        P("fluid", "wall", None, None, None),
        P("fluid", "wall", None),
        P("fluid", "wall", None, None),
    )
    out_specs = (
        P(None, "fluid", None, "wall"),
        P(None, "fluid", None, "wall"),
        P(("fluid", "wall")),
    )
    return jax.shard_map(body, mesh=mesh, in_specs=in_specs, out_specs=out_specs, check_vma=False)
```

```python
import functools

import jax
import jax.numpy as jnp
from jax import lax
from jax.experimental import pallas as pl
from jax.experimental.pallas import tpu as pltpu
from jax.sharding import PartitionSpec as P

CX, CY, TW = 16, 32, 128
CAP = 4
REG_DEV = 16
CELLS = CX * CY
TOP = 8
END = TOP + CY
ROWS = END + 8
MSG = 16
ROW = 8

time_step = 0.12
nu_floor = 0.1
nu_spread = 0.9
relax_sq = 4.0
sens_scale = 0.03

MESH = pl.DeviceIdType.MESH
F32 = jnp.float32
BF16 = jnp.bfloat16


def iota(shape, dim):
    return lax.broadcasted_iota(jnp.int32, shape, dim)


def viscosity(jumps):
    base = 1.0 + relax_sq * (jumps[0] * jumps[0] + jumps[1] * jumps[1] + jumps[2] * jumps[2])
    root = lax.rsqrt(base)
    return nu_floor + nu_spread * (root * lax.rsqrt(root))


def pack_edges(rows_of, zero):
    half = ((iota((8, TW), 1) + 1) % TW) // 2
    total = None
    for k in range(4):
        packed = zero
        for x in range(CX):
            slot = 4 * x + k
            rows = rows_of(x, k)
            if slot:
                rows = pltpu.roll(rows, 2 * slot, 1)
            packed = jnp.where(half == slot, rows, packed)
        total = packed if total is None else total + packed
    return total


def packed_halo(low, high):
    even = iota((8, TW), 1) % 2 == 0
    return jnp.where(even, pltpu.roll(low, 1, 1), pltpu.roll(high, TW - 1, 1))


def unpack_edges(packed, x):
    rolled = [pltpu.roll(packed, TW - 2 * (4 * x + k), 1) if x + k else packed for k in range(4)]
    lane = iota((CY, TW), 1)
    return jnp.where((lane == 0) | (lane == TW - 1), jnp.concatenate(rolled, axis=0), 0.0)


def region_terms(values, masks):
    twice = [jnp.concatenate([value, value], axis=0).astype(BF16) for value in values]
    rows = [jnp.concatenate([masks(k, pair) * v for k, v in enumerate(twice)], axis=1) for pair in range(4)]
    return jnp.concatenate(rows, axis=0)


def label_pairs(labels, count, store):
    for pair in range(count // 2):
        both = [jnp.where(labels == 2 * pair + i, 1.0, 0.0) for i in range(2)]
        store(pair, jnp.concatenate(both, axis=0).astype(BF16))


def contract_lanes(a, b):
    return lax.dot_general(a, b, (((1,), (1,)), ((), ())), preferred_element_type=F32)


def kernel(
    nf, nw, tiles,
    flow, regions, obs, meas_in, dest_in, cells_in,
    vn, adj, sens_out,
    vp, fp, hxs, hxr, fxs, fxr, nux, nuy, nuz, nuzu, nup, vnp, zo, zl, zh, fo, fl, fh,
    wts, reg, meas16, mask16, gat, gatt, route, obsv, big, sb, rb, mis, contrib, sb2, rb2, rhs,
    onelo, maskhi, onez, maskz, pick, lhs, inner, ps, pr, meas, dest, cells,
    row_sem, wall_sem, load_sem, hs, hr, hs2, hr2, as1, ar1, as2, ar2, ws, wr,
):
    f = lax.axis_index("fluid")
    w = lax.axis_index("wall")
    flow_loads = [
        pltpu.make_async_copy(flow.at[c], vp.at[c, 1 : CX + 1, TOP:END, :], load_sem.at[c]) for c in range(4)
    ]
    for load in flow_loads:
        load.start()
    table_loads = [
        pltpu.make_async_copy(cells_in, cells, load_sem.at[6]),
        pltpu.make_async_copy(dest_in, dest, load_sem.at[7]),
        pltpu.make_async_copy(meas_in, meas, load_sem.at[8]),
    ]
    for load in table_loads:
        load.start()

    def signal(sem, to_f, to_w):
        pl.semaphore_signal(
            sem, inc=1, device_id={"fluid": lax.rem(to_f + nf, nf), "wall": lax.rem(to_w + nw, nw)}, device_id_type=MESH)

    barrier = pltpu.get_barrier_semaphore()
    many_rows = nf > ROW
    in_row = lax.rem(f, ROW)
    flip = 1 - 2 * lax.rem(f, 2)

    def away(dx, dy):
        return lax.rem((f // ROW + dy) * ROW + nf, nf) + lax.rem(in_row + 2 * dx + ROW, ROW)

    beside = [away(1, 0), away(-1, 0)]
    beyond = [away(2, 0)]
    if many_rows:
        beside += [away(0, 1), away(0, -1)]
        beyond += [away(0, 2), away(1, 1), away(1, -1), away(-1, 1), away(-1, -1)]
    near = [(f, w + 1), (f, w - 1), (f + flip, w)]
    near += [(at, w) for at in beside] + [(at + flip, w) for at in beside]
    pl.when(f < nf - 1)(lambda: signal(barrier, f + 1, w))
    pl.when(f > 0)(lambda: signal(barrier, f - 1, w))
    for to_f, to_w in near:
        signal(barrier, to_f, to_w)
    expected = len(near) + (f + nf - 1) // nf + (2 * nf - 2 - f) // nf
    rounds = (beside, beyond)

    def pass_rows(stage):
        for at in rounds[stage]:
            signal(row_sem.at[stage], at, w)

    def wait_rows(stage):
        pl.semaphore_wait(row_sem.at[stage], len(rounds[stage]))

    def pass_walls(stage):
        signal(wall_sem.at[stage], f, w + 1)
        signal(wall_sem.at[stage], f, w - 1)

    def wait_walls(stage):
        pl.semaphore_wait(wall_sem.at[stage], 2)

    def halo_copies(low_src, low_dst, high_src, high_dst, packed, from_low, from_high, ss, rr):
        up = pltpu.make_async_remote_copy(
            src_ref=high_src, dst_ref=low_dst, send_sem=ss.at[0], recv_sem=rr.at[0],
            device_id={"fluid": lax.rem(f + 1, nf), "wall": w}, device_id_type=MESH)
        down = pltpu.make_async_remote_copy(
            src_ref=low_src, dst_ref=high_dst, send_sem=ss.at[1], recv_sem=rr.at[1],
            device_id={"fluid": lax.rem(f + nf - 1, nf), "wall": w}, device_id_type=MESH)
        right = pltpu.make_async_remote_copy(
            src_ref=packed, dst_ref=from_low, send_sem=ss.at[2], recv_sem=rr.at[2],
            device_id={"fluid": f, "wall": lax.rem(w + 1, nw)}, device_id_type=MESH)
        left = pltpu.make_async_remote_copy(
            src_ref=packed, dst_ref=from_high, send_sem=ss.at[3], recv_sem=rr.at[3],
            device_id={"fluid": f, "wall": lax.rem(w + nw - 1, nw)}, device_id_type=MESH)
        return up, down, right, left

    def start_x(copies):
        pl.when(f < nf - 1)(copies[0].start)
        pl.when(f > 0)(copies[1].start)

    def start_z(copies):
        pl.when(w < nw - 1)(copies[2].start)
        pl.when(w > 0)(copies[3].start)

    def wait_halo(copies):
        pl.when(f > 0)(copies[0].wait_recv)
        pl.when(f < nf - 1)(copies[1].wait_recv)
        pl.when(w > 0)(copies[2].wait_recv)
        pl.when(w < nw - 1)(copies[3].wait_recv)

    def wait_halo_sent(copies):
        pl.when(f < nf - 1)(copies[0].wait_send)
        pl.when(f > 0)(copies[1].wait_send)
        pl.when(w < nw - 1)(copies[2].wait_send)
        pl.when(w > 0)(copies[3].wait_send)

    @pl.when(f == 0)
    def _():
        hxr[0] = jnp.zeros((4, CY, TW), BF16)
        fxr[0] = jnp.zeros((3, CY, TW), BF16)

    @pl.when(f == nf - 1)
    def _():
        hxr[1] = jnp.zeros((4, CY, TW), BF16)
        fxr[1] = jnp.zeros((3, CY, TW), BF16)

    @pl.when(w == 0)
    def _():
        zl[...] = jnp.zeros((4, 8, TW), F32)
        fl[...] = jnp.zeros((3, 8, TW), F32)

    @pl.when(w == nw - 1)
    def _():
        zh[...] = jnp.zeros((4, 8, TW), F32)
        fh[...] = jnp.zeros((3, 8, TW), F32)

    row16 = iota((MSG, TW), 0)
    lane16 = iota((MSG, TW), 1)
    slot16 = row16 // CAP
    comp16 = row16 % CAP

    def build_gather(i, _):
        ids = jnp.full((MSG, TW), -1, jnp.int32)
        for u in range(MSG):
            ids = jnp.where(row16 == u, cells[u % CAP, 4 * i + u // CAP], ids)
        at = pl.ds(pl.multiple_of(i * MSG, MSG), MSG)
        for q in range(CELLS // TW):
            gat[at, q * TW : (q + 1) * TW] = jnp.where(ids == lane16 + q * TW, 1.0, 0.0).astype(BF16)
        return 0

    def zero_pads(x, _):
        for c in range(4):
            vp[c, x + 1, 0:TOP, :] = jnp.zeros((TOP, TW), F32)
            vp[c, x + 1, END:ROWS, :] = jnp.zeros((ROWS - END, TW), F32)
        for c in range(3):
            fp[c, x + 1, 0:TOP, :] = jnp.zeros((TOP, TW), F32)
            fp[c, x + 1, END:ROWS, :] = jnp.zeros((ROWS - END, TW), F32)
        return 0

    lax.fori_loop(0, CX, zero_pads, 0)

    for c in range(4):
        flow_loads[c].wait()
        hxs[0, c] = vp[c, 1, TOP:END, :].astype(BF16)
        hxs[1, c] = vp[c, CX, TOP:END, :].astype(BF16)
        zo[c] = pack_edges(lambda x, k: vp[c, x + 1, TOP + 8 * k : TOP + 8 * k + 8, :], jnp.zeros((8, TW), F32))
    halo = halo_copies(
        hxs.at[0], hxr.at[0], hxs.at[1], hxr.at[1], zo, zl, zh, hs, hr)
    pl.semaphore_wait(barrier, expected)
    start_x(halo)
    start_z(halo)
    pass_rows(0)
    pass_walls(0)
    reg_load = pltpu.make_async_copy(regions, reg, load_sem.at[4])
    reg_load.start()
    obs_load = pltpu.make_async_copy(obs, wts, load_sem.at[5])
    obs_load.start()
    big[...] = jnp.zeros((nf * MSG, TW), F32)
    for load in table_loads:
        load.wait()
    lax.fori_loop(0, nf // 4, build_gather, 0)

    lane32 = iota((CY, TW), 1)
    first_lane = lane32 == 0
    last_lane = lane32 == TW - 1

    def forward_plane(x, carry, last):
        low_flux, low_p = carry[:3], carry[3]
        cur = [vp[c, x + 1, TOP:END, :] for c in range(4)]
        if last:
            flux_x = [jnp.zeros((CY, TW), F32) for _ in range(3)]
            high_p = jnp.zeros((CY, TW), F32)
        else:
            jump = [vp[c, x + 2, TOP:END, :] - cur[c] for c in range(3)]
            nu = viscosity(jump)
            nux[x + 1] = nu
            flux_x = [nu * j for j in jump]
            high_p = vp[3, x + 2, TOP:END, :]
        jump = [vp[c, x + 1, TOP:ROWS, :] - vp[c, x + 1, TOP - 1 : ROWS - 1, :] for c in range(3)]
        nu = viscosity(jump)
        nuy[x] = nu
        flux_y = [nu * j for j in jump]
        jump = [cur[c] - pltpu.roll(cur[c], 1, 1) for c in range(3)]
        nu = jnp.where(first_lane, 0.0, viscosity(jump))
        nuz[x] = nu
        nu_up = pltpu.roll(nu, TW - 1, 1)
        nuzu[x] = nu_up
        flux_z = [nu_up * (pltpu.roll(cur[c], TW - 1, 1) - cur[c]) - nu * jump[c] for c in range(3)]
        grad = [
            high_p - low_p,
            vp[3, x + 1, TOP + 1 : END + 1, :] - vp[3, x + 1, TOP - 1 : END - 1, :],
            jnp.where(last_lane, 0.0, pltpu.roll(cur[3], TW - 1, 1)) - jnp.where(first_lane, 0.0, pltpu.roll(cur[3], 1, 1)),
        ]
        for c in range(3):
            div = (flux_x[c] - low_flux[c]) + (flux_y[c][1 : CY + 1] - flux_y[c][0:CY])
            div = div + flux_z[c]
            vn[c, x] = cur[c] + time_step * (div - 0.5 * grad[c])
        return (*flux_x, cur[3])

    start = tuple(jnp.zeros((CY, TW), F32) for _ in range(4))
    carry = lax.fori_loop(0, 9, lambda x, carry: forward_plane(x, carry, False), start, unroll=3)
    wait_rows(0)
    pass_rows(1)
    carry = lax.fori_loop(9, CX - 1, lambda x, carry: forward_plane(x, carry, False), carry, unroll=3)
    forward_plane(CX - 1, carry, True)

    wait_walls(0)
    pass_walls(1)
    wait_halo(halo)
    for plane, side, face, sign in ((0, 0, 0, 1.0), (CX - 1, 1, CX, -1.0)):
        ghost = [hxr[side, c].astype(F32) for c in range(4)]
        jump = [ghost[c] - vp[c, plane + 1, TOP:END, :] for c in range(3)]
        nu = viscosity(jump)
        nux[face] = nu
        for c in range(3):
            add = nu * jump[c]
            if c == 0:
                add = add + (0.5 * sign) * ghost[3]
            vn[c, plane] = vn[c, plane] + time_step * add
    halo_p = packed_halo(zl[3], zh[3])
    jump = [packed_halo(zl[c], zh[c]) - zo[c] for c in range(3)]
    nu = viscosity(jump)
    nup[...] = nu
    even = iota((8, TW), 1) % 2 == 0
    fix = [time_step * nu * j for j in jump]
    fix[2] = fix[2] + jnp.where(even, 0.5 * time_step, -0.5 * time_step) * halo_p

    for x in range(CX):
        for c in range(3):
            value = vn[c, x] + unpack_edges(fix[c], x)
            vn[c, x] = value
            obsv[x * CY : (x + 1) * CY, c * TW : (c + 1) * TW] = value.astype(BF16)

    picked = jnp.dot(gat[...], obsv[...], preferred_element_type=F32)
    for c in range(3):
        big[pl.ds(c, nf * CAP, stride=CAP), :] = picked[:, c * TW : (c + 1) * TW]
    sb[...] = big[...].astype(BF16).reshape(nf, MSG, TW)

    def hops(d):
        chip, side = d // 2, 4
        return sum(min(at, side - at) for at in (chip % side, chip // side % side))

    far_first = sorted(range(1, nf), key=lambda d: -hops(d))

    def exchange(src, dst, ss, rr):
        def send():
            for d in far_first:
                peer = lax.rem(f + d, nf)
                pltpu.make_async_remote_copy(
                    src_ref=src.at[peer], dst_ref=dst.at[f], send_sem=ss, recv_sem=rr,
                    device_id={"fluid": peer, "wall": w}, device_id_type=MESH).start()

        every = pltpu.make_async_remote_copy(
            src_ref=src.at[0 : nf - 1], dst_ref=dst.at[0 : nf - 1], send_sem=ss, recv_sem=rr,
            device_id={"fluid": lax.rem(f + 1, nf), "wall": w}, device_id_type=MESH)
        return send, every.wait_recv, every.wait_send

    send1, receive1, sent1 = exchange(sb, rb, as1, ar1)
    send2, receive2, sent2 = exchange(sb2, rb2, as2, ar2)
    wait_rows(1)
    send1()
    wait_walls(1)
    pass_walls(2)
    rb[f] = sb[f]

    by_tile = [meas[c].astype(F32) for c in range(3)]
    dest_lane = jnp.full((MSG, TW), -1, jnp.int32)
    for t in range(tiles):
        dest_lane = jnp.where(lane16 == t, dest[t], dest_lane)
    for t in range(tiles):
        earlier = jnp.where((dest_lane == dest[t]) & (lane16 < t), 1.0, 0.0)
        rank = jnp.sum(earlier, axis=1, keepdims=True)
        at_row, at_lane = MSG * (t % 2), TW * (t % 2)
        blank = jnp.zeros((MSG, TW), F32)
        mask16[t // 2, at_row : at_row + MSG, at_lane : at_lane + TW] = jnp.where(
            (slot16.astype(F32) == rank) & (comp16 < 3), 1.0, 0.0)
        mask16[t // 2, at_row : at_row + MSG, TW - at_lane : 2 * TW - at_lane] = blank
        meas16[t // 2, at_row : at_row + MSG, TW - at_lane : 2 * TW - at_lane] = blank
        meas16[t // 2, at_row : at_row + MSG, at_lane : at_lane + TW] = jnp.where(
            comp16 == 0, by_tile[0][t : t + 1],
            jnp.where(comp16 == 1, by_tile[1][t : t + 1], jnp.where(comp16 == 2, by_tile[2][t : t + 1], 0.0)))
    route[...] = jnp.where(jnp.broadcast_to(dest_lane[0:1], (nf, TW)) == iota((nf, TW), 0), 1.0, 0.0).astype(BF16)
    cell_of = jnp.full((MSG, TW), -1, jnp.int32)
    for p in range(nf):
        for k in range(CAP):
            cell_of = jnp.where(lane16 == p * CAP + k, cells[k, p], cell_of)

    def build_scatter(i, _):
        at = pl.ds(pl.multiple_of(i * MSG, MSG), MSG)
        first = jnp.where(i < 2, i * MSG, jnp.where(i < 4, (i + 2 * CX - 4) * MSG, (i - 2) * MSG))
        gatt[at, :] = jnp.where(cell_of == row16 + first, 1.0, 0.0).astype(BF16)
        return 0

    lax.fori_loop(0, CELLS // MSG, build_scatter, 0, unroll=4)
    if nf * CAP < TW:
        rhs[...] = jnp.zeros((TW, 3 * TW), BF16)
    reg_load.wait()

    label_of_lane = iota((TW, TW), 1) // 8

    def by_fine_label(ids):
        fine = jnp.concatenate([(ids % REG_DEV).astype(F32)] * REG_DEV, axis=0)
        return jnp.where(fine.T == label_of_lane.astype(F32), 1.0, 0.0).astype(BF16)

    def build_regions(x, _):
        for k in range(4):
            ids = reg[x, 8 * k : 8 * k + 8, :]
            onelo[pl.ds(pl.multiple_of((4 * x + k) * TW, TW), TW), :] = by_fine_label(ids)

            def store_mask(pair, rows, k=k):
                maskhi[x, k, pair] = rows

            label_pairs(ids // REG_DEV, 8, store_mask)
        return 0

    lax.fori_loop(0, CX, build_regions, 0)
    packed_ids = pack_edges(lambda x, k: reg[x, 8 * k : 8 * k + 8, :], jnp.zeros((8, TW), jnp.int32))

    onez[0:TW, :] = by_fine_label(packed_ids)

    def store_zmask(pair, rows):
        maskz[pair] = rows

    label_pairs(packed_ids // REG_DEV, 8, store_zmask)
    pick[...] = jnp.where(iota((TW, TW), 0) // 8 == iota((TW, TW), 1), 1.0, 0.0).astype(BF16)
    obs_load.wait()
    receive1()
    for p in range(tiles // 2):
        pair = wts[2 * p : 2 * p + 2].reshape(2 * TW, TW)
        predicted = contract_lanes(jnp.concatenate([rb[dest[2 * p]], rb[dest[2 * p + 1]]], axis=0), pair)
        mis[p] = ((predicted - meas16[p]) * mask16[p]).astype(BF16)
    for p in range(tiles // 2):
        pair = wts[2 * p : 2 * p + 2].reshape(2 * TW, TW)
        contrib[2 * p * MSG : 2 * (p + 1) * MSG, :] = jnp.dot(mis[p], pair, preferred_element_type=F32)
    used = [r for r in range(MSG) if r % CAP < 3]
    flat = jnp.concatenate([contrib[pl.ds(r, tiles, stride=MSG), :].astype(BF16) for r in used], axis=1)
    routed = jnp.dot(route[:, 0:tiles], flat, preferred_element_type=F32)
    for i, r in enumerate(used):
        big[pl.ds(r, nf, stride=MSG), :] = routed[:, i * TW : (i + 1) * TW]
    sb2[...] = big[...].astype(BF16).reshape(nf, MSG, TW)
    send2()
    wait_walls(2)
    rb2[f] = sb2[f]

    onez[TW : 5 * TW, :] = onelo[0 : 4 * TW, :]
    onez[5 * TW : 9 * TW, :] = onelo[(CX - 1) * 4 * TW : CX * 4 * TW, :]
    for c in range(3):
        vnp[c] = pack_edges(lambda x, k: vn[c, x, 8 * k : 8 * k + 8, :], jnp.zeros((8, TW), F32))
    receive2()
    big[...] = rb2[...].reshape(nf * MSG, TW).astype(F32)
    for c in range(3):
        rhs[0 : nf * CAP, c * TW : (c + 1) * TW] = big[pl.ds(c, nf * CAP, stride=CAP), :].astype(BF16)

    def force_rows(first, planes):
        rows = gatt[first * CY : (first + len(planes)) * CY, :]
        force = jnp.dot(rows, rhs[...], preferred_element_type=F32)
        for i, x in enumerate(planes):
            for c in range(3):
                fp[c, x + 1, TOP:END, :] = force[i * CY : (i + 1) * CY, c * TW : (c + 1) * TW]

    force_rows(0, (0, CX - 1))
    for c in range(3):
        fxs[0, c] = fp[c, 1, TOP:END, :].astype(BF16)
        fxs[1, c] = fp[c, CX, TOP:END, :].astype(BF16)
    halo2 = halo_copies(
        fxs.at[0], fxr.at[0], fxs.at[1], fxr.at[1], fo, fl, fh, hs2, hr2)
    start_x(halo2)
    force_rows(2, range(1, CX - 1))
    for c in range(3):
        fo[c] = pack_edges(lambda x, k: fp[c, x + 1, TOP + 8 * k : TOP + 8 * k + 8, :], jnp.zeros((8, TW), F32))
    start_z(halo2)

    def adjoint_plane(x, carry, last):
        flux_x = []
        total = None
        for c in range(3):
            cur = fp[c, x + 1, TOP:END, :]
            if last:
                flux = jnp.zeros((CY, TW), F32)
            else:
                flux = nux[x + 1] * (fp[c, x + 2, TOP:END, :] - cur)
            flux_x.append(flux)
            div = flux - carry[c]
            div = div + nuy[x, 1 : CY + 1, :] * (fp[c, x + 1, TOP + 1 : END + 1, :] - cur)
            div = div - nuy[x, 0:CY, :] * (cur - fp[c, x + 1, TOP - 1 : END - 1, :])
            div = div + nuzu[x] * (pltpu.roll(cur, TW - 1, 1) - cur)
            div = div - nuz[x] * (cur - pltpu.roll(cur, 1, 1))
            value = cur + time_step * div
            adj[c, x] = value
            part = value * vn[c, x]
            total = part if total is None else total + part
        at = pl.ds(pl.multiple_of(x * 4 * TW, 4 * TW), 4 * TW)
        lhs[:, at] = region_terms([total[8 * k : 8 * k + 8] for k in range(4)], lambda k, h: maskhi[x, k, h])
        return tuple(flux_x)

    carry = lax.fori_loop(0, CX - 1, lambda x, carry: adjoint_plane(x, carry, False), start[:3], unroll=3)
    adjoint_plane(CX - 1, carry, True)
    inner[...] = jnp.dot(lhs[...], onelo[...], preferred_element_type=F32)

    wait_halo(halo2)
    fix2 = [time_step * nup[...] * (packed_halo(fl[c], fh[c]) - fo[c]) for c in range(3)]
    total = fix2[0] * vnp[0] + fix2[1] * vnp[1] + fix2[2] * vnp[2]
    edge_terms = [region_terms([total], lambda k, h: maskz[h])]
    for plane, side, face in ((0, 0, 0), (CX - 1, 1, CX)):
        total = None
        for c in range(3):
            jump = fxr[side, c].astype(F32) - fp[c, plane + 1, TOP:END, :]
            value = time_step * (nux[face] * jump)
            adj[c, plane] = adj[c, plane] + value
            part = value * vn[c, plane]
            total = part if total is None else total + part
        edge_terms.append(
            region_terms([total[8 * k : 8 * k + 8] for k in range(4)], lambda k, h, x=plane: maskhi[x, k, h]))
    sums = inner[...] + jnp.dot(
        jnp.concatenate(edge_terms, axis=1), onez[...], preferred_element_type=F32)

    sums = jnp.where(iota((TW // 2, TW), 0) % 8 == iota((TW // 2, TW), 1) % 8, sums, 0.0)
    coarse_rows = [jnp.sum(sums[8 * h : 8 * h + 8], axis=0, keepdims=True) for h in range(8)]
    by_label = jnp.concatenate(coarse_rows, axis=0)
    parts = []
    for _ in range(3):
        part = by_label.astype(BF16)
        parts.append(part)
        by_label = by_label - part.astype(F32)
    owned = jnp.dot(jnp.concatenate(parts, axis=0), pick[...], preferred_element_type=F32)
    owned = owned[0:8] + owned[8:16] + owned[16:24]
    for p in range(nw):
        ps[p] = owned

    def wall_copy(peer, src, dst):
        return pltpu.make_async_remote_copy(
            src_ref=src, dst_ref=dst, send_sem=ws, recv_sem=wr,
            device_id={"fluid": f, "wall": peer}, device_id_type=MESH)

    every_wall = wall_copy(lax.rem(w + 1, nw), ps.at[0 : nw - 1], pr.at[0 : nw - 1])
    for d in sorted(range(1, nw), key=lambda d: -min(d, nw - d)):
        peer = lax.rem(w + d, nw)
        wall_copy(peer, ps.at[peer], pr.at[w]).start()
    pr[w] = owned
    for x in range(CX):
        for c in range(3):
            adj[c, x] = adj[c, x] + unpack_edges(fix2[c], x)
    wait_halo_sent(halo)
    wait_halo_sent(halo2)
    sent1()
    sent2()
    every_wall.wait_recv()
    total = pr[0]
    for p in range(1, nw):
        total = total + pr[p]
    mine = jnp.sum(jnp.where(iota((8, TW), 0) == w, total, 0.0), axis=0, keepdims=True)
    sens_out[...] = sens_scale * mine[:, 0:REG_DEV]
    every_wall.wait_send()


def write_out(vn, adj, sens, vn_out, adj_out, sens_out, sems):
    copies = [pltpu.make_async_copy(sens, sens_out, sems.at[0])]
    for c in range(3):
        copies.append(pltpu.make_async_copy(vn.at[c], vn_out.at[c], sems.at[1 + c]))
        copies.append(pltpu.make_async_copy(adj.at[c], adj_out.at[c], sems.at[4 + c]))
    for copy in copies:
        copy.start()
    for copy in copies:
        copy.wait()


def solution(mesh):
    nf, nw = mesh.shape["fluid"], mesh.shape["wall"]

    def body(flow_state, regions, obs_tiles, measured, tile_dest, cell_list):
        tiles = obs_tiles.shape[2]
        in_hbm = pl.BlockSpec(memory_space=pltpu.HBM)
        in_vmem = pl.BlockSpec(memory_space=pltpu.VMEM)
        dma = pltpu.SemaphoreType.DMA
        vn, adj, sens = pl.pallas_call(
            functools.partial(kernel, nf, nw, tiles),
            out_shape=(
                pltpu.VMEM((3, CX, CY, TW), F32),
                pltpu.VMEM((3, CX, CY, TW), F32),
                pltpu.VMEM((1, REG_DEV), F32),
            ),
            in_specs=[in_hbm] * 6,
            out_specs=(in_vmem, in_vmem, in_vmem),
            scratch_shapes=[
                pltpu.VMEM((4, CX + 2, ROWS, TW), F32),
                pltpu.VMEM((3, CX + 2, ROWS, TW), F32),
                pltpu.VMEM((2, 4, CY, TW), BF16),
                pltpu.VMEM((2, 4, CY, TW), BF16),
                pltpu.VMEM((2, 3, CY, TW), BF16),
                pltpu.VMEM((2, 3, CY, TW), BF16),
                pltpu.VMEM((CX + 1, CY, TW), F32),
                pltpu.VMEM((CX, ROWS - TOP, TW), F32),
                pltpu.VMEM((CX, CY, TW), F32),
                pltpu.VMEM((CX, CY, TW), F32),
                pltpu.VMEM((8, TW), F32),
                pltpu.VMEM((3, 8, TW), F32),
                pltpu.VMEM((4, 8, TW), F32),
                pltpu.VMEM((4, 8, TW), F32),
                pltpu.VMEM((4, 8, TW), F32),
                pltpu.VMEM((3, 8, TW), F32),
                pltpu.VMEM((3, 8, TW), F32),
                pltpu.VMEM((3, 8, TW), F32),
                pltpu.VMEM((tiles, TW, TW), BF16),
                pltpu.VMEM((CX, CY, TW), jnp.int32),
                pltpu.VMEM((tiles // 2, 2 * MSG, 2 * TW), F32),
                pltpu.VMEM((tiles // 2, 2 * MSG, 2 * TW), F32),
                pltpu.VMEM((nf * CAP, CELLS), BF16),
                pltpu.VMEM((CELLS, TW), BF16),
                pltpu.VMEM((nf, TW), BF16),
                pltpu.VMEM((CELLS, 3 * TW), BF16),
                pltpu.VMEM((nf * MSG, TW), F32),
                pltpu.VMEM((nf, MSG, TW), BF16),
                pltpu.VMEM((nf, MSG, TW), BF16),
                pltpu.VMEM((tiles // 2, 2 * MSG, 2 * TW), BF16),
                pltpu.VMEM((tiles * MSG, TW), F32),
                pltpu.VMEM((nf, MSG, TW), BF16),
                pltpu.VMEM((nf, MSG, TW), BF16),
                pltpu.VMEM((TW, 3 * TW), BF16),
                pltpu.VMEM((CX * 4 * TW, TW), BF16),
                pltpu.VMEM((CX, 4, 4, MSG, TW), BF16),
                pltpu.VMEM((9 * TW, TW), BF16),
                pltpu.VMEM((4, MSG, TW), BF16),
                pltpu.VMEM((TW, TW), BF16),
                pltpu.VMEM((TW // 2, CX * 4 * TW), BF16),
                pltpu.VMEM((TW // 2, TW), F32),
                pltpu.VMEM((nw, 8, TW), F32),
                pltpu.VMEM((nw, 8, TW), F32),
                pltpu.VMEM((3, tiles, TW), BF16),
                pltpu.SMEM((tiles,), jnp.int32),
                pltpu.SMEM((CAP, nf), jnp.int32),
                pltpu.SemaphoreType.REGULAR((2,)),
                pltpu.SemaphoreType.REGULAR((3,)),
                dma((9,)),
                dma((4,)),
                dma((4,)),
                dma((4,)),
                dma((4,)),
                dma(()),
                dma(()),
                dma(()),
                dma(()),
                dma(()),
                dma(()),
            ],
            compiler_params=pltpu.CompilerParams(collective_id=0, has_side_effects=True, vmem_limit_bytes=60 * 1024 * 1024),
        )(
            flow_state, regions, obs_tiles[0, 0], measured[0, 0].transpose(1, 0, 2), tile_dest[0, 0],
            cell_list[0, 0].T,
        )
        vn, adj, sens = pl.pallas_call(
            write_out,
            out_shape=tuple(jax.ShapeDtypeStruct(a.shape, a.dtype) for a in (vn, adj, sens)),
            in_specs=[in_vmem, in_vmem, in_vmem],
            out_specs=(in_hbm, in_hbm, in_hbm),
            scratch_shapes=[dma((7,))],
            compiler_params=pltpu.CompilerParams(vmem_limit_bytes=8 << 20),
        )(vn, adj, sens)
        return vn, adj, sens.reshape(REG_DEV)

    in_specs = (
        P(None, "fluid", None, "wall"),
        P("fluid", None, "wall"),
        P("fluid", "wall", None, None, None),
        P("fluid", "wall", None, None, None),
        P("fluid", "wall", None),
        P("fluid", "wall", None, None),
    )
    out_specs = (
        P(None, "fluid", None, "wall"),
        P(None, "fluid", None, "wall"),
        P(("fluid", "wall")),
    )
    return jax.shard_map(body, mesh=mesh, in_specs=in_specs, out_specs=out_specs, check_vma=False)
```
